32 devices in a mesh: dp: 4 (over y, x), seq: 8 (over z, core).
Axes of the slice: x: 2, y: 2, z: 4, core: 2. Of those that a mesh axis runs over, the one named last changes fastest.
Arguments:
- tokens: bfloat16 [8, 4096, 1024], P('dp', 'seq'), may hold values from -6 to 6
- segment_ids: int32 [8, 4096], P('dp', 'seq'), may hold values from 0 to 3, as said below
- positions: int32 [8, 4096], P('dp', 'seq'), may hold values from 0 to 1791, as said below
- adapter_id: int32 [8], P('dp'), may hold values from 0 to 7, as said below
- gain_attn: float32 [1024], replicated, may hold values from 0.25 to 1.75
- gain_mlp: float32 [1024], replicated, may hold values from 0.25 to 1.75
- w_qkv: bfloat16 [1024, 3072], P(('dp', 'seq')), may hold values from -0.1875 to 0.1875
- w_out: bfloat16 [1024, 1024], P(('dp', 'seq')), may hold values from -3 to 3
- w_in: bfloat16 [1024, 5248], P(('dp', 'seq')), may hold values from -0.1875 to 0.1875
- w_out2: bfloat16 [2624, 1024], P(None, ('dp', 'seq')), may hold values from -0.125 to 0.125
- a_qkv: bfloat16 [8, 16, 1024], replicated, may hold values from -0.1875 to 0.1875
- b_qkv: bfloat16 [8, 16, 3072], replicated, may hold values from -1.5 to 1.5
- a_out: bfloat16 [8, 16, 1024], replicated, may hold values from -3 to 3
- b_out: bfloat16 [8, 16, 1024], replicated, may hold values from -1.5 to 1.5
- a_in: bfloat16 [8, 16, 1024], replicated, may hold values from -0.1875 to 0.1875
- b_in: bfloat16 [8, 16, 5248], replicated, may hold values from -1.5 to 1.5
- a_out2: bfloat16 [8, 16, 2624], replicated, may hold values from -0.125 to 0.125
- b_out2: bfloat16 [8, 16, 1024], replicated, may hold values from -1.5 to 1.5
- cotangent: bfloat16 [8, 4096, 1024], P('dp', 'seq'), may hold values from -6 to 6
Outputs:
- layer_out: bfloat16 [8, 4096, 1024], P('dp', 'seq')
- input_grad: bfloat16 [8, 4096, 1024], P('dp', 'seq')
- grad_a_qkv: float32 [8, 16, 1024], replicated
- grad_b_qkv: float32 [8, 16, 3072], replicated
- grad_a_out: float32 [8, 16, 1024], replicated
- grad_b_out: float32 [8, 16, 1024], replicated
- grad_a_in: float32 [8, 16, 1024], replicated
- grad_b_in: float32 [8, 16, 5248], replicated
- grad_a_out2: float32 [8, 16, 2624], replicated
- grad_b_out2: float32 [8, 16, 1024], replicated
The draws below stay inside these ranges and needn't reach their ends.
Inputs may be any that keep to these rules, and one draw needn't show every extreme that they name: `segment_ids`: within each sequence the document numbers never fall and run from 0 to 3; each of the four documents holds at least one token. `positions`: 0 at the first token of each document, rising by one per token up to the document's end; some document in every draw reaches the largest value. `adapter_id`: each adapter serves exactly 1 sequence.
All inputs are finite; a program needn't handle non-finite values.
Results may differ from the reference program's by a relative error of at most 0.018.
The reference program's roundings to bfloat16 on the way count: a program that leaves them out, or rounds other values in their place, can miss the bound.
Values may be sent and summed in bfloat16 or wider, within the bound.
No kernel may reach another device: no remote copies, remote signals or barrier semaphores. Data moves between devices by JAX's collectives and lax.ppermute only.
A program may use at most 256 MiB of HBM per device.

```python
import jax
import jax.numpy as jnp
from jax import lax

D = 1024
HEADS = 16
HD = 64
FF = 2624
RANK = 16
ADAPTERS = 8
SEQ_LEN = 4096
SEQS = 8


def document_cuts(key):
    quarter = SEQ_LEN // 4
    reach = 3 * quarter // 8
    jitter = jax.random.randint(jax.random.fold_in(key, 7), (SEQS, 3), -reach, reach + 1).astype(jnp.int32)
    forced = jnp.array([1, -1, 1], dtype=jnp.int32) * reach
    first_row = (jnp.arange(SEQS, dtype=jnp.int32) == 0)[:, None]
    jitter = jnp.where(first_row, forced[None, :], jitter).astype(jnp.int32)
    cuts = quarter * jnp.arange(1, 4, dtype=jnp.int32)[None, :] + jitter
    starts = jnp.concatenate([jnp.zeros((SEQS, 1), jnp.int32), cuts], 1)
    place = jnp.arange(SEQ_LEN, dtype=jnp.int32)
    inside = starts[:, None, :] <= place[None, :, None]
    segments = jnp.sum(inside.astype(jnp.int32), -1) - 1
    first = jnp.max(jnp.where(inside, starts[:, None, :], 0), -1)
    return (segments.astype(jnp.int32), (place[None, :] - first).astype(jnp.int32))


def draw_segment_ids(key, part):
    return document_cuts(key)[0]


def draw_positions(key, part):
    return document_cuts(key)[1]


def draw_adapter_id(key, part):
    order = jax.random.permutation(jax.random.fold_in(key, 11), SEQS)
    return (order % ADAPTERS).astype(jnp.int32)


def block_levels(rng, extent, shards, smallest, largest):
    def one(dim, parts):
        draws = jax.random.uniform(jax.random.fold_in(jax.random.fold_in(rng, 6), dim), (parts,), jnp.float32, smallest / len(shards), largest / len(shards))
        return jnp.repeat(jnp.exp(draws), extent[dim] // parts).reshape((-1,) + (1,) * (len(extent) - dim - 1))

    factor_of = one(*shards[0])
    for cut in shards[1:]:
        factor_of = factor_of * one(*cut)
    return factor_of


def scatter_about(stream_key, extent, scale, bound, cuts=(), kind=jnp.bfloat16):
    values = scale * jax.random.normal(stream_key, extent, jnp.float32)
    if cuts:
        values = values * block_levels(stream_key, extent, cuts, -0.22, 0.18)
    return jnp.clip(values, -bound, bound).astype(kind)


def setup_inputs(seed: int = 0) -> dict:
    splits = jax.random.split(jax.random.key(seed), 20)
    return {
        "tokens": scatter_about(splits[0], (SEQS, SEQ_LEN, D), 1.0, 6.0, ((0, 4), (1, 8))),
        "segment_ids": draw_segment_ids(jax.random.fold_in(splits[19], 71), 0),
        "positions": draw_positions(jax.random.fold_in(splits[19], 71), 0),
        "adapter_id": draw_adapter_id(jax.random.fold_in(splits[19], 71), 0),
        "gain_attn": jnp.clip(1.0 + 0.15 * jax.random.normal(splits[4], (D,), jnp.float32), 0.25, 1.75),
        "gain_mlp": jnp.clip(1.0 + 0.15 * jax.random.normal(splits[5], (D,), jnp.float32), 0.25, 1.75),
        "w_qkv": scatter_about(splits[6], (D, 3 * D), D ** -0.5, 0.1875, ((0, 32),)),
        "w_out": scatter_about(splits[7], (D, D), (max(D // 256, 1)) ** -0.5, 3.0, ((0, 32),)),
        "w_in": scatter_about(splits[8], (D, 2 * FF), D ** -0.5, 0.1875, ((0, 32),)),
        "w_out2": scatter_about(splits[9], (FF, D), FF ** -0.5, 0.125, ((1, 32),)),
        "a_qkv": scatter_about(splits[10], (ADAPTERS, RANK, D), D ** -0.5, 0.1875),
        "b_qkv": scatter_about(splits[11], (ADAPTERS, RANK, 3 * D), RANK ** -0.5, 1.5),
        "a_out": scatter_about(splits[12], (ADAPTERS, RANK, D), (max(D // 256, 1)) ** -0.5, 3.0),
        "b_out": scatter_about(splits[13], (ADAPTERS, RANK, D), RANK ** -0.5, 1.5),
        "a_in": scatter_about(splits[14], (ADAPTERS, RANK, D), D ** -0.5, 0.1875),
        "b_in": scatter_about(splits[15], (ADAPTERS, RANK, 2 * FF), RANK ** -0.5, 1.5),
        "a_out2": scatter_about(splits[16], (ADAPTERS, RANK, FF), FF ** -0.5, 0.125),
        "b_out2": scatter_about(splits[17], (ADAPTERS, RANK, D), RANK ** -0.5, 1.5),
        "cotangent": scatter_about(splits[18], (SEQS, SEQ_LEN, D), 1.0, 6.0, ((0, 4), (1, 8))),
    }


@jax.custom_vjp
def low(v):
    return lax.optimization_barrier(v.astype(jnp.bfloat16)).astype(jnp.float32)

@jax.custom_vjp
def low_back(v):
    return v

def low_keep(v):
    return (low(v), None)

def low_pass(kept, grad):
    return (grad,)

def back_keep(v):
    return (v, None)

def back_low(kept, grad):
    return (low(grad),)
low.defvjp(low_keep, low_pass)
low_back.defvjp(back_keep, back_low)
highest = lax.Precision.HIGHEST
eps_norm = 1e-05
theta_base = 160000.0

def matmul(left, right):
    return jnp.dot(left, right, precision=highest, preferred_element_type=jnp.float32)

def layer_norm(values, gain):
    center = values - lax.optimization_barrier(jnp.mean(values, axis=-1, keepdims=True))
    spread = lax.optimization_barrier(jnp.mean(center * center, axis=-1, keepdims=True))
    return center * lax.rsqrt(spread + eps_norm) * gain

def rope_tables(place):
    half_size = HD // 2
    frequency = theta_base ** (-(jnp.arange(half_size, dtype=jnp.float32) * 2.0) / HD)
    angles = place.astype(jnp.float32)[:, None] * frequency[None, :]
    cosine = jnp.cos(angles)
    sine_table = jnp.sin(angles)
    return (jnp.concatenate([cosine, cosine], -1), jnp.concatenate([sine_table, sine_table], -1))

def rotate(vector, cosine, sine_table):
    half_size = HD // 2
    turned = jnp.concatenate([-vector[..., half_size:], vector[..., :half_size]], -1)
    return vector * cosine[:, None, :] + turned * sine_table[:, None, :]

def one_head(queries, key_rows, value_rows, segments):
    scores = low_back(matmul(queries, key_rows.T) * 0.125)
    same_doc = segments[:, None] == segments[None, :]
    scores = jnp.where(same_doc, scores, -1e+30)
    probability = low(jax.nn.softmax(scores, axis=-1))
    return matmul(probability, value_rows)

def sequence(inputs, adapters, segments, place, chosen, gain_attn, gain_mlp, w_qkv, w_out, w_in, w_out2):
    a_qkv, b_qkv, a_out, b_out, a_in, b_in, a_out2, b_out2 = [table[chosen] for table in adapters]
    length = inputs.shape[0]
    normed1 = low(layer_norm(inputs, gain_attn))
    small1 = low_back(low(matmul(normed1, a_qkv.T)))
    lin_qkv = low_back(matmul(normed1, w_qkv) + matmul(small1, b_qkv))
    split = lin_qkv.reshape(length, 3, HEADS, HD)
    cosine, sine_table = rope_tables(place)
    queries = low_back(low(rotate(split[:, 0], cosine, sine_table)))
    key_rows = low_back(low(rotate(split[:, 1], cosine, sine_table)))
    value_rows = low_back(low(split[:, 2]))

    def head_fn(triple):
        return one_head(triple[0], triple[1], triple[2], segments)
    heads_out = lax.map(jax.checkpoint(head_fn), (queries.transpose(1, 0, 2), key_rows.transpose(1, 0, 2), value_rows.transpose(1, 0, 2)))
    attended = low_back(low(heads_out.transpose(1, 0, 2).reshape(length, HEADS * HD)))
    small2 = low_back(low(matmul(attended, a_out.T)))
    attn_branch = low_back(matmul(attended, w_out) + matmul(small2, b_out))
    middle = inputs + attn_branch
    normed2 = low(layer_norm(middle, gain_mlp))
    small3 = low_back(low(matmul(normed2, a_in.T)))
    gate_up = low_back(matmul(normed2, w_in) + matmul(small3, b_in))
    mixed = low(jax.nn.gelu(gate_up[:, :FF], approximate=False) * gate_up[:, FF:])
    small4 = low_back(low(matmul(mixed, a_out2.T)))
    branch = low_back(matmul(mixed, w_out2) + matmul(small4, b_out2))
    return middle + branch

def reference(tokens, segment_ids, positions, adapter_id, gain_attn, gain_mlp, w_qkv, w_out, w_in, w_out2, a_qkv, b_qkv, a_out, b_out, a_in, b_in, a_out2, b_out2, cotangent):
    frozen = tuple((w.astype(jnp.float32) for w in (w_qkv, w_out, w_in, w_out2)))
    adapters = tuple((t.astype(jnp.float32) for t in (a_qkv, b_qkv, a_out, b_out, a_in, b_in, a_out2, b_out2)))
    gains = (gain_attn.astype(jnp.float32), gain_mlp.astype(jnp.float32))

    def step(totals, element):
        inputs, segments, place, chosen, cot = element

        def forward(values, tables):
            return sequence(values, tables, segments, place, chosen, gains[0], gains[1], frozen[0], frozen[1], frozen[2], frozen[3])
        result, pull = jax.vjp(forward, inputs.astype(jnp.float32), adapters)
        dinputs, dtables = pull(cot.astype(jnp.float32))
        totals = tuple((a + b for a, b in zip(totals, dtables)))
        return (totals, (result.astype(jnp.bfloat16), dinputs.astype(jnp.bfloat16)))
    zeros = tuple((jnp.zeros(t.shape, jnp.float32) for t in adapters))
    totals, (outputs, grads) = lax.scan(step, zeros, (tokens, segment_ids, positions, adapter_id, cotangent))
    return (outputs, grads, totals[0], totals[1], totals[2], totals[3], totals[4], totals[5], totals[6], totals[7])
```

```python
import functools

import jax
import jax.numpy as jnp
from jax import lax
from jax.experimental import pallas as pl
from jax.experimental.pallas import tpu as pltpu
from jax.sharding import PartitionSpec as P

HEADS = 16
HD = 64
DOCS = 4
COL = 256
BLOCK_PAD = 1

eps_norm = 1e-05
theta_base = 160000.0
LOG2E = 1.4426950408889634
NEG = -1e30
RSQRT2 = 0.7071067811865476
RSQRT2PI = 0.3989422804014327
bf16 = jnp.bfloat16
f32 = jnp.float32


def nt(left, right):
    return lax.dot_general(left, right, (((1,), (1,)), ((), ())), preferred_element_type=f32)


def nn(left, right):
    return lax.dot_general(left, right, (((1,), (0,)), ((), ())), preferred_element_type=f32)


def tn(left, right):
    return lax.dot_general(left, right, (((0,), (0,)), ((), ())), preferred_element_type=f32)


def params():
    return pltpu.CompilerParams(dimension_semantics=("arbitrary",))


def whole_spec(shape):
    zeros = (0,) * len(shape)
    return pl.BlockSpec(shape, lambda *_: zeros)


def stack_heads(rows, groups):
    if groups == 1:
        return rows
    lane = lax.broadcasted_iota(jnp.int32, rows.shape, 1)
    return jnp.concatenate(
        [
            jnp.where((lane >= h * HD) & (lane < (h + 1) * HD), rows, jnp.zeros_like(rows))
            for h in range(groups)
        ],
        0,
    )


def tile_range(cuts_ref, doc, index, tile, length):
    first = cuts_ref[doc]
    last = cuts_ref[doc + 1]
    nominal = (first // 16) * 16 + index * tile
    off = pl.multiple_of(jnp.minimum(nominal, length - tile), 16)
    low = jnp.maximum(nominal, first) - off
    high = jnp.minimum(nominal + tile, last) - off
    return off, low, high


def tile_count(cuts_ref, doc, tile):
    base = (cuts_ref[doc] // 16) * 16
    return lax.div(cuts_ref[doc + 1] - base + (tile - 1), tile)


def keep_rows(low, high, shape):
    row = lax.broadcasted_iota(jnp.int32, shape, 0)
    return (row >= low) & (row < high)


def attend_kernel(
    cuts_ref, q_ref, k_ref, v_ref, o_ref, lse_ref, vt_ref, m_ref, acc_ref, *, tile, groups, length
):
    width = groups * HD
    qf = q_ref.reshape(length, width)
    kf = k_ref.reshape(length, width)
    vf = v_ref.reshape(length, width)
    of = o_ref.reshape(length, width)
    wide = groups * tile
    vt_ref[:, width:, :] = jnp.ones((vt_ref.shape[0], 16, tile), bf16)

    def doc_step(doc, first_tile):
        count = tile_count(cuts_ref, doc, tile)

        def prepare(j, carry):
            off, low, high = tile_range(cuts_ref, doc, j, tile, length)
            vt_ref[j, 0:width, :] = vf[pl.ds(off, tile), :].T
            return carry

        lax.fori_loop(0, count, prepare, 0)

        def q_tile(i, carry):
            off, low, high = tile_range(cuts_ref, doc, i, tile, length)
            qm = stack_heads(qf[pl.ds(off, tile), :] * bf16(0.125), groups)
            m_ref[...] = jnp.full(m_ref.shape, NEG, f32)
            acc_ref[...] = jnp.zeros(acc_ref.shape, f32)

            def k_tile(j, inner):
                koff, klow, khigh = tile_range(cuts_ref, doc, j, tile, length)
                keep = keep_rows(klow, khigh, (tile, wide))
                s = jnp.where(keep, nt(kf[pl.ds(koff, tile), :], qm) * LOG2E, NEG)
                m_old = m_ref[0:1, :]
                m_new = jnp.maximum(m_old, jnp.max(s, axis=0, keepdims=True))
                p = jnp.exp2(s - m_new).astype(bf16)
                acc_ref[...] = acc_ref[...] * jnp.exp2(m_old - m_new) + nn(vt_ref[j], p)
                m_ref[0:1, :] = m_new
                return inner

            lax.fori_loop(0, count, k_tile, 0)
            total = acc_ref[width : width + 1, :]
            inverse = 1.0 / total
            lse_ref[first_tile + i, 0:1, :] = m_ref[0:1, :] + jnp.log2(total)
            parts = [
                acc_ref[h * HD : (h + 1) * HD, h * tile : (h + 1) * tile]
                * inverse[:, h * tile : (h + 1) * tile]
                for h in range(groups)
            ]
            out = (jnp.concatenate(parts, 0) if groups > 1 else parts[0]).T.astype(bf16)
            keep = keep_rows(low, high, (tile, width))
            of[pl.ds(off, tile), :] = jnp.where(keep, out, of[pl.ds(off, tile), :])
            return carry

        lax.fori_loop(0, count, q_tile, 0)
        return first_tile + count

    lax.fori_loop(0, DOCS, doc_step, 0)


def qkv_spec(shape, which):
    pieces, _, piece_len, width = shape
    return pl.BlockSpec((pieces, None, piece_len, width), lambda i, cuts: (0, which, 0, 0))


def attend(packed, cuts, tile):
    pieces, _, piece_len, width = packed.shape
    groups = width // HD
    length = pieces * piece_len
    tiles = length // tile + DOCS
    wide = groups * tile
    return pl.pallas_call(
        functools.partial(attend_kernel, tile=tile, groups=groups, length=length),
        out_shape=(
            jax.ShapeDtypeStruct((pieces, piece_len, width), bf16),
            jax.ShapeDtypeStruct((tiles, 8, wide), f32),
        ),
        grid_spec=pltpu.PrefetchScalarGridSpec(
            num_scalar_prefetch=1,
            grid=(1,),
            in_specs=[qkv_spec(packed.shape, w) for w in range(3)],
            out_specs=[whole_spec((pieces, piece_len, width)), whole_spec((tiles, 8, wide))],
            scratch_shapes=[
                pltpu.VMEM((length // tile + 1, width + 16, tile), bf16),
                pltpu.VMEM((8, wide), f32),
                pltpu.VMEM((width + 16, wide), f32),
            ],
        ),
        compiler_params=params(),
        name="attend",
    )(cuts, packed, packed, packed)


def attend_back_kernel(
    cuts_ref,
    q_ref,
    k_ref,
    v_ref,
    o_ref,
    do_ref,
    lse_ref,
    out_ref,
    lse_s,
    delta_s,
    dqt_s,
    dk_s,
    dv_s,
    dqf,
    dkf,
    dvf,
    *,
    tile,
    groups,
    length,
):
    width = groups * HD
    qf = q_ref.reshape(length, width)
    kf = k_ref.reshape(length, width)
    vf = v_ref.reshape(length, width)
    of = o_ref.reshape(length, width)
    dof = do_ref.reshape(length, width)
    wide = groups * tile
    head_row = lax.broadcasted_iota(jnp.int32, (16, width), 0)
    head_lane = lax.broadcasted_iota(jnp.int32, (16, width), 1)
    head_rows = jnp.where(head_row == head_lane // HD, 1.0, 0.0).astype(bf16)

    def doc_step(doc, first_tile):
        count = tile_count(cuts_ref, doc, tile)

        def prepare(i, carry):
            off, low, high = tile_range(cuts_ref, doc, i, tile, length)
            product = dof[pl.ds(off, tile), :].astype(f32) * of[pl.ds(off, tile), :].astype(f32)
            upper = product.astype(bf16)
            lower = (product - upper.astype(f32)).astype(bf16)
            sums = nt(head_rows, upper) + nt(head_rows, lower)
            column = lax.broadcasted_iota(jnp.int32, (1, tile), 1)
            valid = (column >= low) & (column < high)
            for h in range(groups):
                lanes = slice(h * tile, (h + 1) * tile)
                delta_s[i, 0:1, lanes] = sums[h : h + 1, :]
                lse_s[i, 0:1, lanes] = jnp.where(valid, lse_ref[first_tile + i, 0:1, lanes], -NEG)
            dqt_s[i] = jnp.zeros((width, tile), f32)
            return carry

        lax.fori_loop(0, count, prepare, 0)

        def k_tile(j, carry):
            koff, klow, khigh = tile_range(cuts_ref, doc, j, tile, length)
            keys = kf[pl.ds(koff, tile), :]
            values = vf[pl.ds(koff, tile), :]
            keys_t = keys.T
            dk_s[...] = jnp.zeros(dk_s.shape, f32)
            dv_s[...] = jnp.zeros(dv_s.shape, f32)

            def q_tile(i, inner):
                off, low, high = tile_range(cuts_ref, doc, i, tile, length)
                qm = stack_heads(qf[pl.ds(off, tile), :] * bf16(0.125), groups)
                dom = stack_heads(dof[pl.ds(off, tile), :], groups)
                s = jnp.where(keep_rows(klow, khigh, (tile, wide)), nt(keys, qm) * LOG2E, NEG)
                p = jnp.exp2(s - lse_s[i, 0:1, :])
                ds = (p * (nt(values, dom) - delta_s[i, 0:1, :])).astype(bf16)
                dv_s[...] += nn(p.astype(bf16), dom)
                dk_s[...] += nn(ds, qm)
                dqt = nn(keys_t, ds)
                parts = [
                    dqt[h * HD : (h + 1) * HD, h * tile : (h + 1) * tile] for h in range(groups)
                ]
                dqt_s[i] += jnp.concatenate(parts, 0) if groups > 1 else parts[0]
                return inner

            lax.fori_loop(0, count, q_tile, 0)
            keep = keep_rows(klow, khigh, (tile, width))
            spot = pl.ds(koff, tile)
            dkf[spot, :] = jnp.where(keep, dk_s[...].astype(bf16), dkf[spot, :])
            dvf[spot, :] = jnp.where(keep, dv_s[...].astype(bf16), dvf[spot, :])
            return carry

        lax.fori_loop(0, count, k_tile, 0)

        def finish(i, carry):
            off, low, high = tile_range(cuts_ref, doc, i, tile, length)
            out = (dqt_s[i] * 0.125).T.astype(bf16)
            spot = pl.ds(off, tile)
            dqf[spot, :] = jnp.where(keep_rows(low, high, (tile, width)), out, dqf[spot, :])
            return carry

        lax.fori_loop(0, count, finish, 0)
        return first_tile + count

    lax.fori_loop(0, DOCS, doc_step, 0)
    piece_len = q_ref.shape[1]
    for at in range(q_ref.shape[0]):
        for which, full in enumerate((dqf, dkf, dvf)):
            out_ref[at, which] = full[at * piece_len : (at + 1) * piece_len, :]


def attend_back(packed, o, do, lse, cuts, tile):
    pieces, _, piece_len, width = packed.shape
    groups = width // HD
    length = pieces * piece_len
    tiles = length // tile + DOCS
    wide = groups * tile
    per_doc = length // tile + 1
    flat = whole_spec((pieces, piece_len, width))
    return pl.pallas_call(
        functools.partial(attend_back_kernel, tile=tile, groups=groups, length=length),
        out_shape=jax.ShapeDtypeStruct((pieces, 3, piece_len, width), bf16),
        grid_spec=pltpu.PrefetchScalarGridSpec(
            num_scalar_prefetch=1,
            grid=(1,),
            in_specs=[qkv_spec(packed.shape, w) for w in range(3)]
            + [flat, flat, whole_spec((tiles, 8, wide))],
            out_specs=whole_spec((pieces, 3, piece_len, width)),
            scratch_shapes=[
                pltpu.VMEM((per_doc, 8, wide), f32),
                pltpu.VMEM((per_doc, 8, wide), f32),
                pltpu.VMEM((per_doc, width, tile), f32),
                pltpu.VMEM((tile, width), f32),
                pltpu.VMEM((tile, width), f32),
            ]
            + [pltpu.VMEM((length, width), bf16)] * 3,
        ),
        compiler_params=params(),
        name="attend_back",
    )(cuts, packed, packed, packed, o, do, lse)


def normalize(values):
    center = values - jnp.mean(values, axis=-1, keepdims=True)
    spread = jnp.mean(center * center, axis=-1, keepdims=True)
    scale = lax.rsqrt(spread + eps_norm)
    return center * scale, scale


def norm_back(unit, scale, scaled_grad):
    return scale * (
        scaled_grad
        - jnp.mean(scaled_grad, axis=-1, keepdims=True)
        - unit * jnp.mean(scaled_grad * unit, axis=-1, keepdims=True)
    )


def lane_swap(values):
    lane = lax.broadcasted_iota(jnp.int32, values.shape, 1)
    size = values.shape[1]
    half = HD // 2
    return jnp.where(
        lane % HD < half, pltpu.roll(values, size - half, 1), pltpu.roll(values, half, 1)
    )


def qkv_kernel(
    x_ref, g_ref, wq_ref, wk_ref, wv_ref, a_ref, b_ref, cos_ref, sin_ref,
    out_ref, norm_ref, small_ref, *, width,
):
    @pl.when(pl.program_id(0) == 0)
    def _():
        unit, _ = normalize(x_ref[...].astype(f32))
        norm = (unit * g_ref[...]).astype(bf16)
        norm_ref[...] = norm
        small_ref[...] = nt(a_ref[...], norm).astype(bf16)

    norm = norm_ref[...]
    small = small_ref[...]
    for which, w_ref in enumerate((wq_ref, wk_ref, wv_ref)):
        lin = nn(norm, w_ref[...]) + tn(small, b_ref[which])
        for part in range(COL // 128):
            u = lin[:, part * 128 : (part + 1) * 128]
            if which < 2:
                u = u * cos_ref[...] + lane_swap(u) * sin_ref[...]
            u = u.astype(bf16)
            for sub in range(128 // width):
                out_ref[part * (128 // width) + sub, which] = u[:, sub * width : (sub + 1) * width]


def qkv_project(x, gain, w, a, b, cosine, sine, pieces, width):
    rows, model = x.shape
    dests = COL // width
    steps = model // COL
    rank = a.shape[0]
    w_spec = lambda which: pl.BlockSpec((model, COL), lambda j: (0, which * steps + j))
    return pl.pallas_call(
        functools.partial(qkv_kernel, width=width),
        grid=(steps,),
        out_shape=(
            jax.ShapeDtypeStruct((pieces, 3, rows, width), bf16),
            jax.ShapeDtypeStruct((rows, model), bf16),
            jax.ShapeDtypeStruct((rank, rows), bf16),
        ),
        in_specs=[whole_spec((rows, model)), whole_spec((1, model))]
        + [w_spec(which) for which in range(3)]
        + [
            whole_spec((rank, model)),
            pl.BlockSpec((3, rank, COL), lambda j: (0, 0, j)),
            whole_spec((rows, 128)),
            whole_spec((rows, 128)),
        ],
        out_specs=[
            pl.BlockSpec((dests, 3, rows, width), lambda j: (j, 0, 0, 0)),
            whole_spec((rows, model)),
            whole_spec((rank, rows)),
        ],
        compiler_params=params(),
        name="qkv_project",
    )(x, gain, w, w, w, a, b, cosine, sine)


def input_grad_kernel(
    dqkv_ref, x_ref, g_ref, norm_ref, small_ref, dmid_ref, wq_ref, wk_ref, wv_ref, a_ref, b_ref,
    cos_ref, sin_ref, out_ref, grad_ref, acc_ref, dsmall_ref, *, width,
):
    step = pl.program_id(0)

    @pl.when(step == 0)
    def _():
        acc_ref[...] = jnp.zeros(acc_ref.shape, f32)
        dsmall_ref[...] = jnp.zeros(dsmall_ref.shape, f32)

    small = small_ref[...]
    per = 128 // width
    for which, w_ref in enumerate((wq_ref, wk_ref, wv_ref)):
        pieces = []
        for part in range(COL // 128):
            subs = [dqkv_ref[part * per + sub, which] for sub in range(per)]
            u = jnp.concatenate(subs, 1) if per > 1 else subs[0]
            if which < 2:
                u = u.astype(f32)
                u = (u * cos_ref[...] - lane_swap(u) * sin_ref[...]).astype(bf16)
            pieces.append(u)
        dlin = jnp.concatenate(pieces, 1)
        acc_ref[...] += nt(dlin, w_ref[...])
        dsmall_ref[...] += nt(b_ref[which], dlin)
        grad_ref[(which + 1) * pl.num_programs(0) + step] = nn(small, dlin)

    @pl.when(step == pl.num_programs(0) - 1)
    def _():
        dsmall = dsmall_ref[...].astype(bf16)
        dnorm = acc_ref[...] + tn(dsmall, a_ref[...])
        grad_a = nn(dsmall, norm_ref[...])
        for at in range(grad_a.shape[1] // COL):
            grad_ref[at] = grad_a[:, at * COL : (at + 1) * COL]
        unit, scale = normalize(x_ref[...].astype(f32))
        out_ref[...] = (dmid_ref[...] + norm_back(unit, scale, dnorm * g_ref[...])).astype(bf16)


def input_grad_call(dqkv, x, gain, norm, small, dmid, w, a, b, cosine, sine):
    pieces, _, rows, width = dqkv.shape
    model = x.shape[1]
    rank = a.shape[0]
    dests = COL // width
    steps = model // COL
    w_spec = lambda which: pl.BlockSpec((model, COL), lambda j: (0, which * steps + j))
    return pl.pallas_call(
        functools.partial(input_grad_kernel, width=width),
        grid=(steps,),
        out_shape=(
            jax.ShapeDtypeStruct((rows, model), bf16),
            jax.ShapeDtypeStruct((4 * steps, rank, COL), f32),
        ),
        in_specs=[
            pl.BlockSpec((dests, 3, rows, width), lambda j: (j, 0, 0, 0)),
            whole_spec((rows, model)),
            whole_spec((1, model)),
            whole_spec((rows, model)),
            whole_spec((rank, rows)),
            whole_spec((rows, model)),
        ]
        + [w_spec(which) for which in range(3)]
        + [
            whole_spec((rank, model)),
            pl.BlockSpec((3, rank, COL), lambda j: (0, 0, j)),
            whole_spec((rows, 128)),
            whole_spec((rows, 128)),
        ],
        out_specs=[
            whole_spec((rows, model)),
            whole_spec((4 * steps, rank, COL)),
        ],
        scratch_shapes=[pltpu.VMEM((rows, model), f32), pltpu.VMEM((rank, rows), f32)],
        compiler_params=params(),
        name="input_grad",
    )(dqkv, x, gain, norm, small, dmid, w, w, w, a, b, cosine, sine)


def mlp_kernel(
    x_ref, cot_ref, o_ref, g_ref, wo_ref, wu_ref, wv_ref, wt_ref,
    aout_ref, bout_ref, ain_ref, bu_ref, bv_ref, a2_ref, b2_ref,
    out_ref, dmid_ref, datt_ref, grad_ref,
    att_s, norm_s, unit_s, scale_s, acc_s, dnorm_s, small2_s, small3_s, small4_s, dsmall4_s, dsmall3_s,
    *, width,
):
    step = pl.program_id(0)
    pieces = o_ref.shape[0]
    model = x_ref.shape[1]
    per = model // COL
    first_block = grad_ref.shape[0] - BLOCK_PAD - 4 * per

    def put(which, value):
        for at in range(per):
            grad_ref[first_block + which * per + at] = value[:, at * COL : (at + 1) * COL]

    @pl.when(step == 0)
    def _():
        grad_ref[first_block + 4 * per :] = jnp.zeros((BLOCK_PAD,) + grad_ref.shape[1:], f32)
        for at in range(pieces):
            att_s[:, at * width : (at + 1) * width] = o_ref[at]
        att = att_s[...]
        small2 = nt(aout_ref[...], att).astype(bf16)
        small2_s[...] = small2
        middle = x_ref[...].astype(f32) + nn(att, wo_ref[...]) + tn(small2, bout_ref[...])
        acc_s[...] = middle
        unit, scale = normalize(middle)
        unit_s[...] = unit
        scale_s[...] = jnp.broadcast_to(scale, scale_s.shape)
        norm = (unit * g_ref[...]).astype(bf16)
        norm_s[...] = norm
        small3_s[...] = nt(ain_ref[...], norm).astype(bf16)
        dsmall4_s[...] = nt(b2_ref[...], cot_ref[...]).astype(bf16)
        dnorm_s[...] = jnp.zeros(dnorm_s.shape, f32)
        small4_s[...] = jnp.zeros(small4_s.shape, f32)
        dsmall3_s[...] = jnp.zeros(dsmall3_s.shape, f32)

    norm = norm_s[...]
    small3 = small3_s[...]
    dsmall4 = dsmall4_s[...]
    u = nn(norm, wu_ref[...]) + tn(small3, bu_ref[...])
    v = nn(norm, wv_ref[...]) + tn(small3, bv_ref[...])
    dmixed = nn(cot_ref[...], wt_ref[...]) + tn(dsmall4, a2_ref[...])
    below = 0.5 * (1.0 + lax.erf(u * RSQRT2))
    gelu = u * below
    mixed = (gelu * v).astype(bf16)
    slope = below + u * (jnp.exp(-0.5 * u * u) * RSQRT2PI)
    du = (dmixed * v * slope).astype(bf16)
    dv = (dmixed * gelu).astype(bf16)
    acc_s[...] += nt(mixed, wt_ref[...])
    dnorm_s[...] += nt(du, wu_ref[...]) + nt(dv, wv_ref[...])
    small4_s[...] += nt(a2_ref[...], mixed)
    dsmall3_s[...] += nt(bu_ref[...], du) + nt(bv_ref[...], dv)
    steps = pl.num_programs(0)
    grad_ref[step] = nn(small3, du)
    grad_ref[steps + step] = nn(small3, dv)
    grad_ref[2 * steps + step] = nn(dsmall4, mixed)

    @pl.when(step == pl.num_programs(0) - 1)
    def _():
        small4 = small4_s[...].astype(bf16)
        dsmall3 = dsmall3_s[...].astype(bf16)
        out_ref[...] = (acc_s[...] + tn(small4, b2_ref[...])).astype(bf16)
        put(3, nn(small4, cot_ref[...]))
        dnorm = dnorm_s[...] + tn(dsmall3, ain_ref[...])
        put(2, nn(dsmall3, norm_s[...]))
        dmid = cot_ref[...].astype(f32) + norm_back(unit_s[...], scale_s[:, 0:1], dnorm * g_ref[...])
        dmid_ref[...] = dmid
        dlow = dmid.astype(bf16)
        dsmall2 = nt(bout_ref[...], dlow).astype(bf16)
        put(1, nn(small2_s[...], dlow))
        put(0, nn(dsmall2, att_s[...]))
        datt = (nt(dlow, wo_ref[...]) + tn(dsmall2, aout_ref[...])).astype(bf16)
        for at in range(pieces):
            datt_ref[at] = datt[:, at * width : (at + 1) * width]


def mlp_call(x, cot, o, gain, w_out, w_ff, a_out, b_out, a_in, b_u, b_v, a_out2, b_out2):
    rows, model = x.shape
    pieces, _, width = o.shape
    rank = a_out.shape[0]
    hidden = b_u.shape[1]
    steps = hidden // COL
    blocks = 3 * steps + 4 * (model // COL) + BLOCK_PAD
    full = lambda shape: pl.BlockSpec(shape, lambda j: (0,) * len(shape), pipeline_mode=pl.Buffered(1))
    ff_spec = lambda which: pl.BlockSpec((model, COL), lambda j: (0, which * steps + j))
    small_ff = pl.BlockSpec((rank, COL), lambda j: (0, j))
    small = full((rank, model))
    return pl.pallas_call(
        functools.partial(mlp_kernel, width=width),
        grid=(steps,),
        out_shape=(
            jax.ShapeDtypeStruct((rows, model), bf16),
            jax.ShapeDtypeStruct((rows, model), f32),
            jax.ShapeDtypeStruct((pieces, rows, width), bf16),
            jax.ShapeDtypeStruct((blocks, rank, COL), f32),
        ),
        in_specs=[
            full((rows, model)),
            full((rows, model)),
            full((pieces, rows, width)),
            full((1, model)),
            full((model, model)),
            ff_spec(0),
            ff_spec(1),
            ff_spec(2),
            small,
            small,
            small,
            small_ff,
            small_ff,
            small_ff,
            small,
        ],
        out_specs=[
            whole_spec((rows, model)),
            whole_spec((rows, model)),
            whole_spec((pieces, rows, width)),
            whole_spec((blocks, rank, COL)),
        ],
        scratch_shapes=[
            pltpu.VMEM((rows, model), bf16),
            pltpu.VMEM((rows, model), bf16),
            pltpu.VMEM((rows, model), f32),
            pltpu.VMEM((rows, 128), f32),
            pltpu.VMEM((rows, model), f32),
            pltpu.VMEM((rows, model), f32),
            pltpu.VMEM((rank, rows), bf16),
            pltpu.VMEM((rank, rows), bf16),
            pltpu.VMEM((rank, rows), f32),
            pltpu.VMEM((rank, rows), bf16),
            pltpu.VMEM((rank, rows), f32),
        ],
        compiler_params=params(),
        name="feed_forward",
    )(x, cot, o, gain, w_out, w_ff, w_ff, w_ff, a_out, b_out, a_in, b_u, b_v, a_out2, b_out2)


def pad_columns(values, size):
    return jnp.pad(values, [(0, 0)] * (values.ndim - 1) + [(0, size - values.shape[-1])])


def local(
    tokens,
    segment_ids,
    positions,
    adapter_id,
    gain_attn,
    gain_mlp,
    w_qkv,
    w_out,
    w_in,
    w_out2,
    a_qkv,
    b_qkv,
    a_out,
    b_out,
    a_in,
    b_in,
    a_out2,
    b_out2,
    cotangent,
):
    seq_count, piece_len, model = tokens.shape
    pieces = lax.axis_size("seq")
    groups = HEADS // pieces
    width = groups * HD
    length = piece_len * pieces
    rank = a_qkv.shape[1]
    adapters = a_qkv.shape[0]
    hidden = w_out2.shape[0]
    padded = -(-hidden // COL) * COL
    tile = min(512, length)
    both = ("dp", "seq")

    dp = lax.axis_size("dp")
    group = lax.axis_index("dp")
    before = [jnp.sum((segment_ids < d).astype(jnp.int32), axis=1) for d in range(1, DOCS)]
    own_id = jnp.where(lax.axis_index("seq") == 0, adapter_id, 0)
    facts = jnp.stack(before + [own_id], 1)
    slot = (jnp.arange(dp, dtype=jnp.int32) == group).astype(jnp.int32)
    facts = lax.psum(slot[:, None, None] * facts[None], both)
    first_tokens, facts = lax.optimization_barrier((tokens, facts))
    every_id = facts[:, :, DOCS - 1].reshape(-1)
    counts = lax.dynamic_index_in_dim(facts, group, 0, keepdims=False)[:, : DOCS - 1]
    cuts = jnp.concatenate(
        [
            jnp.zeros((seq_count, 1), jnp.int32),
            counts,
            jnp.full((seq_count, 1), length, jnp.int32),
        ],
        1,
    )
    full_qkv = lax.all_gather(w_qkv, both, axis=0, tiled=True)
    full_out = lax.all_gather(w_out, both, axis=0, tiled=True)
    local_ff = jnp.concatenate(
        [
            pad_columns(w_in[:, :hidden], padded),
            pad_columns(w_in[:, hidden:], padded),
            pad_columns(w_out2.T, padded),
        ],
        1,
    )
    full_ff = lax.all_gather(local_ff, both, axis=0, tiled=True)

    half = HD // 2
    lane = jnp.arange(128, dtype=jnp.int32) % HD
    frequency = theta_base ** (-((lane % half).astype(f32) * 2.0) / HD)
    angles = positions.astype(f32)[..., None] * frequency
    cosine = jnp.cos(angles)
    sine = jnp.where(lane < half, -1.0, 1.0) * jnp.sin(angles)

    gain1 = gain_attn.reshape(1, model)
    gain2 = gain_mlp.reshape(1, model)
    pick = lambda table, s: lax.dynamic_index_in_dim(table, adapter_id[s], 0, keepdims=False)
    swap = lambda value: lax.all_to_all(value, "seq", split_axis=0, concat_axis=0, tiled=True)
    each = range(seq_count)

    aq = [pick(a_qkv, s) for s in each]
    bq = [pick(b_qkv, s).reshape(rank, 3, model).transpose(1, 0, 2) for s in each]
    projected = [
        qkv_project(
            first_tokens[s], gain1, full_qkv, aq[s], bq[s], cosine[s], sine[s], pieces, width
        )
        for s in each
    ]
    headed = [swap(projected[s][0]) for s in each]
    attended = [attend(headed[s], cuts[s], tile) for s in each]
    o_tokens = [swap(attended[s][0]) for s in each]
    middle = []
    for s in each:
        b_in_s = pick(b_in, s)
        middle.append(
            mlp_call(
                tokens[s],
                cotangent[s],
                o_tokens[s],
                gain2,
                full_out,
                full_ff,
                pick(a_out, s),
                pick(b_out, s),
                pick(a_in, s),
                pad_columns(b_in_s[:, :hidden], padded),
                pad_columns(b_in_s[:, hidden:], padded),
                pad_columns(pick(a_out2, s), padded),
                pick(b_out2, s),
            )
        )
    do_items = [swap(middle[s][2]) for s in each]
    back = [
        attend_back(headed[s], attended[s][0], do_items[s], attended[s][1], cuts[s], tile)
        for s in each
    ]
    dqkv = [swap(back[s]) for s in each]
    final = [
        input_grad_call(
            dqkv[s], tokens[s], gain1, projected[s][1], projected[s][2], middle[s][1],
            full_qkv, aq[s], bq[s], cosine[s], sine[s],
        )
        for s in each
    ]

    chosen = (jnp.arange(adapters, dtype=jnp.int32)[:, None] == every_id[None, :]).astype(bf16)

    def assemble(every, blocks):
        return jnp.einsum(
            "es,sbrc->ebrc",
            chosen,
            every.reshape(dp * seq_count, blocks, rank, COL),
            preferred_element_type=f32,
        )

    def columns(blocked, first, count, size):
        part = blocked[:, first : first + count].transpose(0, 2, 1, 3)
        return part.reshape(adapters, rank, count * COL)[..., :size]

    def gather_early(per_sequence):
        stacked = jnp.concatenate(per_sequence, 0)
        blocks = stacked.shape[0] // seq_count
        lead = stacked.reshape(-1, COL)
        mine = lax.psum_scatter(lead, "seq", scatter_dimension=0, tiled=True).astype(bf16)
        return assemble(lax.all_gather(mine, both, axis=0, tiled=True), blocks)

    def spread(value, axis):
        count = lax.axis_size(axis)
        copies = jnp.broadcast_to(value[None], (count,) + value.shape)
        return lax.all_to_all(copies, axis, split_axis=0, concat_axis=0, tiled=True)

    def gather_late(per_sequence):
        stacked = jnp.stack(per_sequence, 0)
        blocks = stacked.shape[1]
        lead = stacked.astype(bf16).reshape(pieces, -1, COL)
        parts = lax.all_to_all(lead, "seq", split_axis=0, concat_axis=0, tiled=True)
        mine = jnp.sum(parts.astype(f32), 0).astype(bf16)
        every = spread(spread(mine, "seq"), "dp")
        return assemble(every, blocks)

    early = gather_early([middle[s][3] for s in each])
    late = gather_late([final[s][1] for s in each])
    ff = padded // COL
    per = model // COL
    layer_out = jnp.stack([middle[s][0] for s in each], 0)
    input_grad = jnp.stack([final[s][0] for s in each], 0)
    mods = 3 * ff
    return (
        layer_out,
        input_grad,
        columns(late, 0, per, model),
        columns(late, per, 3 * per, 3 * model),
        columns(early, mods, per, model),
        columns(early, mods + per, per, model),
        columns(early, mods + 2 * per, per, model),
        jnp.concatenate(
            [columns(early, 0, ff, hidden), columns(early, ff, ff, hidden)], -1
        ),
        columns(early, 2 * ff, ff, hidden),
        columns(early, mods + 3 * per, per, model),
    )


def solution(mesh):
    placed = (
        P("dp", "seq", None),
        P("dp", "seq"),
        P("dp", "seq"),
        P("dp"),
        P(),
        P(),
        P(("dp", "seq"), None),
        P(("dp", "seq"), None),
        P(("dp", "seq"), None),
        P(None, ("dp", "seq")),
        P(),
        P(),
        P(),
        P(),
        P(),
        P(),
        P(),
        P(),
        P("dp", "seq", None),
    )
    return jax.shard_map(
        local,
        mesh=mesh,
        in_specs=placed,
        out_specs=(
            P("dp", "seq", None),
            P("dp", "seq", None),
            P(),
            P(),
            P(),
            P(),
            P(),
            P(),
            P(),
            P(),
        ),
        check_vma=False,
    )
```

```python
import functools

import jax
import jax.numpy as jnp
from jax import lax
from jax.experimental import pallas as pl
from jax.experimental.pallas import tpu as pltpu
from jax.sharding import PartitionSpec as P

HEADS = 16
HD = 64
DOCS = 4
COL = 256
BLOCK_PAD = 1

eps_norm = 1e-05
theta_base = 160000.0
LOG2E = 1.4426950408889634
NEG = -1e30
RSQRT2 = 0.7071067811865476
RSQRT2PI = 0.3989422804014327
bf16 = jnp.bfloat16
f32 = jnp.float32


def nt(left, right):
    return lax.dot_general(left, right, (((1,), (1,)), ((), ())), preferred_element_type=f32)


def nn(left, right):
    return lax.dot_general(left, right, (((1,), (0,)), ((), ())), preferred_element_type=f32)


def tn(left, right):
    return lax.dot_general(left, right, (((0,), (0,)), ((), ())), preferred_element_type=f32)


def params():
    return pltpu.CompilerParams(dimension_semantics=("arbitrary",))


def work(amount):
    return pl.CostEstimate(flops=int(amount), transcendentals=0, bytes_accessed=0)


def whole_spec(shape):
    zeros = (0,) * len(shape)
    return pl.BlockSpec(shape, lambda *_: zeros)


def mask_heads(rows, heads, groups):
    if groups == 1:
        return rows
    lane = lax.broadcasted_iota(jnp.int32, rows.shape, 1)
    parts = [
        jnp.where((lane >= h * HD) & (lane < (h + 1) * HD), rows, jnp.zeros_like(rows))
        for h in heads
    ]
    return jnp.concatenate(parts, 0) if len(parts) > 1 else parts[0]


def inside(low, high, shape, axis):
    at = lax.broadcasted_iota(jnp.int32, shape, axis)
    return (at >= low) & (at < high)

def safe_keys(keys, low, high):
    pick = jnp.where(lax.broadcasted_iota(jnp.int32, (16, keys.shape[0]), 1) == low, 1.0, 0.0)
    row = nn(pick.astype(bf16), keys)[0:1, :].astype(bf16)
    return jnp.where(inside(low, high, keys.shape, 0), keys, jnp.broadcast_to(row, keys.shape))


def tile_range(cuts_ref, doc, index, tile, length):
    first = cuts_ref[doc]
    last = cuts_ref[doc + 1]
    nominal = (first // 16) * 16 + index * tile
    off = pl.multiple_of(jnp.minimum(nominal, length - tile), 16)
    low = jnp.maximum(nominal, first) - off
    high = jnp.minimum(nominal + tile, last) - off
    return off, low, high


def tile_count(cuts_ref, doc, tile):
    base = (cuts_ref[doc] // 16) * 16
    return lax.div(cuts_ref[doc + 1] - base + (tile - 1), tile)


def attend_kernel(
    cuts_ref, q_ref, k_ref, v_ref, o_ref, lse_ref, vt_ref, m_ref, acc_ref, *, tile, groups, length
):
    width = groups * HD
    qf = q_ref.reshape(length, width)
    kf = k_ref.reshape(length, width)
    vf = v_ref.reshape(length, width)
    of = o_ref.reshape(length, width)
    wide = groups * tile
    vt_ref[:, width:, :] = jnp.ones((vt_ref.shape[0], 16, tile), bf16)

    def doc_step(doc, first_tile):
        count = tile_count(cuts_ref, doc, tile)

        def prepare(j, carry):
            off, low, high = tile_range(cuts_ref, doc, j, tile, length)
            vt_ref[j, 0:width, :] = vf[pl.ds(off, tile), :].T
            return carry

        lax.fori_loop(0, count, prepare, 0)

        def q_tile(i, carry):
            off, low, high = tile_range(cuts_ref, doc, i, tile, length)
            qm = mask_heads(qf[pl.ds(off, tile), :] * bf16(0.125), range(groups), groups)
            m_ref[...] = jnp.full(m_ref.shape, NEG, f32)
            acc_ref[...] = jnp.zeros(acc_ref.shape, f32)

            def k_tile(j, inner):
                koff, klow, khigh = tile_range(cuts_ref, doc, j, tile, length)
                keep = inside(klow, khigh, (tile, wide), 0)
                s = jnp.where(keep, nt(kf[pl.ds(koff, tile), :], qm) * LOG2E, NEG)
                m_old = m_ref[0:1, :]
                m_new = jnp.maximum(m_old, jnp.max(s, axis=0, keepdims=True))
                p = jnp.exp2(s - m_new).astype(bf16)
                acc_ref[...] = acc_ref[...] * jnp.exp2(m_old - m_new) + nn(vt_ref[j], p)
                m_ref[0:1, :] = m_new
                return inner

            lax.fori_loop(0, count, k_tile, 0)
            total = acc_ref[width : width + 1, :]
            inverse = 1.0 / total
            lse_ref[first_tile + i, 0:1, :] = m_ref[0:1, :] + jnp.log2(total)
            parts = [
                acc_ref[h * HD : (h + 1) * HD, h * tile : (h + 1) * tile]
                * inverse[:, h * tile : (h + 1) * tile]
                for h in range(groups)
            ]
            out = (jnp.concatenate(parts, 0) if groups > 1 else parts[0]).T.astype(bf16)
            keep = inside(low, high, (tile, width), 0)
            of[pl.ds(off, tile), :] = jnp.where(keep, out, of[pl.ds(off, tile), :])
            return carry

        lax.fori_loop(0, count, q_tile, 0)
        return first_tile + count

    lax.fori_loop(0, DOCS, doc_step, 0)


def qkv_spec(shape, which):
    pieces, _, piece_len, width = shape
    return pl.BlockSpec((pieces, None, piece_len, width), lambda i, cuts: (0, which, 0, 0))


def attend(packed, cuts, tile):
    pieces, _, piece_len, width = packed.shape
    groups = width // HD
    length = pieces * piece_len
    tiles = length // tile + DOCS
    wide = groups * tile
    return pl.pallas_call(
        functools.partial(attend_kernel, tile=tile, groups=groups, length=length),
        out_shape=(
            jax.ShapeDtypeStruct((pieces, piece_len, width), bf16),
            jax.ShapeDtypeStruct((tiles, 8, wide), f32),
        ),
        grid_spec=pltpu.PrefetchScalarGridSpec(
            num_scalar_prefetch=1,
            grid=(1,),
            in_specs=[qkv_spec(packed.shape, w) for w in range(3)],
            out_specs=[whole_spec((pieces, piece_len, width)), whole_spec((tiles, 8, wide))],
            scratch_shapes=[
                pltpu.VMEM((length // tile + 1, width + 16, tile), bf16),
                pltpu.VMEM((8, wide), f32),
                pltpu.VMEM((width + 16, wide), f32),
            ],
        ),
        compiler_params=params(),
        name="attend",
        cost_estimate=work(8192 * length * wide),
    )(cuts, packed, packed, packed)


def attend_back_kernel(
    cuts_ref, q_ref, k_ref, v_ref, o_ref, do_ref, lse_ref, out_ref,
    qm_s, dom_s, lse_s, delta_s, dqt_s, ks_s, kt_s, p_s, ds_s, dk_s, dv_s, dqf, dkf, dvf,
    *, tile, groups, length, head,
):
    width = groups * HD
    own = slice(head * HD, (head + 1) * HD)
    qf = q_ref.reshape(length, width)
    kf = k_ref.reshape(length, width)
    vf = v_ref.reshape(length, width)
    of = o_ref.reshape(length, width)
    dof = do_ref.reshape(length, width)
    head_lane = lax.broadcasted_iota(jnp.int32, (16, width), 1)
    head_row = jnp.where(head_lane // HD == head, 1.0, 0.0).astype(bf16)

    def doc_step(doc, first_tile):
        count = tile_count(cuts_ref, doc, tile)

        def prepare(i, carry):
            off, low, high = tile_range(cuts_ref, doc, i, tile, length)
            spot = pl.ds(off, tile)
            qm_s[i] = mask_heads(qf[spot, :] * bf16(0.125), [head], groups)
            dom_s[i] = mask_heads(dof[spot, :], [head], groups)
            product = dof[spot, :].astype(f32) * of[spot, :].astype(f32)
            upper = product.astype(bf16)
            lower = (product - upper.astype(f32)).astype(bf16)
            delta_s[i, 0:1, :] = (nt(head_row, upper) + nt(head_row, lower))[0:1, :]
            lse = lse_ref[first_tile + i, 0:1, head * tile : (head + 1) * tile]
            lse_s[i, 0:1, :] = jnp.where(inside(low, high, (1, tile), 1), lse, -NEG)
            dqt_s[i] = jnp.zeros((HD, tile), f32)
            return carry

        lax.fori_loop(0, count, prepare, 0)

        def k_tile(j, carry):
            koff, klow, khigh = tile_range(cuts_ref, doc, j, tile, length)
            spot = pl.ds(koff, tile)
            keys = kf[spot, :]
            ks_s[...] = safe_keys(keys, klow, khigh)
            keys = jnp.where(inside(klow, khigh, keys.shape, 0), keys, jnp.zeros_like(keys))
            kt_s[...] = keys.T[own, :]
            dk_s[...] = jnp.zeros(dk_s.shape, f32)
            dv_s[...] = jnp.zeros(dv_s.shape, f32)

            def q_tile(i, inner):
                for c in range(0, tile, COL):
                    lanes = slice(c, c + COL)
                    qm = qm_s[i, lanes, :]
                    dom = dom_s[i, lanes, :]
                    for r in range(0, tile, COL):
                        rows = slice(r, r + COL)
                        s = nt(ks_s[rows, :], qm)
                        dp = nt(vf[pl.ds(pl.multiple_of(koff + r, 16), COL), :], dom)
                        p = jnp.exp2(s * LOG2E - lse_s[i, 0:1, lanes])
                        p_s[rows, lanes] = p.astype(bf16)
                        ds_s[rows, lanes] = (p * (dp - delta_s[i, 0:1, lanes])).astype(bf16)
                dv_s[...] += nn(p_s[...], dom_s[i])
                dk_s[...] += nn(ds_s[...], qm_s[i])
                dqt_s[i] += nn(kt_s[...], ds_s[...])
                return inner

            lax.fori_loop(0, count, q_tile, 0)
            keep = inside(klow, khigh, (tile, HD), 0)
            dkf[spot, :] = jnp.where(keep, dk_s[:, own].astype(bf16), dkf[spot, :])
            dvf[spot, :] = jnp.where(keep, dv_s[:, own].astype(bf16), dvf[spot, :])
            return carry

        lax.fori_loop(0, count, k_tile, 0)

        def finish(i, carry):
            off, low, high = tile_range(cuts_ref, doc, i, tile, length)
            out = (dqt_s[i] * 0.125).T.astype(bf16)
            spot = pl.ds(off, tile)
            dqf[spot, :] = jnp.where(inside(low, high, (tile, HD), 0), out, dqf[spot, :])
            return carry

        lax.fori_loop(0, count, finish, 0)
        return first_tile + count

    lax.fori_loop(0, DOCS, doc_step, 0)
    piece_len = q_ref.shape[1]
    fold = piece_len // groups
    for at in range(q_ref.shape[0]):
        for which, full in enumerate((dqf, dkf, dvf)):
            start = at * piece_len
            parts = [full[start + g * fold : start + (g + 1) * fold, :] for g in range(groups)]
            out_ref[at, which] = jnp.concatenate(parts, 1) if groups > 1 else parts[0]

def attend_back(packed, o, do, lse, cuts, tile, head):
    pieces, _, piece_len, width = packed.shape
    groups = width // HD
    length = pieces * piece_len
    tiles = length // tile + DOCS
    per_doc = length // tile + 1
    flat = whole_spec((pieces, piece_len, width))
    out = (pieces, 3, piece_len // groups, width)
    return pl.pallas_call(
        functools.partial(attend_back_kernel, tile=tile, groups=groups, length=length, head=head),
        out_shape=jax.ShapeDtypeStruct(out, bf16),
        grid_spec=pltpu.PrefetchScalarGridSpec(
            num_scalar_prefetch=1,
            grid=(1,),
            in_specs=[qkv_spec(packed.shape, w) for w in range(3)]
            + [flat, flat, whole_spec((tiles, 8, groups * tile))],
            out_specs=whole_spec(out),
            scratch_shapes=[
                pltpu.VMEM((per_doc, tile, width), bf16),
                pltpu.VMEM((per_doc, tile, width), bf16),
                pltpu.VMEM((per_doc, 8, tile), f32),
                pltpu.VMEM((per_doc, 8, tile), f32),
                pltpu.VMEM((per_doc, HD, tile), f32),
                pltpu.VMEM((tile, width), bf16),
                pltpu.VMEM((HD, tile), bf16),
                pltpu.VMEM((tile, tile), bf16),
                pltpu.VMEM((tile, tile), bf16),
                pltpu.VMEM((tile, width), f32),
                pltpu.VMEM((tile, width), f32),
            ]
            + [pltpu.VMEM((length, HD), bf16)] * 3,
        ),
        compiler_params=params(),
        name="attend_back",
        cost_estimate=work(16384 * length * tile),
    )(cuts, packed, packed, packed, o, do, lse)


def normalize(values):
    center = values - jnp.mean(values, axis=-1, keepdims=True)
    spread = jnp.mean(center * center, axis=-1, keepdims=True)
    scale = lax.rsqrt(spread + eps_norm)
    return center * scale, scale


def norm_back(unit, scale, scaled_grad):
    return scale * (
        scaled_grad
        - jnp.mean(scaled_grad, axis=-1, keepdims=True)
        - unit * jnp.mean(scaled_grad * unit, axis=-1, keepdims=True)
    )


def lane_swap(values):
    lane = lax.broadcasted_iota(jnp.int32, values.shape, 1)
    size = values.shape[1]
    half = HD // 2
    return jnp.where(
        lane % HD < half, pltpu.roll(values, size - half, 1), pltpu.roll(values, half, 1)
    )


def norm_kernel(x_ref, g_ref, a_ref, norm_ref, small_ref):
    unit, _ = normalize(x_ref[...].astype(f32))
    norm = (unit * g_ref[...]).astype(bf16)
    norm_ref[...] = norm
    small_ref[...] = nt(a_ref[...], norm).astype(bf16)


def norm_call(x, gain, a):
    count, rows, model = x.shape
    rank = a.shape[1]
    return pl.pallas_call(
        norm_kernel,
        grid=(count,),
        out_shape=(
            jax.ShapeDtypeStruct((count, rows, model), bf16),
            jax.ShapeDtypeStruct((count, rank, rows), bf16),
        ),
        in_specs=[
            pl.BlockSpec((None, rows, model), lambda s: (s, 0, 0)),
            whole_spec((1, model)),
            pl.BlockSpec((None, rank, model), lambda s: (s, 0, 0)),
        ],
        out_specs=[
            pl.BlockSpec((None, rows, model), lambda s: (s, 0, 0)),
            pl.BlockSpec((None, rank, rows), lambda s: (s, 0, 0)),
        ],
        compiler_params=params(),
        name="norm",
        cost_estimate=work(4096 * count * rows * model),
    )(x, gain, a)


def both_halves(core, own_ref, other_ref):
    groups, chips = own_ref.shape[:2]
    slabs = []
    for d in range(groups):
        for c in range(chips):
            own, other = own_ref[d, c], other_ref[d, c]
            slabs += [jnp.where(core == 0, own, other), jnp.where(core == 0, other, own)]
    return jnp.concatenate(slabs, 0)


def qkv_kernel(core_ref, norm_ref, small_ref, *refs, width):
    w_refs = refs[:6]
    b_ref, cos_ref, sin_ref, out_ref = refs[6:]
    core = core_ref[0]
    norm = norm_ref[...]
    small = small_ref[...]
    for which in range(3):
        w = both_halves(core, w_refs[2 * which], w_refs[2 * which + 1])
        lin = nn(norm, w) + tn(small, b_ref[which])
        for part in range(COL // 128):
            u = lin[:, part * 128 : (part + 1) * 128]
            if which < 2:
                u = u * cos_ref[...] + lane_swap(u) * sin_ref[...]
            u = u.astype(bf16)
            for sub in range(128 // width):
                out_ref[part * (128 // width) + sub, which] = u[:, sub * width : (sub + 1) * width]


def half_specs(shape, steps):
    block = shape[:-1] + (COL,)
    spec = lambda which: pl.BlockSpec(block, lambda j, core: (0, 0, 0, which * steps + j))
    return [spec(which) for which in range(3) for _ in range(2)]


def qkv_project(at, norm, small, core, halves, b, cosine, sine, pieces, width):
    _, rows, model = norm.shape
    dests = COL // width
    steps = model // COL
    rank = small.shape[1]
    row_spec = lambda shape: pl.BlockSpec((None,) + shape, lambda j, core: (at, 0, 0))
    return pl.pallas_call(
        functools.partial(qkv_kernel, width=width),
        out_shape=jax.ShapeDtypeStruct((pieces, 3, rows, width), bf16),
        grid_spec=pltpu.PrefetchScalarGridSpec(
            num_scalar_prefetch=1,
            grid=(steps,),
            in_specs=[row_spec((rows, model)), row_spec((rank, rows))]
            + half_specs(halves[0].shape, steps)
            + [
                pl.BlockSpec((3, rank, COL), lambda j, core: (0, 0, j)),
                row_spec((rows, 128)),
                row_spec((rows, 128)),
            ],
            out_specs=pl.BlockSpec((dests, 3, rows, width), lambda j, core: (j, 0, 0, 0)),
        ),
        compiler_params=params(),
        name="qkv_project",
        cost_estimate=work(6 * rows * model * model),
    )(core, norm, small, *halves * 3, b, cosine, sine)


def join_heads(refs, dest, which):
    if len(refs) == 1:
        return refs[0][dest, which]
    blocks = [ref[dest, which] for ref in refs]
    folds = [
        jnp.concatenate([block[:, g * HD : (g + 1) * HD] for block in blocks], 1)
        for g in range(len(refs))
    ]
    return jnp.concatenate(folds, 0)


def dlin_kernel(*args, width, heads):
    dqkv_refs = args[:heads]
    (norm_ref, small_ref, b_ref, cos_ref, sin_ref, dlin_ref, dsmall_ref, grad_ref, acc_ref) = args[
        heads:
    ]
    step = pl.program_id(0)

    @pl.when(step == 0)
    def _():
        acc_ref[...] = jnp.zeros(acc_ref.shape, f32)

    small = small_ref[...]
    per = 128 // width
    for which in range(3):
        pieces = []
        for part in range(COL // 128):
            subs = [join_heads(dqkv_refs, part * per + sub, which) for sub in range(per)]
            u = jnp.concatenate(subs, 1) if per > 1 else subs[0]
            if which < 2:
                u = u.astype(f32)
                u = (u * cos_ref[...] - lane_swap(u) * sin_ref[...]).astype(bf16)
            pieces.append(u)
        dlin = jnp.concatenate(pieces, 1)
        dlin_ref[which] = dlin
        acc_ref[...] += nt(b_ref[which], dlin)
        grad_ref[(which + 1) * pl.num_programs(0) + step] = nn(small, dlin)

    @pl.when(step == pl.num_programs(0) - 1)
    def _():
        dsmall = acc_ref[...].astype(bf16)
        dsmall_ref[...] = dsmall
        grad_a = nn(dsmall, norm_ref[...])
        for at in range(grad_a.shape[1] // COL):
            grad_ref[at] = grad_a[:, at * COL : (at + 1) * COL]


def dlin_call(at, dqkv, norm, small, b, cosine, sine):
    _, _, fold, width = dqkv[0].shape
    _, rows, model = norm.shape
    rank = small.shape[1]
    dests = COL // width
    steps = model // COL
    row_spec = lambda shape: pl.BlockSpec((None,) + shape, lambda j: (at, 0, 0))
    return pl.pallas_call(
        functools.partial(dlin_kernel, width=width, heads=len(dqkv)),
        grid=(steps,),
        out_shape=(
            jax.ShapeDtypeStruct((3, rows, model), bf16),
            jax.ShapeDtypeStruct((rank, rows), bf16),
            jax.ShapeDtypeStruct((4 * steps, rank, COL), f32),
        ),
        in_specs=[pl.BlockSpec((dests, 3, fold, width), lambda j: (j, 0, 0, 0))] * len(dqkv)
        + [
            row_spec((rows, model)),
            row_spec((rank, rows)),
            pl.BlockSpec((3, rank, COL), lambda j: (0, 0, j)),
            row_spec((rows, 128)),
            row_spec((rows, 128)),
        ],
        out_specs=[
            pl.BlockSpec((3, rows, COL), lambda j: (0, 0, j)),
            whole_spec((rank, rows)),
            whole_spec((4 * steps, rank, COL)),
        ],
        scratch_shapes=[pltpu.VMEM((rank, rows), f32)],
        compiler_params=params(),
        name="dlin",
        cost_estimate=work(4 * rows * model * model),
    )(*dqkv, norm, small, b, cosine, sine)


def input_grad_kernel(core_ref, dlin_ref, dsmall_ref, x_ref, g_ref, dmid_ref, *refs):
    w_refs = refs[:6]
    a_ref = refs[6]
    out_ref, acc_ref = refs[-2:]
    step = pl.program_id(0)
    core = core_ref[0]
    value = sum(
        nt(dlin_ref[which], both_halves(core, w_refs[2 * which], w_refs[2 * which + 1]))
        for which in range(3)
    )

    @pl.when(step == 0)
    def _():
        acc_ref[...] = value + tn(dsmall_ref[...], a_ref[...])

    @pl.when(step > 0)
    def _():
        acc_ref[...] += value

    @pl.when(step == pl.num_programs(0) - 1)
    def _():
        unit, scale = normalize(x_ref[...].astype(f32))
        out_ref[...] = (
            dmid_ref[...] + norm_back(unit, scale, acc_ref[...] * g_ref[...])
        ).astype(bf16)


def input_grad_call(at, count, given, dlin, dsmall, x, gain, dmid, core, halves, a):
    rows, model = x.shape
    given = [] if given is None else [given]
    rank = a.shape[0]
    steps = model // COL
    return pl.pallas_call(
        input_grad_kernel,
        out_shape=jax.ShapeDtypeStruct((count, rows, model), bf16),
        grid_spec=pltpu.PrefetchScalarGridSpec(
            num_scalar_prefetch=1,
            grid=(steps,),
            in_specs=[
                pl.BlockSpec((3, rows, COL), lambda j, core: (0, 0, j)),
                whole_spec((rank, rows)),
                whole_spec((rows, model)),
                whole_spec((1, model)),
                whole_spec((rows, model)),
            ]
            + half_specs(halves[0].shape, steps)
            + [whole_spec((rank, model))]
            + [pl.BlockSpec(memory_space=pl.ANY)] * len(given),
            out_specs=pl.BlockSpec((None, rows, model), lambda j, core: (at, 0, 0)),
            scratch_shapes=[pltpu.VMEM((rows, model), f32)],
        ),
        input_output_aliases={13: 0} if given else {},
        compiler_params=params(),
        name="input_grad",
        cost_estimate=work(8 * rows * model * model),
    )(core, dlin, dsmall, x, gain, dmid, *halves * 3, a, *given)


def mlp_kernel(
    x_ref, cot_ref, o_ref, g_ref, wo_ref, wu_ref, wv_ref, wt_ref,
    aout_ref, bout_ref, ain_ref, bu_ref, bv_ref, a2_ref, b2_ref, *rest, width, given,
):
    mlp_body(
        x_ref, cot_ref, o_ref, g_ref, wo_ref, wu_ref, wv_ref, wt_ref,
        aout_ref, bout_ref, ain_ref, bu_ref, bv_ref, a2_ref, b2_ref, *rest[given:], width=width,
    )


def natural(ref):
    cores, groups, chips = ref.shape[:3]
    return jnp.concatenate(
        [ref[core, d, c] for d in range(groups) for c in range(chips) for core in range(cores)], 0
    )


def mlp_body(
    x_ref, cot_ref, o_ref, g_ref, wo_ref, wu_ref, wv_ref, wt_ref,
    aout_ref, bout_ref, ain_ref, bu_ref, bv_ref, a2_ref, b2_ref,
    out_ref, dmid_ref, datt_ref, grad_ref,
    att_s, norm_s, unit_s, scale_s, acc_s, dnorm_s, small2_s, small3_s, small4_s, dsmall4_s, dsmall3_s,
    *, width,
):
    step = pl.program_id(0)
    pieces = o_ref.shape[0]
    model = x_ref.shape[1]
    per = model // COL
    first_block = grad_ref.shape[0] - BLOCK_PAD - 4 * per

    def put(which, value):
        for at in range(per):
            grad_ref[first_block + which * per + at] = value[:, at * COL : (at + 1) * COL]

    @pl.when(step == 0)
    def _():
        grad_ref[first_block + 4 * per :] = jnp.zeros((BLOCK_PAD,) + grad_ref.shape[1:], f32)
        for at in range(pieces):
            att_s[:, at * width : (at + 1) * width] = o_ref[at]
        att = att_s[...]
        small2 = nt(aout_ref[...], att).astype(bf16)
        small2_s[...] = small2
        middle = x_ref[...].astype(f32) + nn(att, natural(wo_ref)) + tn(small2, bout_ref[...])
        acc_s[...] = middle
        unit, scale = normalize(middle)
        unit_s[...] = unit
        scale_s[...] = jnp.broadcast_to(scale, scale_s.shape)
        norm = (unit * g_ref[...]).astype(bf16)
        norm_s[...] = norm
        small3_s[...] = nt(ain_ref[...], norm).astype(bf16)
        dsmall4_s[...] = nt(b2_ref[...], cot_ref[...]).astype(bf16)
        dnorm_s[...] = jnp.zeros(dnorm_s.shape, f32)
        small4_s[...] = jnp.zeros(small4_s.shape, f32)
        dsmall3_s[...] = jnp.zeros(dsmall3_s.shape, f32)

    norm = norm_s[...]
    small3 = small3_s[...]
    dsmall4 = dsmall4_s[...]
    wu, wv, wt = natural(wu_ref), natural(wv_ref), natural(wt_ref)
    u = nn(norm, wu) + tn(small3, bu_ref[...])
    v = nn(norm, wv) + tn(small3, bv_ref[...])
    dmixed = nn(cot_ref[...], wt) + tn(dsmall4, a2_ref[...])
    below = 0.5 * (1.0 + lax.erf(u * RSQRT2))
    gelu = u * below
    mixed = (gelu * v).astype(bf16)
    slope = below + u * (jnp.exp(-0.5 * u * u) * RSQRT2PI)
    du = (dmixed * v * slope).astype(bf16)
    dv = (dmixed * gelu).astype(bf16)
    acc_s[...] += nt(mixed, wt)
    dnorm_s[...] += nt(du, wu) + nt(dv, wv)
    small4_s[...] += nt(a2_ref[...], mixed)
    dsmall3_s[...] += nt(bu_ref[...], du) + nt(bv_ref[...], dv)
    steps = pl.num_programs(0)
    grad_ref[step] = nn(small3, du)
    grad_ref[steps + step] = nn(small3, dv)
    grad_ref[2 * steps + step] = nn(dsmall4, mixed)

    @pl.when(step == pl.num_programs(0) - 1)
    def _():
        small4 = small4_s[...].astype(bf16)
        dsmall3 = dsmall3_s[...].astype(bf16)
        out_ref[...] = (acc_s[...] + tn(small4, b2_ref[...])).astype(bf16)
        put(3, nn(small4, cot_ref[...]))
        dnorm = dnorm_s[...] + tn(dsmall3, ain_ref[...])
        put(2, nn(dsmall3, norm_s[...]))
        dmid = cot_ref[...].astype(f32) + norm_back(unit_s[...], scale_s[:, 0:1], dnorm * g_ref[...])
        dmid_ref[...] = dmid
        dlow = dmid.astype(bf16)
        dsmall2 = nt(bout_ref[...], dlow).astype(bf16)
        put(1, nn(small2_s[...], dlow))
        put(0, nn(dsmall2, att_s[...]))
        datt = (nt(dlow, natural(wo_ref)) + tn(dsmall2, aout_ref[...])).astype(bf16)
        for at in range(pieces):
            datt_ref[at] = datt[:, at * width : (at + 1) * width]


def mlp_call(which_seq, seq_count, grads, x, cot, o, gain, w_all, a_out, b_out, a_in, b_u, b_v, a_out2, b_out2):
    rows, model = x.shape
    pieces, _, width = o.shape
    rank = a_out.shape[0]
    hidden = b_u.shape[1]
    steps = hidden // COL
    blocks = 3 * steps + 4 * (model // COL) + BLOCK_PAD
    full = lambda shape: pl.BlockSpec(shape, lambda j: (0,) * len(shape), pipeline_mode=pl.Buffered(1))
    lead = w_all.shape[:-1]
    ff_spec = lambda which: pl.BlockSpec(
        lead + (COL,), lambda j: (0, 0, 0, 0, model // COL + which * steps + j)
    )
    given = [] if grads is None else [grads]
    small_ff = pl.BlockSpec((rank, COL), lambda j: (0, j))
    small = full((rank, model))
    return pl.pallas_call(
        functools.partial(mlp_kernel, width=width, given=len(given)),
        grid=(steps,),
        out_shape=(
            jax.ShapeDtypeStruct((rows, model), bf16),
            jax.ShapeDtypeStruct((rows, model), f32),
            jax.ShapeDtypeStruct((pieces, rows, width), bf16),
            jax.ShapeDtypeStruct((seq_count, blocks, rank, COL), f32),
        ),
        in_specs=[
            full((rows, model)),
            full((rows, model)),
            full((pieces, rows, width)),
            full((1, model)),
            full(lead + (model,)),
            ff_spec(0),
            ff_spec(1),
            ff_spec(2),
            small,
            small,
            small,
            small_ff,
            small_ff,
            small_ff,
            small,
        ]
        + [pl.BlockSpec(memory_space=pl.ANY)] * len(given),
        out_specs=[
            whole_spec((rows, model)),
            whole_spec((rows, model)),
            whole_spec((pieces, rows, width)),
            pl.BlockSpec((None, blocks, rank, COL), lambda j: (which_seq, 0, 0, 0)),
        ],
        scratch_shapes=[
            pltpu.VMEM((rows, model), bf16),
            pltpu.VMEM((rows, model), bf16),
            pltpu.VMEM((rows, model), f32),
            pltpu.VMEM((rows, 128), f32),
            pltpu.VMEM((rows, model), f32),
            pltpu.VMEM((rows, model), f32),
            pltpu.VMEM((rank, rows), bf16),
            pltpu.VMEM((rank, rows), bf16),
            pltpu.VMEM((rank, rows), f32),
            pltpu.VMEM((rank, rows), bf16),
            pltpu.VMEM((rank, rows), f32),
        ],
        compiler_params=params(),
        input_output_aliases={15: 3} if given else {},
        name="feed_forward",
        cost_estimate=work(26 * rows * model * hidden),
    )(
        x, cot, o, gain, w_all, w_all, w_all, w_all, a_out, b_out, a_in, b_u, b_v, a_out2, b_out2,
        *given,
    )


def assemble_kernel(ids_ref, *refs, layout, arrays):
    which = pl.program_id(0)
    sources, outs, acc_ref = refs[:arrays], refs[arrays:-1], refs[-1]
    acc_ref[...] = jnp.zeros(acc_ref.shape, f32)
    count = sources[0].shape[0]
    for at, source in enumerate(sources):

        def add(index, carry):
            @pl.when(ids_ref[at * count + index] == which)
            def _():
                acc_ref[...] += source[index].astype(f32)

            return carry

        lax.fori_loop(0, count, add, 0)
    for out_ref, segments in zip(outs, layout):
        start = 0
        for first, blocks, size in segments:
            for block in range(blocks):
                wide = min(COL, size - block * COL)
                if wide > 0:
                    spot = start + block * COL
                    out_ref[:, spot : spot + wide] = acc_ref[first + block][:, :wide]
            start += size


def assemble_call(sources, ids, adapters, layout):
    _, blocks, rank, _ = sources[0].shape
    sizes = [sum(size for _, _, size in segments) for segments in layout]
    return pl.pallas_call(
        functools.partial(assemble_kernel, layout=layout, arrays=len(sources)),
        out_shape=[jax.ShapeDtypeStruct((adapters, rank, size), f32) for size in sizes],
        grid_spec=pltpu.PrefetchScalarGridSpec(
            num_scalar_prefetch=1,
            grid=(adapters,),
            in_specs=[whole_spec(source.shape) for source in sources],
            out_specs=[pl.BlockSpec((None, rank, size), lambda e, ids: (e, 0, 0)) for size in sizes],
            scratch_shapes=[pltpu.VMEM((blocks, rank, COL), f32)],
        ),
        compiler_params=params(),
        name="assemble",
        cost_estimate=work(4096 * adapters * rank * sum(sizes) // 256),
    )(ids, *sources)


def pad_columns(values, size):
    return jnp.pad(values, [(0, 0)] * (values.ndim - 1) + [(0, size - values.shape[-1])])


def local(
    tokens,
    segment_ids,
    positions,
    adapter_id,
    gain_attn,
    gain_mlp,
    w_qkv,
    w_out,
    w_in,
    w_out2,
    a_qkv,
    b_qkv,
    a_out,
    b_out,
    a_in,
    b_in,
    a_out2,
    b_out2,
    cotangent,
):
    seq_count, piece_len, model = tokens.shape
    pieces = lax.axis_size("seq")
    groups = HEADS // pieces
    width = groups * HD
    length = piece_len * pieces
    rank = a_qkv.shape[1]
    adapters = a_qkv.shape[0]
    hidden = w_out2.shape[0]
    padded = -(-hidden // COL) * COL
    tile = min(512, length)
    both = ("dp", "seq")

    dp = lax.axis_size("dp")
    group = lax.axis_index("dp")
    before = [jnp.sum((segment_ids < d).astype(jnp.int32), axis=1) for d in range(1, DOCS)]
    facts = jnp.stack(before + [adapter_id], 1)
    facts = lax.all_to_all(
        jnp.broadcast_to(facts[None], (dp * pieces,) + facts.shape),
        both,
        split_axis=0,
        concat_axis=0,
        tiled=True,
    ).reshape(dp, pieces, seq_count, DOCS)
    every_id = facts[:, 0, :, DOCS - 1].reshape(-1)
    counts = jnp.sum(lax.dynamic_index_in_dim(facts, group, 0, keepdims=False), 0)[:, : DOCS - 1]
    shard = jnp.concatenate(
        [
            w_qkv,
            w_out,
            pad_columns(w_in[:, :hidden], padded),
            pad_columns(w_in[:, hidden:], padded),
            pad_columns(w_out2.T, padded),
        ],
        1,
    )
    chips = pieces // 2
    same_core = [[2 * chip + core for chip in range(chips)] for core in range(2)]
    same_chip = [[2 * chip, 2 * chip + 1] for chip in range(chips)]
    half = HD // 2
    lane = jnp.arange(128, dtype=jnp.int32) % HD
    frequency = theta_base ** (-((lane % half).astype(f32) * 2.0) / HD)
    angles = positions.astype(f32)[..., None] * frequency
    cosine = jnp.cos(angles)
    sine = jnp.where(lane < half, -1.0, 1.0) * jnp.sin(angles)

    gain1 = gain_attn.reshape(1, model)
    gain2 = gain_mlp.reshape(1, model)
    pick = lambda table, s: lax.dynamic_index_in_dim(table, adapter_id[s], 0, keepdims=False)
    swap = lambda value: lax.all_to_all(value, "seq", split_axis=0, concat_axis=0, tiled=True)
    each = range(seq_count)

    aq = [pick(a_qkv, s) for s in each]
    bq = [pick(b_qkv, s).reshape(rank, 3, model).transpose(1, 0, 2) for s in each]
    norm, small = norm_call(tokens, gain1, jnp.stack(aq, 0))
    maps = []
    for s in each:
        b_in_s = pick(b_in, s)
        maps.append(
            (
                pick(a_out, s),
                pick(b_out, s),
                pick(a_in, s),
                pad_columns(b_in_s[:, :hidden], padded),
                pad_columns(b_in_s[:, hidden:], padded),
                pad_columns(pick(a_out2, s), padded),
                pick(b_out2, s),
            )
        )
    same_pair = [(at, at ^ 1) for at in range(pieces)]
    core = (lax.axis_index("seq") % 2).astype(jnp.int32).reshape(1)
    column = lax.all_gather(shard, "seq", axis=0, tiled=True, axis_index_groups=same_core)
    ready = (column, counts, norm, small, cosine, sine, bq, maps)
    column, counts, norm, small, cosine, sine, bq, maps = lax.optimization_barrier(ready)
    qkv_own = lax.all_gather(column[:, : 3 * model], "dp", axis=0, tiled=True)
    qkv_own = qkv_own.reshape(dp, chips, -1, 3 * model)
    column, qkv_own = lax.optimization_barrier((column[:, 3 * model :], qkv_own))
    qkv_other = lax.ppermute(qkv_own, "seq", same_pair)
    own = lax.all_gather(column, "dp", axis=0, tiled=True)
    halves = [qkv_own, qkv_other]

    cuts = jnp.concatenate(
        [
            jnp.zeros((seq_count, 1), jnp.int32),
            counts,
            jnp.full((seq_count, 1), length, jnp.int32),
        ],
        1,
    )
    packed = []
    for s in each:
        packed.append(qkv_project(s, norm, small, core, halves, bq[s], cosine, sine, pieces, width))
        norm, packed[s] = lax.optimization_barrier((norm, packed[s]))
    headed = [swap(packed[0])]
    packed[1], headed[0] = lax.optimization_barrier((packed[1], headed[0]))
    headed += [swap(packed[s]) for s in each[1:]]
    attended = [attend(headed[0], cuts[0], tile)]
    headed[1], own, attended[0] = lax.optimization_barrier((headed[1], own, attended[0]))
    full_rest = lax.all_gather(own, "seq", axis=0, tiled=True, axis_index_groups=same_chip)
    full_rest = full_rest.reshape(2, dp, chips, -1, full_rest.shape[-1])
    attended += [attend(headed[s], cuts[s], tile) for s in each[1:]]
    o_tokens = [swap(attended[s][0]) for s in each]
    middle = []
    for s in each:
        middle.append(
            mlp_call(
                s,
                seq_count,
                middle[s - 1][3] if s else None,
                tokens[s],
                cotangent[s],
                o_tokens[s],
                gain2,
                full_rest,
                *maps[s],
            )
        )
    early_grads = middle[-1][3]
    do_items = [swap(middle[s][2]) for s in each]
    do_items[0], early_grads = lax.optimization_barrier((do_items[0], early_grads))
    blocks = early_grads.shape[1]
    summed = lax.psum_scatter(
        early_grads.reshape(-1, COL), "seq", scatter_dimension=0, tiled=True
    ).astype(bf16)
    ff = padded // COL
    per = model // COL
    mods = 3 * ff

    def back(s, h):
        return attend_back(
            headed[s], attended[s][0], do_items[s], attended[s][1], cuts[s], tile, h
        )

    def dlin_of(s):
        return dlin_call(s, dqkv[s], norm, small, bq[s], cosine, sine)

    def input_grad_of(s, dlin, given):
        return input_grad_call(
            s, seq_count, given, dlin[0], dlin[1], tokens[s], gain1, middle[s][1], core, halves, aq[s]
        )

    first_back, summed, do_items = lax.optimization_barrier((back(0, 0), summed, do_items))
    dqkv = [[swap(first_back)]]
    gathered = lax.all_gather(summed, both, axis=0, tiled=True).reshape(-1, blocks, rank, COL)
    dqkv[0] += [swap(back(0, h)) for h in range(1, groups)]
    dqkv += [[swap(back(s, h)) for h in range(groups)] for s in each[1:]]
    dlins = [dlin_of(0)]
    input_grads = input_grad_of(0, dlins[0], None)
    early = assemble_call(
        [gathered],
        every_id,
        adapters,
        [[(mods + which * per, per, model)] for which in range(3)]
        + [[(0, ff, hidden), (ff, ff, hidden)], [(2 * ff, ff, hidden)], [(mods + 3 * per, per, model)]],
    )
    dqkv[1], early, input_grads = lax.optimization_barrier((dqkv[1], early, input_grads))
    dlins += [dlin_of(s) for s in each[1:]]
    late_grads = jnp.stack([dlins[s][2] for s in each], 0)
    parts = swap(late_grads.astype(bf16).reshape(pieces, -1, COL))
    mine = jnp.sum(parts.astype(f32), 0).astype(bf16)
    copies = jnp.broadcast_to(mine[None], (dp * pieces,) + mine.shape)
    every = lax.all_to_all(copies, both, split_axis=0, concat_axis=0, tiled=True)
    for s in each[1:]:
        input_grads = input_grad_of(s, dlins[s], input_grads)
    late = assemble_call(
        [every.reshape((dp * seq_count,) + late_grads.shape[1:])],
        every_id,
        adapters,
        [[(0, per, model)], [(per, 3 * per, 3 * model)]],
    )
    layer_out = jnp.stack([middle[s][0] for s in each], 0)
    return (
        layer_out,
        input_grads,
        late[0],
        late[1],
        early[0],
        early[1],
        early[2],
        early[3],
        early[4],
        early[5],
    )


def solution(mesh):
    placed = (
        P("dp", "seq", None),
        P("dp", "seq"),
        P("dp", "seq"),
        P("dp"),
        P(),
        P(),
        P(("dp", "seq"), None),
        P(("dp", "seq"), None),
        P(("dp", "seq"), None),
        P(None, ("dp", "seq")),
        P(),
        P(),
        P(),
        P(),
        P(),
        P(),
        P(),
        P(),
        P("dp", "seq", None),
    )
    return jax.shard_map(
        local,
        mesh=mesh,
        in_specs=placed,
        out_specs=(
            P("dp", "seq", None),
            P("dp", "seq", None),
            P(),
            P(),
            P(),
            P(),
            P(),
            P(),
            P(),
            P(),
        ),
        check_vma=False,
    )
```

```python
import functools

import jax
import jax.numpy as jnp
from jax import lax
from jax.experimental import pallas as pl
from jax.experimental.pallas import tpu as pltpu
from jax.sharding import PartitionSpec as P

HEADS = 16
HD = 64
DOCS = 4
COL = 256
BLOCK_PAD = 7

eps_norm = 1e-05
theta_base = 160000.0
LOG2E = 1.4426950408889634
NEG = -1e30
RSQRT2 = 0.7071067811865476
RSQRT2PI = 0.3989422804014327
bf16 = jnp.bfloat16
f32 = jnp.float32


def nt(left, right):
    return lax.dot_general(left, right, (((1,), (1,)), ((), ())), preferred_element_type=f32)


def nn(left, right):
    return lax.dot_general(left, right, (((1,), (0,)), ((), ())), preferred_element_type=f32)


def tn(left, right):
    return lax.dot_general(left, right, (((0,), (0,)), ((), ())), preferred_element_type=f32)


def params():
    return pltpu.CompilerParams(dimension_semantics=("arbitrary",))


def work(amount):
    return pl.CostEstimate(flops=int(amount), transcendentals=0, bytes_accessed=0)


def whole_spec(shape):
    zeros = (0,) * len(shape)
    return pl.BlockSpec(shape, lambda *_: zeros)


def mask_heads(rows, heads, groups):
    if groups == 1:
        return rows
    lane = lax.broadcasted_iota(jnp.int32, rows.shape, 1)
    parts = [
        jnp.where((lane >= h * HD) & (lane < (h + 1) * HD), rows, jnp.zeros_like(rows))
        for h in heads
    ]
    return jnp.concatenate(parts, 0) if len(parts) > 1 else parts[0]


def inside(low, high, shape, axis):
    at = lax.broadcasted_iota(jnp.int32, shape, axis)
    return (at >= low) & (at < high)

def safe_keys(keys, low, high):
    pick = jnp.where(lax.broadcasted_iota(jnp.int32, (16, keys.shape[0]), 1) == low, 1.0, 0.0)
    row = nn(pick.astype(bf16), keys)[0:1, :].astype(bf16)
    return jnp.where(inside(low, high, keys.shape, 0), keys, jnp.broadcast_to(row, keys.shape))


def tile_range(cuts_ref, doc, index, tile, length):
    first = cuts_ref[doc]
    last = cuts_ref[doc + 1]
    nominal = (first // 16) * 16 + index * tile
    off = pl.multiple_of(jnp.minimum(nominal, length - tile), 16)
    low = jnp.maximum(nominal, first) - off
    high = jnp.minimum(nominal + tile, last) - off
    return off, low, high


def tile_count(cuts_ref, doc, tile):
    base = (cuts_ref[doc] // 16) * 16
    return lax.div(cuts_ref[doc + 1] - base + (tile - 1), tile)


def attend_kernel(
    cuts_ref, q_ref, k_ref, v_ref, o_ref, lse_ref, vt_ref, m_ref, acc_ref, *, tile, groups, length
):
    width = groups * HD
    qf = q_ref.reshape(length, width)
    kf = k_ref.reshape(length, width)
    vf = v_ref.reshape(length, width)
    of = o_ref.reshape(length, width)
    wide = groups * tile
    vt_ref[:, width:, :] = jnp.ones((vt_ref.shape[0], 16, tile), bf16)

    def doc_step(doc, first_tile):
        count = tile_count(cuts_ref, doc, tile)

        def prepare(j, carry):
            off, low, high = tile_range(cuts_ref, doc, j, tile, length)
            vt_ref[j, 0:width, :] = vf[pl.ds(off, tile), :].T
            return carry

        lax.fori_loop(0, count, prepare, 0)

        def q_tile(i, carry):
            off, low, high = tile_range(cuts_ref, doc, i, tile, length)
            qm = mask_heads(qf[pl.ds(off, tile), :] * bf16(0.125), range(groups), groups)
            m_ref[...] = jnp.full(m_ref.shape, NEG, f32)
            acc_ref[...] = jnp.zeros(acc_ref.shape, f32)

            def k_tile(j, inner):
                koff, klow, khigh = tile_range(cuts_ref, doc, j, tile, length)
                keep = inside(klow, khigh, (tile, wide), 0)
                s = jnp.where(keep, nt(kf[pl.ds(koff, tile), :], qm) * LOG2E, NEG)
                m_old = m_ref[0:1, :]
                m_new = jnp.maximum(m_old, jnp.max(s, axis=0, keepdims=True))
                p = jnp.exp2(s - m_new).astype(bf16)
                acc_ref[...] = acc_ref[...] * jnp.exp2(m_old - m_new) + nn(vt_ref[j], p)
                m_ref[0:1, :] = m_new
                return inner

            lax.fori_loop(0, count, k_tile, 0)
            total = acc_ref[width : width + 1, :]
            inverse = 1.0 / total
            lse_ref[first_tile + i, 0:1, :] = m_ref[0:1, :] + jnp.log2(total)
            parts = [
                acc_ref[h * HD : (h + 1) * HD, h * tile : (h + 1) * tile]
                * inverse[:, h * tile : (h + 1) * tile]
                for h in range(groups)
            ]
            out = (jnp.concatenate(parts, 0) if groups > 1 else parts[0]).T.astype(bf16)
            keep = inside(low, high, (tile, width), 0)
            of[pl.ds(off, tile), :] = jnp.where(keep, out, of[pl.ds(off, tile), :])
            return carry

        lax.fori_loop(0, count, q_tile, 0)
        return first_tile + count

    lax.fori_loop(0, DOCS, doc_step, 0)


def qkv_operands(headed):
    pieces, _, piece_len, width = headed[0].shape
    at = [(headed[0], 0), (headed[0], 1), (headed[-1], headed[-1].shape[1] - 1)]
    spec = lambda which: pl.BlockSpec(
        (pieces, None, piece_len, width), lambda i, cuts: (0, which, 0, 0)
    )
    return [array for array, _ in at], [spec(which) for _, which in at]


def attend(headed, cuts, tile):
    operands, specs = qkv_operands(headed)
    pieces, _, piece_len, width = headed[0].shape
    groups = width // HD
    length = pieces * piece_len
    tiles = length // tile + DOCS
    wide = groups * tile
    return pl.pallas_call(
        functools.partial(attend_kernel, tile=tile, groups=groups, length=length),
        out_shape=(
            jax.ShapeDtypeStruct((pieces, piece_len, width), bf16),
            jax.ShapeDtypeStruct((tiles, 8, wide), f32),
        ),
        grid_spec=pltpu.PrefetchScalarGridSpec(
            num_scalar_prefetch=1,
            grid=(1,),
            in_specs=specs,
            out_specs=[whole_spec((pieces, piece_len, width)), whole_spec((tiles, 8, wide))],
            scratch_shapes=[
                pltpu.VMEM((length // tile + 1, width + 16, tile), bf16),
                pltpu.VMEM((8, wide), f32),
                pltpu.VMEM((width + 16, wide), f32),
            ],
        ),
        compiler_params=params(),
        name="attend",
        cost_estimate=work(8192 * length * wide),
    )(cuts, *operands)


def attend_back_kernel(
    cuts_ref, q_ref, k_ref, v_ref, o_ref, do_ref, lse_ref, out_ref,
    qm_s, dom_s, lse_s, delta_s, dqt_s, ks_s, kt_s, p_s, ds_s, dk_s, dv_s, dqf, dkf, dvf,
    *, tile, groups, length, head,
):
    width = groups * HD
    own = slice(head * HD, (head + 1) * HD)
    qf = q_ref.reshape(length, width)
    kf = k_ref.reshape(length, width)
    vf = v_ref.reshape(length, width)
    of = o_ref.reshape(length, width)
    dof = do_ref.reshape(length, width)
    head_lane = lax.broadcasted_iota(jnp.int32, (16, width), 1)
    head_row = jnp.where(head_lane // HD == head, 1.0, 0.0).astype(bf16)

    def doc_step(doc, first_tile):
        count = tile_count(cuts_ref, doc, tile)

        def prepare(i, carry):
            off, low, high = tile_range(cuts_ref, doc, i, tile, length)
            spot = pl.ds(off, tile)
            qm_s[i] = mask_heads(qf[spot, :] * bf16(0.125), [head], groups)
            dom_s[i] = mask_heads(dof[spot, :], [head], groups)
            product = dof[spot, :].astype(f32) * of[spot, :].astype(f32)
            upper = product.astype(bf16)
            lower = (product - upper.astype(f32)).astype(bf16)
            delta_s[i, 0:1, :] = (nt(head_row, upper) + nt(head_row, lower))[0:1, :]
            lse = lse_ref[first_tile + i, 0:1, head * tile : (head + 1) * tile]
            lse_s[i, 0:1, :] = jnp.where(inside(low, high, (1, tile), 1), lse, -NEG)
            dqt_s[i] = jnp.zeros((HD, tile), f32)
            return carry

        lax.fori_loop(0, count, prepare, 0)

        def k_tile(j, carry):
            koff, klow, khigh = tile_range(cuts_ref, doc, j, tile, length)
            spot = pl.ds(koff, tile)
            keys = kf[spot, :]
            ks_s[...] = safe_keys(keys, klow, khigh)
            keys = jnp.where(inside(klow, khigh, keys.shape, 0), keys, jnp.zeros_like(keys))
            kt_s[...] = keys.T[own, :]
            dk_s[...] = jnp.zeros(dk_s.shape, f32)
            dv_s[...] = jnp.zeros(dv_s.shape, f32)

            def q_tile(i, inner):
                for c in range(0, tile, COL):
                    lanes = slice(c, c + COL)
                    qm = qm_s[i, lanes, :]
                    dom = dom_s[i, lanes, :]
                    for r in range(0, tile, COL):
                        rows = slice(r, r + COL)
                        s = nt(ks_s[rows, :], qm)
                        dp = nt(vf[pl.ds(pl.multiple_of(koff + r, 16), COL), :], dom)
                        p = jnp.exp2(s * LOG2E - lse_s[i, 0:1, lanes])
                        p_s[rows, lanes] = p.astype(bf16)
                        ds_s[rows, lanes] = (p * (dp - delta_s[i, 0:1, lanes])).astype(bf16)
                dv_s[...] += nn(p_s[...], dom_s[i])
                dk_s[...] += nn(ds_s[...], qm_s[i])
                dqt_s[i] += nn(kt_s[...], ds_s[...])
                return inner

            lax.fori_loop(0, count, q_tile, 0)
            keep = inside(klow, khigh, (tile, HD), 0)
            dkf[spot, :] = jnp.where(keep, dk_s[:, own].astype(bf16), dkf[spot, :])
            dvf[spot, :] = jnp.where(keep, dv_s[:, own].astype(bf16), dvf[spot, :])
            return carry

        lax.fori_loop(0, count, k_tile, 0)

        def finish(i, carry):
            off, low, high = tile_range(cuts_ref, doc, i, tile, length)
            out = (dqt_s[i] * 0.125).T.astype(bf16)
            spot = pl.ds(off, tile)
            dqf[spot, :] = jnp.where(inside(low, high, (tile, HD), 0), out, dqf[spot, :])
            return carry

        lax.fori_loop(0, count, finish, 0)
        return first_tile + count

    lax.fori_loop(0, DOCS, doc_step, 0)
    piece_len = q_ref.shape[1]
    fold = piece_len // groups
    for at in range(q_ref.shape[0]):
        for which, full in enumerate((dqf, dkf, dvf)):
            start = at * piece_len
            parts = [full[start + g * fold : start + (g + 1) * fold, :] for g in range(groups)]
            out_ref[at, which] = jnp.concatenate(parts, 1) if groups > 1 else parts[0]

def attend_back(headed, o, do, lse, cuts, tile, head):
    operands, specs = qkv_operands(headed)
    pieces, _, piece_len, width = headed[0].shape
    groups = width // HD
    length = pieces * piece_len
    tiles = length // tile + DOCS
    per_doc = length // tile + 1
    flat = whole_spec((pieces, piece_len, width))
    out = (pieces, 3, piece_len // groups, width)
    return pl.pallas_call(
        functools.partial(attend_back_kernel, tile=tile, groups=groups, length=length, head=head),
        out_shape=jax.ShapeDtypeStruct(out, bf16),
        grid_spec=pltpu.PrefetchScalarGridSpec(
            num_scalar_prefetch=1,
            grid=(1,),
            in_specs=specs
            + [flat, flat, whole_spec((tiles, 8, groups * tile))],
            out_specs=whole_spec(out),
            scratch_shapes=[
                pltpu.VMEM((per_doc, tile, width), bf16),
                pltpu.VMEM((per_doc, tile, width), bf16),
                pltpu.VMEM((per_doc, 8, tile), f32),
                pltpu.VMEM((per_doc, 8, tile), f32),
                pltpu.VMEM((per_doc, HD, tile), f32),
                pltpu.VMEM((tile, width), bf16),
                pltpu.VMEM((HD, tile), bf16),
                pltpu.VMEM((tile, tile), bf16),
                pltpu.VMEM((tile, tile), bf16),
                pltpu.VMEM((tile, width), f32),
                pltpu.VMEM((tile, width), f32),
            ]
            + [pltpu.VMEM((length, HD), bf16)] * 3,
        ),
        compiler_params=params(),
        name="attend_back",
        cost_estimate=work(16384 * length * tile),
    )(cuts, *operands, o, do, lse)


def normalize(values):
    center = values - jnp.mean(values, axis=-1, keepdims=True)
    spread = jnp.mean(center * center, axis=-1, keepdims=True)
    scale = lax.rsqrt(spread + eps_norm)
    return center * scale, scale


def norm_back(unit, scale, scaled_grad):
    return scale * (
        scaled_grad
        - jnp.mean(scaled_grad, axis=-1, keepdims=True)
        - unit * jnp.mean(scaled_grad * unit, axis=-1, keepdims=True)
    )


def lane_swap(values):
    lane = lax.broadcasted_iota(jnp.int32, values.shape, 1)
    size = values.shape[1]
    half = HD // 2
    return jnp.where(
        lane % HD < half, pltpu.roll(values, size - half, 1), pltpu.roll(values, half, 1)
    )


def norm_kernel(x_ref, g_ref, a_ref, norm_ref, small_ref):
    unit, _ = normalize(x_ref[...].astype(f32))
    norm = (unit * g_ref[...]).astype(bf16)
    norm_ref[...] = norm
    small_ref[...] = nt(a_ref[...], norm).astype(bf16)


def norm_call(x, gain, a):
    count, rows, model = x.shape
    rank = a.shape[1]
    return pl.pallas_call(
        norm_kernel,
        grid=(count,),
        out_shape=(
            jax.ShapeDtypeStruct((count, rows, model), bf16),
            jax.ShapeDtypeStruct((count, rank, rows), bf16),
        ),
        in_specs=[
            pl.BlockSpec((None, rows, model), lambda s: (s, 0, 0)),
            whole_spec((1, model)),
            pl.BlockSpec((None, rank, model), lambda s: (s, 0, 0)),
        ],
        out_specs=[
            pl.BlockSpec((None, rows, model), lambda s: (s, 0, 0)),
            pl.BlockSpec((None, rank, rows), lambda s: (s, 0, 0)),
        ],
        compiler_params=params(),
        name="norm",
        cost_estimate=work(4096 * count * rows * model),
    )(x, gain, a)


def both_halves(core, own_ref, other_ref):
    groups, chips = own_ref.shape[:2]
    slabs = []
    for d in range(groups):
        for c in range(chips):
            own, other = own_ref[d, c], other_ref[d, c]
            slabs += [jnp.where(core == 0, own, other), jnp.where(core == 0, other, own)]
    return jnp.concatenate(slabs, 0)


def qkv_kernel(core_ref, norm_ref, small_ref, *refs, width):
    w_refs = refs[:6]
    b_ref, cos_ref, sin_ref = refs[6:9]
    outs = refs[9:]
    core = core_ref[0]
    norm = norm_ref[...]
    small = small_ref[...]
    for which in range(3):
        w = both_halves(core, w_refs[2 * which], w_refs[2 * which + 1])
        lin = nn(norm, w) + tn(small, b_ref[which])
        for part in range(COL // 128):
            u = lin[:, part * 128 : (part + 1) * 128]
            if which < 2:
                u = u * cos_ref[...] + lane_swap(u) * sin_ref[...]
            u = u.astype(bf16)
            for sub in range(128 // width):
                dest = part * (128 // width) + sub
                value = u[:, sub * width : (sub + 1) * width]
                if which == 2 and len(outs) == 2:
                    outs[1][dest, 0] = value
                else:
                    outs[0][dest, which] = value


def half_specs(shape, steps):
    block = shape[:-1] + (COL,)
    spec = lambda which: pl.BlockSpec(block, lambda j, core: (0, 0, 0, which * steps + j))
    return [spec(which) for which in range(3) for _ in range(2)]


def qkv_project(at, split, norm, small, core, halves, b, cosine, sine, pieces, width):
    _, rows, model = norm.shape
    dests = COL // width
    steps = model // COL
    rank = small.shape[1]
    row_spec = lambda shape: pl.BlockSpec((None,) + shape, lambda j, core: (at, 0, 0))
    return pl.pallas_call(
        functools.partial(qkv_kernel, width=width),
        out_shape=[jax.ShapeDtypeStruct((pieces, n, rows, width), bf16) for n in split],
        grid_spec=pltpu.PrefetchScalarGridSpec(
            num_scalar_prefetch=1,
            grid=(steps,),
            in_specs=[row_spec((rows, model)), row_spec((rank, rows))]
            + half_specs(halves[0].shape, steps)
            + [
                pl.BlockSpec((3, rank, COL), lambda j, core: (0, 0, j)),
                row_spec((rows, 128)),
                row_spec((rows, 128)),
            ],
            out_specs=[
                pl.BlockSpec((dests, n, rows, width), lambda j, core: (j, 0, 0, 0)) for n in split
            ],
        ),
        compiler_params=params(),
        name="qkv_project",
        cost_estimate=work(6 * rows * model * model),
    )(core, norm, small, *halves * 3, b, cosine, sine)


def join_heads(refs, dest, which):
    if len(refs) == 1:
        return refs[0][dest, which]
    blocks = [ref[dest, which] for ref in refs]
    folds = [
        jnp.concatenate([block[:, g * HD : (g + 1) * HD] for block in blocks], 1)
        for g in range(len(refs))
    ]
    return jnp.concatenate(folds, 0)


def dlin_kernel(*args, width, heads):
    dqkv_refs = args[:heads]
    (norm_ref, small_ref, b_ref, cos_ref, sin_ref, dlin_ref, dsmall_ref, grad_ref, acc_ref) = args[
        heads:
    ]
    step = pl.program_id(0)

    @pl.when(step == 0)
    def _():
        acc_ref[...] = jnp.zeros(acc_ref.shape, f32)

    small = small_ref[...]
    per = 128 // width
    for which in range(3):
        pieces = []
        for part in range(COL // 128):
            subs = [join_heads(dqkv_refs, part * per + sub, which) for sub in range(per)]
            u = jnp.concatenate(subs, 1) if per > 1 else subs[0]
            if which < 2:
                u = u.astype(f32)
                u = (u * cos_ref[...] - lane_swap(u) * sin_ref[...]).astype(bf16)
            pieces.append(u)
        dlin = jnp.concatenate(pieces, 1)
        dlin_ref[which] = dlin
        acc_ref[...] += nt(b_ref[which], dlin)
        grad_ref[(which + 1) * pl.num_programs(0) + step] = nn(small, dlin)

    @pl.when(step == pl.num_programs(0) - 1)
    def _():
        dsmall = acc_ref[...].astype(bf16)
        dsmall_ref[...] = dsmall
        grad_a = nn(dsmall, norm_ref[...])
        for at in range(grad_a.shape[1] // COL):
            grad_ref[at] = grad_a[:, at * COL : (at + 1) * COL]


def dlin_call(at, dqkv, norm, small, b, cosine, sine):
    _, _, fold, width = dqkv[0].shape
    _, rows, model = norm.shape
    rank = small.shape[1]
    dests = COL // width
    steps = model // COL
    row_spec = lambda shape: pl.BlockSpec((None,) + shape, lambda j: (at, 0, 0))
    return pl.pallas_call(
        functools.partial(dlin_kernel, width=width, heads=len(dqkv)),
        grid=(steps,),
        out_shape=(
            jax.ShapeDtypeStruct((3, rows, model), bf16),
            jax.ShapeDtypeStruct((rank, rows), bf16),
            jax.ShapeDtypeStruct((4 * steps, rank, COL), f32),
        ),
        in_specs=[pl.BlockSpec((dests, 3, fold, width), lambda j: (j, 0, 0, 0))] * len(dqkv)
        + [
            row_spec((rows, model)),
            row_spec((rank, rows)),
            pl.BlockSpec((3, rank, COL), lambda j: (0, 0, j)),
            row_spec((rows, 128)),
            row_spec((rows, 128)),
        ],
        out_specs=[
            pl.BlockSpec((3, rows, COL), lambda j: (0, 0, j)),
            whole_spec((rank, rows)),
            whole_spec((4 * steps, rank, COL)),
        ],
        scratch_shapes=[pltpu.VMEM((rank, rows), f32)],
        compiler_params=params(),
        name="dlin",
        cost_estimate=work(4 * rows * model * model),
    )(*dqkv, norm, small, b, cosine, sine)


def input_grad_kernel(core_ref, dlin_ref, dsmall_ref, x_ref, g_ref, dmid_ref, *refs):
    w_refs = refs[:6]
    a_ref = refs[6]
    out_ref, acc_ref = refs[-2:]
    step = pl.program_id(0)
    core = core_ref[0]
    value = sum(
        nt(dlin_ref[which], both_halves(core, w_refs[2 * which], w_refs[2 * which + 1]))
        for which in range(3)
    )

    @pl.when(step == 0)
    def _():
        acc_ref[...] = value + tn(dsmall_ref[...], a_ref[...])

    @pl.when(step > 0)
    def _():
        acc_ref[...] += value

    @pl.when(step == pl.num_programs(0) - 1)
    def _():
        unit, scale = normalize(x_ref[...].astype(f32))
        out_ref[...] = (
            dmid_ref[...] + norm_back(unit, scale, acc_ref[...] * g_ref[...])
        ).astype(bf16)


def input_grad_call(at, given, dlin, dsmall, x, gain, dmid, core, halves, a):
    count, rows, model = x.shape
    given = [] if given is None else [given]
    rank = a.shape[0]
    steps = model // COL
    return pl.pallas_call(
        input_grad_kernel,
        out_shape=jax.ShapeDtypeStruct((count, rows, model), bf16),
        grid_spec=pltpu.PrefetchScalarGridSpec(
            num_scalar_prefetch=1,
            grid=(steps,),
            in_specs=[
                pl.BlockSpec((3, rows, COL), lambda j, core: (0, 0, j)),
                whole_spec((rank, rows)),
                pl.BlockSpec((None, rows, model), lambda j, core: (at, 0, 0)),
                whole_spec((1, model)),
                whole_spec((rows, model)),
            ]
            + half_specs(halves[0].shape, steps)
            + [whole_spec((rank, model))]
            + [pl.BlockSpec(memory_space=pl.ANY)] * len(given),
            out_specs=pl.BlockSpec((None, rows, model), lambda j, core: (at, 0, 0)),
            scratch_shapes=[pltpu.VMEM((rows, model), f32)],
        ),
        input_output_aliases={13: 0} if given else {},
        compiler_params=params(),
        name="input_grad",
        cost_estimate=work(8 * rows * model * model),
    )(core, dlin, dsmall, x, gain, dmid, *halves * 3, a, *given)


def mlp_kernel(
    x_ref, cot_ref, o_ref, g_ref, wo_ref, wu_ref, wv_ref, wt_ref,
    aout_ref, bout_ref, ain_ref, bu_ref, bv_ref, a2_ref, b2_ref, id_ref, *rest, width,
):
    mlp_body(
        x_ref, cot_ref, o_ref, g_ref, wo_ref, wu_ref, wv_ref, wt_ref,
        aout_ref, bout_ref, ain_ref, bu_ref, bv_ref, a2_ref, b2_ref, id_ref, *rest, width=width,
    )


def natural(ref):
    cores, groups, chips = ref.shape[:3]
    return jnp.concatenate(
        [ref[core, d, c] for d in range(groups) for c in range(chips) for core in range(cores)], 0
    )


def mlp_body(
    x_ref, cot_ref, o_ref, g_ref, wo_ref, wu_ref, wv_ref, wt_ref,
    aout_ref, bout_ref, ain_ref, bu_ref, bv_ref, a2_ref, b2_ref, id_ref,
    out_ref, dmid_ref, datt_ref, grad_ref,
    att_s, norm_s, unit_s, scale_s, acc_s, dnorm_s, small2_s, small3_s, small4_s, dsmall4_s, dsmall3_s,
    *, width,
):
    step = pl.program_id(0)
    pieces = o_ref.shape[0]
    model = x_ref.shape[1]
    per = model // COL
    first_block = grad_ref.shape[0] - BLOCK_PAD - 4 * per

    def put(which, value):
        for at in range(per):
            grad_ref[first_block + which * per + at] = value[:, at * COL : (at + 1) * COL]

    @pl.when(step == 0)
    def _():
        for at in range(first_block + 4 * per, grad_ref.shape[0]):
            grad_ref[at] = id_ref[...]
        for at in range(pieces):
            att_s[:, at * width : (at + 1) * width] = o_ref[at]
        att = att_s[...]
        small2 = nt(aout_ref[...], att).astype(bf16)
        small2_s[...] = small2
        middle = x_ref[...].astype(f32) + nn(att, natural(wo_ref)) + tn(small2, bout_ref[...])
        acc_s[...] = middle
        unit, scale = normalize(middle)
        unit_s[...] = unit
        scale_s[...] = jnp.broadcast_to(scale, scale_s.shape)
        norm = (unit * g_ref[...]).astype(bf16)
        norm_s[...] = norm
        small3_s[...] = nt(ain_ref[...], norm).astype(bf16)
        dsmall4_s[...] = nt(b2_ref[...], cot_ref[...]).astype(bf16)
        dnorm_s[...] = jnp.zeros(dnorm_s.shape, f32)
        small4_s[...] = jnp.zeros(small4_s.shape, f32)
        dsmall3_s[...] = jnp.zeros(dsmall3_s.shape, f32)

    norm = norm_s[...]
    small3 = small3_s[...]
    dsmall4 = dsmall4_s[...]
    wu, wv, wt = natural(wu_ref), natural(wv_ref), natural(wt_ref)
    u = nn(norm, wu) + tn(small3, bu_ref[...])
    v = nn(norm, wv) + tn(small3, bv_ref[...])
    dmixed = nn(cot_ref[...], wt) + tn(dsmall4, a2_ref[...])
    below = 0.5 * (1.0 + lax.erf(u * RSQRT2))
    gelu = u * below
    mixed = (gelu * v).astype(bf16)
    slope = below + u * (jnp.exp(-0.5 * u * u) * RSQRT2PI)
    du = (dmixed * v * slope).astype(bf16)
    dv = (dmixed * gelu).astype(bf16)
    acc_s[...] += nt(mixed, wt)
    dnorm_s[...] += nt(du, wu) + nt(dv, wv)
    small4_s[...] += nt(a2_ref[...], mixed)
    dsmall3_s[...] += nt(bu_ref[...], du) + nt(bv_ref[...], dv)
    steps = pl.num_programs(0)
    grad_ref[step] = nn(small3, du)
    grad_ref[steps + step] = nn(small3, dv)
    grad_ref[2 * steps + step] = nn(dsmall4, mixed)

    @pl.when(step == pl.num_programs(0) - 1)
    def _():
        small4 = small4_s[...].astype(bf16)
        dsmall3 = dsmall3_s[...].astype(bf16)
        out_ref[...] = (acc_s[...] + tn(small4, b2_ref[...])).astype(bf16)
        put(3, nn(small4, cot_ref[...]))
        dnorm = dnorm_s[...] + tn(dsmall3, ain_ref[...])
        put(2, nn(dsmall3, norm_s[...]))
        dmid = cot_ref[...].astype(f32) + norm_back(unit_s[...], scale_s[:, 0:1], dnorm * g_ref[...])
        dmid_ref[...] = dmid
        dlow = dmid.astype(bf16)
        dsmall2 = nt(bout_ref[...], dlow).astype(bf16)
        put(1, nn(small2_s[...], dlow))
        put(0, nn(dsmall2, att_s[...]))
        datt = (nt(dlow, natural(wo_ref)) + tn(dsmall2, aout_ref[...])).astype(bf16)
        for at in range(pieces):
            datt_ref[at] = datt[:, at * width : (at + 1) * width]


def mlp_call(
    which_seq, x, cot, o, gain, w_all, a_out, b_out, a_in, b_u, b_v, a_out2, b_out2, own_id
):
    seq_count, rows, model = x.shape
    pieces, _, width = o.shape
    rank = a_out.shape[0]
    hidden = b_u.shape[1]
    steps = hidden // COL
    blocks = 3 * steps + 4 * (model // COL) + BLOCK_PAD
    full = lambda shape: pl.BlockSpec(shape, lambda j: (0,) * len(shape), pipeline_mode=pl.Buffered(1))
    lead = w_all.shape[:-1]
    ff_spec = lambda which: pl.BlockSpec(
        lead + (COL,), lambda j: (0, 0, 0, 0, model // COL + which * steps + j)
    )
    one_seq = pl.BlockSpec((None, rows, model), lambda j: (which_seq, 0, 0))
    small_ff = pl.BlockSpec((rank, COL), lambda j: (0, j))
    small = full((rank, model))
    return pl.pallas_call(
        functools.partial(mlp_kernel, width=width),
        grid=(steps,),
        out_shape=(
            jax.ShapeDtypeStruct((rows, model), bf16),
            jax.ShapeDtypeStruct((rows, model), f32),
            jax.ShapeDtypeStruct((pieces, rows, width), bf16),
            jax.ShapeDtypeStruct((blocks, rank, COL), f32),
        ),
        in_specs=[
            one_seq,
            one_seq,
            full((pieces, rows, width)),
            full((1, model)),
            full(lead + (model,)),
            ff_spec(0),
            ff_spec(1),
            ff_spec(2),
            small,
            small,
            small,
            small_ff,
            small_ff,
            small_ff,
            small,
            full((rank, COL)),
        ],
        out_specs=[
            whole_spec((rows, model)),
            whole_spec((rows, model)),
            whole_spec((pieces, rows, width)),
            whole_spec((blocks, rank, COL)),
        ],
        scratch_shapes=[
            pltpu.VMEM((rows, model), bf16),
            pltpu.VMEM((rows, model), bf16),
            pltpu.VMEM((rows, model), f32),
            pltpu.VMEM((rows, 128), f32),
            pltpu.VMEM((rows, model), f32),
            pltpu.VMEM((rows, model), f32),
            pltpu.VMEM((rank, rows), bf16),
            pltpu.VMEM((rank, rows), bf16),
            pltpu.VMEM((rank, rows), f32),
            pltpu.VMEM((rank, rows), bf16),
            pltpu.VMEM((rank, rows), f32),
        ],
        compiler_params=params(),
        name="feed_forward",
        cost_estimate=work(26 * rows * model * hidden),
    )(
        x, cot, o, gain, w_all, w_all, w_all, w_all, a_out, b_out, a_in, b_u, b_v, a_out2, b_out2,
        own_id,
    )


def assemble_kernel(ids_ref, *refs, layout, arrays):
    which = pl.program_id(0)
    sources, outs, acc_ref = refs[:arrays], refs[arrays:-1], refs[-1]
    acc_ref[...] = jnp.zeros(acc_ref.shape, f32)
    count = sources[0].shape[0]
    for at, source in enumerate(sources):

        def add(index, carry):
            @pl.when(ids_ref[at * count + index] == which)
            def _():
                acc_ref[...] += source[index].astype(f32)

            return carry

        lax.fori_loop(0, count, add, 0)
    for out_ref, segments in zip(outs, layout):
        start = 0
        for first, blocks, size in segments:
            for block in range(blocks):
                wide = min(COL, size - block * COL)
                if wide > 0:
                    spot = start + block * COL
                    out_ref[:, spot : spot + wide] = acc_ref[first + block][:, :wide]
            start += size


def assemble_call(sources, ids, adapters, layout):
    _, blocks, rank, _ = sources[0].shape
    sizes = [sum(size for _, _, size in segments) for segments in layout]
    return pl.pallas_call(
        functools.partial(assemble_kernel, layout=layout, arrays=len(sources)),
        out_shape=[jax.ShapeDtypeStruct((adapters, rank, size), f32) for size in sizes],
        grid_spec=pltpu.PrefetchScalarGridSpec(
            num_scalar_prefetch=1,
            grid=(adapters,),
            in_specs=[whole_spec(source.shape) for source in sources],
            out_specs=[pl.BlockSpec((None, rank, size), lambda e, ids: (e, 0, 0)) for size in sizes],
            scratch_shapes=[pltpu.VMEM((blocks, rank, COL), f32)],
        ),
        compiler_params=params(),
        name="assemble",
        cost_estimate=work(4096 * adapters * rank * sum(sizes) // 256),
    )(ids, *sources)


def pad_columns(values, size):
    return jnp.pad(values, [(0, 0)] * (values.ndim - 1) + [(0, size - values.shape[-1])])


def local(
    tokens,
    segment_ids,
    positions,
    adapter_id,
    gain_attn,
    gain_mlp,
    w_qkv,
    w_out,
    w_in,
    w_out2,
    a_qkv,
    b_qkv,
    a_out,
    b_out,
    a_in,
    b_in,
    a_out2,
    b_out2,
    cotangent,
):
    seq_count, piece_len, model = tokens.shape
    pieces = lax.axis_size("seq")
    groups = HEADS // pieces
    width = groups * HD
    length = piece_len * pieces
    rank = a_qkv.shape[1]
    adapters = a_qkv.shape[0]
    hidden = w_out2.shape[0]
    padded = -(-hidden // COL) * COL
    tile = min(512, length)
    both = ("dp", "seq")

    dp = lax.axis_size("dp")
    before = [jnp.sum((segment_ids < d).astype(jnp.int32), axis=1) for d in range(1, DOCS)]
    swap = lambda value: lax.all_to_all(value, "seq", split_axis=0, concat_axis=0, tiled=True)
    facts = jnp.stack(before, 1)
    shard = jnp.concatenate(
        [
            w_out,
            pad_columns(w_in[:, :hidden], padded),
            pad_columns(w_in[:, hidden:], padded),
            pad_columns(w_out2.T, padded),
        ],
        1,
    )
    chips = pieces // 2
    same_core = [[2 * chip + core for chip in range(chips)] for core in range(2)]
    same_chip = [[2 * chip, 2 * chip + 1] for chip in range(chips)]
    half = HD // 2
    lane = jnp.arange(128, dtype=jnp.int32) % HD
    frequency = theta_base ** (-((lane % half).astype(f32) * 2.0) / HD)
    angles = positions.astype(f32)[..., None] * frequency
    cosine = jnp.cos(angles)
    sine = jnp.where(lane < half, -1.0, 1.0) * jnp.sin(angles)

    gain1 = gain_attn.reshape(1, model)
    gain2 = gain_mlp.reshape(1, model)
    pick = lambda table, s: lax.dynamic_index_in_dim(table, adapter_id[s], 0, keepdims=False)
    each = range(seq_count)

    aq = [pick(a_qkv, s) for s in each]
    bq = [pick(b_qkv, s).reshape(rank, 3, model).transpose(1, 0, 2) for s in each]
    norm, small = norm_call(tokens, gain1, jnp.stack(aq, 0))
    maps = []
    for s in each:
        b_in_s = pick(b_in, s)
        maps.append(
            (
                pick(a_out, s),
                pick(b_out, s),
                pick(a_in, s),
                pad_columns(b_in_s[:, :hidden], padded),
                pad_columns(b_in_s[:, hidden:], padded),
                pad_columns(pick(a_out2, s), padded),
                pick(b_out2, s),
                jnp.full((rank, COL), adapter_id[s].astype(f32)),
            )
        )
    same_pair = [(at, at ^ 1) for at in range(pieces)]
    core = (lax.axis_index("seq") % 2).astype(jnp.int32).reshape(1)
    qkv_column = lax.all_gather(w_qkv, "seq", axis=0, tiled=True, axis_index_groups=same_core)
    qkv_column, shard = lax.optimization_barrier((qkv_column, shard))
    qkv_own = lax.all_to_all(
        jnp.broadcast_to(qkv_column[None], (dp,) + qkv_column.shape),
        "dp",
        split_axis=0,
        concat_axis=0,
        tiled=True,
    ).reshape(dp, chips, -1, 3 * model)
    ready = (qkv_own, facts, norm, small, cosine, sine, bq, maps)
    qkv_own, facts, norm, small, cosine, sine, bq, maps = lax.optimization_barrier(ready)
    counts = jnp.sum(swap(jnp.broadcast_to(facts[None], (pieces,) + facts.shape)), 0)
    cuts = jnp.concatenate(
        [
            jnp.zeros((seq_count, 1), jnp.int32),
            counts,
            jnp.full((seq_count, 1), length, jnp.int32),
        ],
        1,
    )
    qkv_other = lax.ppermute(qkv_own, "seq", same_pair)
    halves = [qkv_own, qkv_other]
    column = lax.all_gather(shard, "seq", axis=0, tiled=True, axis_index_groups=same_core)

    def project_of(s, split):
        return qkv_project(
            s, split, norm, small, core, halves, bq[s], cosine, sine, pieces, width
        )

    packed = [project_of(0, (3,))]
    norm, packed[0], column, cuts = lax.optimization_barrier((norm, packed[0], column, cuts))
    own = lax.all_gather(column, "dp", axis=0, tiled=True)
    packed.append(project_of(1, (2, 1)))
    headed = [[swap(packed[0][0])]]
    packed[1], headed[0] = lax.optimization_barrier((packed[1], headed[0]))
    query_keys = swap(packed[1][0])
    attended = [attend(headed[0], cuts[0], tile)]
    own, attended[0], query_keys = lax.optimization_barrier((own, attended[0], query_keys))
    full_rest = lax.all_gather(own, "seq", axis=0, tiled=True, axis_index_groups=same_chip)
    full_rest = full_rest.reshape(2, dp, chips, -1, full_rest.shape[-1])
    query_keys, o_first = lax.optimization_barrier((query_keys, attended[0][0]))
    o_tokens = [swap(o_first)]
    values, o_tokens[0] = lax.optimization_barrier((packed[1][1], o_tokens[0]))
    values = swap(values)

    def feed_forward(s):
        return mlp_call(
            s, tokens, cotangent, o_tokens[s], gain2, full_rest, *maps[s]
        )

    middle = [feed_forward(0)]

    def scatter(grads):
        lead = grads.reshape(-1, COL)
        return lax.psum_scatter(lead, "seq", scatter_dimension=0, tiled=True).astype(bf16)

    first_sum = scatter(middle[0][3])
    values, query_keys, middle[0] = lax.optimization_barrier((values, query_keys, middle[0]))
    headed.append([query_keys, values])
    do_items = [swap(middle[0][2])]
    attended.append(attend(headed[1], cuts[1], tile))
    do_items[0], attended[1], first_sum = lax.optimization_barrier(
        (do_items[0], attended[1], first_sum)
    )

    def back(s, h):
        return attend_back(
            headed[s], attended[s][0], do_items[s], attended[s][1], cuts[s], tile, h
        )

    first_back = back(0, 0)
    o_tokens.append(swap(attended[1][0]))
    o_tokens[1], _ = lax.optimization_barrier((o_tokens[1], first_back))
    dqkv = [[swap(first_back)]]
    middle.append(feed_forward(1))
    second_sum = scatter(middle[1][3])
    dqkv[0][0], do_second = lax.optimization_barrier((dqkv[0][0], middle[1][2]))
    do_items.append(swap(do_second))
    do_items[0], _ = lax.optimization_barrier((do_items[0], middle[1][3]))
    ff = padded // COL
    per = model // COL
    mods = 3 * ff

    def dlin_of(s):
        return dlin_call(s, dqkv[s], norm, small, bq[s], cosine, sine)

    def input_grad_of(s, dlin, given):
        return input_grad_call(
            s, given, dlin[0], dlin[1], tokens, gain1, middle[s][1], core, halves, aq[s]
        )

    others = [back(0, h) for h in range(1, groups)]
    dqkv[0] += [swap(part) for part in others]
    do_items[1], second_sum, _ = lax.optimization_barrier((do_items[1], second_sum, others))
    sums = jnp.stack([first_sum, second_sum], 0)
    every = lax.all_gather(sums[None], both, axis=0, tiled=True)
    every = every.reshape((dp, pieces) + sums.shape)
    gathered = [every[:, :, s].reshape(dp, -1, rank, COL) for s in each]
    ids = [
        (part[:, -1, 0, 0].astype(f32) * (1.0 / pieces)).astype(jnp.int32) for part in gathered
    ]
    dqkv += [[swap(back(s, h)) for h in range(groups)] for s in each[1:]]
    dlins = [dlin_of(0)]
    input_grads = input_grad_of(0, dlins[0], None)
    early = assemble_call(
        gathered,
        jnp.concatenate(ids),
        adapters,
        [[(mods + which * per, per, model)] for which in range(3)]
        + [[(0, ff, hidden), (ff, ff, hidden)], [(2 * ff, ff, hidden)], [(mods + 3 * per, per, model)]],
    )
    dqkv[1], early, input_grads = lax.optimization_barrier((dqkv[1], early, input_grads))
    dlins += [dlin_of(s) for s in each[1:]]
    late_grads = jnp.stack([dlins[s][2] for s in each], 0)
    parts = swap(late_grads.astype(bf16).reshape(pieces, -1, COL))
    mine = jnp.sum(parts.astype(f32), 0).astype(bf16)
    copies = jnp.broadcast_to(mine[None], (dp * pieces,) + mine.shape)
    every = lax.all_to_all(copies, both, split_axis=0, concat_axis=0, tiled=True)
    for s in each[1:]:
        input_grads = input_grad_of(s, dlins[s], input_grads)
    late = assemble_call(
        [every.reshape((dp * seq_count,) + late_grads.shape[1:])],
        jnp.stack(ids, 1).reshape(-1),
        adapters,
        [[(0, per, model)], [(per, 3 * per, 3 * model)]],
    )
    layer_out = jnp.stack([middle[s][0] for s in each], 0)
    return (
        layer_out,
        input_grads,
        late[0],
        late[1],
        early[0],
        early[1],
        early[2],
        early[3],
        early[4],
        early[5],
    )


def solution(mesh):
    placed = (
        P("dp", "seq", None),
        P("dp", "seq"),
        P("dp", "seq"),
        P("dp"),
        P(),
        P(),
        P(("dp", "seq"), None),
        P(("dp", "seq"), None),
        P(("dp", "seq"), None),
        P(None, ("dp", "seq")),
        P(),
        P(),
        P(),
        P(),
        P(),
        P(),
        P(),
        P(),
        P("dp", "seq", None),
    )
    return jax.shard_map(
        local,
        mesh=mesh,
        in_specs=placed,
        out_specs=(
            P("dp", "seq", None),
            P("dp", "seq", None),
            P(),
            P(),
            P(),
            P(),
            P(),
            P(),
            P(),
            P(),
        ),
        check_vma=False,
    )
```

```python
import functools

import jax
import jax.numpy as jnp
from jax import lax
from jax.experimental import pallas as pl
from jax.experimental.pallas import tpu as pltpu
from jax.sharding import PartitionSpec as P

HEADS = 16
HD = 64
DOCS = 4
COL = 256
BLOCK_PAD = 7

eps_norm = 1e-05
theta_base = 160000.0
LOG2E = 1.4426950408889634
NEG = -1e30
RSQRT2 = 0.7071067811865476
RSQRT2PI = 0.3989422804014327
bf16 = jnp.bfloat16
f32 = jnp.float32


def nt(left, right):
    return lax.dot_general(left, right, (((1,), (1,)), ((), ())), preferred_element_type=f32)


def nn(left, right):
    return lax.dot_general(left, right, (((1,), (0,)), ((), ())), preferred_element_type=f32)


def tn(left, right):
    return lax.dot_general(left, right, (((0,), (0,)), ((), ())), preferred_element_type=f32)


def params():
    return pltpu.CompilerParams(dimension_semantics=("arbitrary",))


def work(amount):
    return pl.CostEstimate(flops=int(amount), transcendentals=0, bytes_accessed=0)


def whole_spec(shape):
    zeros = (0,) * len(shape)
    return pl.BlockSpec(shape, lambda *_: zeros)


def mask_heads(rows, heads, groups):
    if groups == 1:
        return rows
    lane = lax.broadcasted_iota(jnp.int32, rows.shape, 1)
    parts = [
        jnp.where((lane >= h * HD) & (lane < (h + 1) * HD), rows, jnp.zeros_like(rows))
        for h in heads
    ]
    return jnp.concatenate(parts, 0) if len(parts) > 1 else parts[0]


def inside(low, high, shape, axis):
    at = lax.broadcasted_iota(jnp.int32, shape, axis)
    return (at >= low) & (at < high)

def safe_keys(keys, low, high):
    pick = jnp.where(lax.broadcasted_iota(jnp.int32, (16, keys.shape[0]), 1) == low, 1.0, 0.0)
    row = nn(pick.astype(bf16), keys)[0:1, :].astype(bf16)
    return jnp.where(inside(low, high, keys.shape, 0), keys, jnp.broadcast_to(row, keys.shape))


def tile_range(cuts_ref, doc, index, tile, length):
    first = cuts_ref[doc]
    last = cuts_ref[doc + 1]
    nominal = (first // 16) * 16 + index * tile
    off = pl.multiple_of(jnp.minimum(nominal, length - tile), 16)
    low = jnp.maximum(nominal, first) - off
    high = jnp.minimum(nominal + tile, last) - off
    return off, low, high


def tile_count(cuts_ref, doc, tile):
    base = (cuts_ref[doc] // 16) * 16
    return lax.div(cuts_ref[doc + 1] - base + (tile - 1), tile)


def attend_kernel(
    cuts_ref, q_ref, k_ref, v_ref, o_ref, lse_ref, vt_ref, m_ref, acc_ref, *, tile, groups, length
):
    width = groups * HD
    qf = q_ref.reshape(length, width)
    kf = k_ref.reshape(length, width)
    vf = v_ref.reshape(length, width)
    of = o_ref.reshape(length, width)
    wide = groups * tile
    vt_ref[:, width:, :] = jnp.ones((vt_ref.shape[0], 16, tile), bf16)

    def doc_step(doc, first_tile):
        count = tile_count(cuts_ref, doc, tile)

        def prepare(j, carry):
            off, low, high = tile_range(cuts_ref, doc, j, tile, length)
            vt_ref[j, 0:width, :] = vf[pl.ds(off, tile), :].T
            return carry

        lax.fori_loop(0, count, prepare, 0)

        def q_tile(i, carry):
            off, low, high = tile_range(cuts_ref, doc, i, tile, length)
            qm = mask_heads(qf[pl.ds(off, tile), :] * bf16(0.125), range(groups), groups)
            m_ref[...] = jnp.full(m_ref.shape, NEG, f32)
            acc_ref[...] = jnp.zeros(acc_ref.shape, f32)

            def k_tile(j, inner):
                koff, klow, khigh = tile_range(cuts_ref, doc, j, tile, length)
                keep = inside(klow, khigh, (tile, wide), 0)
                s = jnp.where(keep, nt(kf[pl.ds(koff, tile), :], qm) * LOG2E, NEG)
                m_old = m_ref[0:1, :]
                m_new = jnp.maximum(m_old, jnp.max(s, axis=0, keepdims=True))
                p = jnp.exp2(s - m_new).astype(bf16)
                acc_ref[...] = acc_ref[...] * jnp.exp2(m_old - m_new) + nn(vt_ref[j], p)
                m_ref[0:1, :] = m_new
                return inner

            lax.fori_loop(0, count, k_tile, 0)
            total = acc_ref[width : width + 1, :]
            inverse = 1.0 / total
            lse_ref[first_tile + i, 0:1, :] = m_ref[0:1, :] + jnp.log2(total)
            parts = [
                acc_ref[h * HD : (h + 1) * HD, h * tile : (h + 1) * tile]
                * inverse[:, h * tile : (h + 1) * tile]
                for h in range(groups)
            ]
            out = (jnp.concatenate(parts, 0) if groups > 1 else parts[0]).T.astype(bf16)
            keep = inside(low, high, (tile, width), 0)
            of[pl.ds(off, tile), :] = jnp.where(keep, out, of[pl.ds(off, tile), :])
            return carry

        lax.fori_loop(0, count, q_tile, 0)
        return first_tile + count

    lax.fori_loop(0, DOCS, doc_step, 0)


def qkv_operands(headed):
    pieces, _, piece_len, width = headed[0].shape
    last = headed[-1].shape[1] - 1
    at = [(headed[0], 0), (headed[-1], last - 1), (headed[-1], last)]
    spec = lambda which: pl.BlockSpec(
        (pieces, None, piece_len, width), lambda i, cuts: (0, which, 0, 0)
    )
    return [array for array, _ in at], [spec(which) for _, which in at]


def attend(headed, cuts, tile):
    operands, specs = qkv_operands(headed)
    pieces, _, piece_len, width = headed[0].shape
    groups = width // HD
    length = pieces * piece_len
    tiles = length // tile + DOCS
    wide = groups * tile
    return pl.pallas_call(
        functools.partial(attend_kernel, tile=tile, groups=groups, length=length),
        out_shape=(
            jax.ShapeDtypeStruct((pieces, piece_len, width), bf16),
            jax.ShapeDtypeStruct((tiles, 8, wide), f32),
        ),
        grid_spec=pltpu.PrefetchScalarGridSpec(
            num_scalar_prefetch=1,
            grid=(1,),
            in_specs=specs,
            out_specs=[whole_spec((pieces, piece_len, width)), whole_spec((tiles, 8, wide))],
            scratch_shapes=[
                pltpu.VMEM((length // tile + 1, width + 16, tile), bf16),
                pltpu.VMEM((8, wide), f32),
                pltpu.VMEM((width + 16, wide), f32),
            ],
        ),
        compiler_params=params(),
        name="attend",
        cost_estimate=work(8192 * length * wide),
    )(cuts, *operands)


def attend_back_kernel(
    cuts_ref, q_ref, k_ref, v_ref, o_ref, do_ref, lse_ref, out_ref,
    qm_s, dom_s, lse_s, delta_s, dqt_s, ks_s, kt_s, p_s, ds_s, dk_s, dv_s, dqf, dkf, dvf,
    *, tile, groups, length, head,
):
    width = groups * HD
    own = slice(head * HD, (head + 1) * HD)
    qf = q_ref.reshape(length, width)
    kf = k_ref.reshape(length, width)
    vf = v_ref.reshape(length, width)
    of = o_ref.reshape(length, width)
    dof = do_ref.reshape(length, width)
    head_lane = lax.broadcasted_iota(jnp.int32, (16, width), 1)
    head_row = jnp.where(head_lane // HD == head, 1.0, 0.0).astype(bf16)

    def doc_step(doc, first_tile):
        count = tile_count(cuts_ref, doc, tile)

        def prepare(i, carry):
            off, low, high = tile_range(cuts_ref, doc, i, tile, length)
            spot = pl.ds(off, tile)
            qm_s[i] = mask_heads(qf[spot, :] * bf16(0.125), [head], groups)
            dom_s[i] = mask_heads(dof[spot, :], [head], groups)
            product = dof[spot, :].astype(f32) * of[spot, :].astype(f32)
            upper = product.astype(bf16)
            lower = (product - upper.astype(f32)).astype(bf16)
            delta_s[i, 0:1, :] = (nt(head_row, upper) + nt(head_row, lower))[0:1, :]
            lse = lse_ref[first_tile + i, 0:1, head * tile : (head + 1) * tile]
            lse_s[i, 0:1, :] = jnp.where(inside(low, high, (1, tile), 1), lse, -NEG)
            dqt_s[i] = jnp.zeros((HD, tile), f32)
            return carry

        lax.fori_loop(0, count, prepare, 0)

        def k_tile(j, carry):
            koff, klow, khigh = tile_range(cuts_ref, doc, j, tile, length)
            spot = pl.ds(koff, tile)
            keys = kf[spot, :]
            ks_s[...] = safe_keys(keys, klow, khigh)
            keys = jnp.where(inside(klow, khigh, keys.shape, 0), keys, jnp.zeros_like(keys))
            kt_s[...] = keys.T[own, :]
            dk_s[...] = jnp.zeros(dk_s.shape, f32)
            dv_s[...] = jnp.zeros(dv_s.shape, f32)

            def q_tile(i, inner):
                for c in range(0, tile, COL):
                    lanes = slice(c, c + COL)
                    qm = qm_s[i, lanes, :]
                    dom = dom_s[i, lanes, :]
                    for r in range(0, tile, COL):
                        rows = slice(r, r + COL)
                        s = nt(ks_s[rows, :], qm)
                        dp = nt(vf[pl.ds(pl.multiple_of(koff + r, 16), COL), :], dom)
                        p = jnp.exp2(s * LOG2E - lse_s[i, 0:1, lanes])
                        p_s[rows, lanes] = p.astype(bf16)
                        ds_s[rows, lanes] = (p * (dp - delta_s[i, 0:1, lanes])).astype(bf16)
                dv_s[...] += nn(p_s[...], dom_s[i])
                dk_s[...] += nn(ds_s[...], qm_s[i])
                dqt_s[i] += nn(kt_s[...], ds_s[...])
                return inner

            lax.fori_loop(0, count, q_tile, 0)
            keep = inside(klow, khigh, (tile, HD), 0)
            dkf[spot, :] = jnp.where(keep, dk_s[:, own].astype(bf16), dkf[spot, :])
            dvf[spot, :] = jnp.where(keep, dv_s[:, own].astype(bf16), dvf[spot, :])
            return carry

        lax.fori_loop(0, count, k_tile, 0)

        def finish(i, carry):
            off, low, high = tile_range(cuts_ref, doc, i, tile, length)
            out = (dqt_s[i] * 0.125).T.astype(bf16)
            spot = pl.ds(off, tile)
            dqf[spot, :] = jnp.where(inside(low, high, (tile, HD), 0), out, dqf[spot, :])
            return carry

        lax.fori_loop(0, count, finish, 0)
        return first_tile + count

    lax.fori_loop(0, DOCS, doc_step, 0)
    piece_len = q_ref.shape[1]
    fold = piece_len // groups
    for at in range(q_ref.shape[0]):
        for which, full in enumerate((dqf, dkf, dvf)):
            start = at * piece_len
            parts = [full[start + g * fold : start + (g + 1) * fold, :] for g in range(groups)]
            out_ref[at, which] = jnp.concatenate(parts, 1) if groups > 1 else parts[0]

def attend_back(headed, o, do, lse, cuts, tile, head):
    operands, specs = qkv_operands(headed)
    pieces, _, piece_len, width = headed[0].shape
    groups = width // HD
    length = pieces * piece_len
    tiles = length // tile + DOCS
    per_doc = length // tile + 1
    flat = whole_spec((pieces, piece_len, width))
    out = (pieces, 3, piece_len // groups, width)
    return pl.pallas_call(
        functools.partial(attend_back_kernel, tile=tile, groups=groups, length=length, head=head),
        out_shape=jax.ShapeDtypeStruct(out, bf16),
        grid_spec=pltpu.PrefetchScalarGridSpec(
            num_scalar_prefetch=1,
            grid=(1,),
            in_specs=specs
            + [flat, flat, whole_spec((tiles, 8, groups * tile))],
            out_specs=whole_spec(out),
            scratch_shapes=[
                pltpu.VMEM((per_doc, tile, width), bf16),
                pltpu.VMEM((per_doc, tile, width), bf16),
                pltpu.VMEM((per_doc, 8, tile), f32),
                pltpu.VMEM((per_doc, 8, tile), f32),
                pltpu.VMEM((per_doc, HD, tile), f32),
                pltpu.VMEM((tile, width), bf16),
                pltpu.VMEM((HD, tile), bf16),
                pltpu.VMEM((tile, tile), bf16),
                pltpu.VMEM((tile, tile), bf16),
                pltpu.VMEM((tile, width), f32),
                pltpu.VMEM((tile, width), f32),
            ]
            + [pltpu.VMEM((length, HD), bf16)] * 3,
        ),
        compiler_params=params(),
        name="attend_back",
        cost_estimate=work(16384 * length * tile),
    )(cuts, *operands, o, do, lse)


def normalize(values):
    center = values - jnp.mean(values, axis=-1, keepdims=True)
    spread = jnp.mean(center * center, axis=-1, keepdims=True)
    scale = lax.rsqrt(spread + eps_norm)
    return center * scale, scale


def norm_back(unit, scale, scaled_grad):
    return scale * (
        scaled_grad
        - jnp.mean(scaled_grad, axis=-1, keepdims=True)
        - unit * jnp.mean(scaled_grad * unit, axis=-1, keepdims=True)
    )


def lane_swap(values):
    lane = lax.broadcasted_iota(jnp.int32, values.shape, 1)
    size = values.shape[1]
    half = HD // 2
    return jnp.where(
        lane % HD < half, pltpu.roll(values, size - half, 1), pltpu.roll(values, half, 1)
    )


def norm_kernel(x_ref, g_ref, a_ref, norm_ref, small_ref):
    unit, _ = normalize(x_ref[...].astype(f32))
    norm = (unit * g_ref[...]).astype(bf16)
    norm_ref[...] = norm
    small_ref[...] = nt(a_ref[...], norm).astype(bf16)


def norm_call(x, gain, a):
    count, rows, model = x.shape
    rank = a.shape[1]
    return pl.pallas_call(
        norm_kernel,
        grid=(count,),
        out_shape=(
            jax.ShapeDtypeStruct((count, rows, model), bf16),
            jax.ShapeDtypeStruct((count, rank, rows), bf16),
        ),
        in_specs=[
            pl.BlockSpec((None, rows, model), lambda s: (s, 0, 0)),
            whole_spec((1, model)),
            pl.BlockSpec((None, rank, model), lambda s: (s, 0, 0)),
        ],
        out_specs=[
            pl.BlockSpec((None, rows, model), lambda s: (s, 0, 0)),
            pl.BlockSpec((None, rank, rows), lambda s: (s, 0, 0)),
        ],
        compiler_params=params(),
        name="norm",
        cost_estimate=work(4096 * count * rows * model),
    )(x, gain, a)


def both_halves(core, own_ref, other_ref):
    groups, chips = own_ref.shape[:2]
    slabs = []
    for d in range(groups):
        for c in range(chips):
            own, other = own_ref[d, c], other_ref[d, c]
            slabs += [jnp.where(core == 0, own, other), jnp.where(core == 0, other, own)]
    return jnp.concatenate(slabs, 0)


def qkv_kernel(core_ref, norm_ref, small_ref, *refs, width, kinds):
    count = len(kinds)
    w_refs, b_refs = refs[: 2 * count], refs[2 * count : 3 * count]
    cos_ref, sin_ref, out_ref = refs[3 * count :]
    core = core_ref[0]
    norm = norm_ref[...]
    small = small_ref[...]
    for at, kind in enumerate(kinds):
        w = both_halves(core, w_refs[2 * at], w_refs[2 * at + 1])
        lin = nn(norm, w) + tn(small, b_refs[at][...])
        for part in range(COL // 128):
            u = lin[:, part * 128 : (part + 1) * 128]
            if kind < 2:
                u = u * cos_ref[...] + lane_swap(u) * sin_ref[...]
            u = u.astype(bf16)
            for sub in range(128 // width):
                dest = part * (128 // width) + sub
                out_ref[dest, at] = u[:, sub * width : (sub + 1) * width]


def half_specs(shape, steps, kinds):
    block = shape[:-1] + (COL,)
    spec = lambda kind: pl.BlockSpec(block, lambda j, core: (0, 0, 0, kind * steps + j))
    return [spec(kind) for kind in kinds for _ in range(2)]


def qkv_project(at, kinds, norm, small, core, halves, b, cosine, sine, pieces, width):
    _, rows, model = norm.shape
    dests = COL // width
    steps = model // COL
    rank = small.shape[1]
    count = len(kinds)
    row_spec = lambda shape: pl.BlockSpec((None,) + shape, lambda j, core: (at, 0, 0))
    b_spec = lambda kind: pl.BlockSpec((rank, COL), lambda j, core: (0, kind * steps + j))
    return pl.pallas_call(
        functools.partial(qkv_kernel, width=width, kinds=kinds),
        out_shape=jax.ShapeDtypeStruct((pieces, count, rows, width), bf16),
        grid_spec=pltpu.PrefetchScalarGridSpec(
            num_scalar_prefetch=1,
            grid=(steps,),
            in_specs=[row_spec((rows, model)), row_spec((rank, rows))]
            + half_specs(halves[0].shape, steps, kinds)
            + [b_spec(kind) for kind in kinds]
            + [row_spec((rows, 128)), row_spec((rows, 128))],
            out_specs=pl.BlockSpec((dests, count, rows, width), lambda j, core: (j, 0, 0, 0)),
        ),
        compiler_params=params(),
        name="qkv_project",
        cost_estimate=work(2 * count * rows * model * model),
    )(core, norm, small, *halves * count, *[b] * count, cosine, sine)


def join_heads(refs, dest, which):
    if len(refs) == 1:
        return refs[0][dest, which]
    blocks = [ref[dest, which] for ref in refs]
    folds = [
        jnp.concatenate([block[:, g * HD : (g + 1) * HD] for block in blocks], 1)
        for g in range(len(refs))
    ]
    return jnp.concatenate(folds, 0)


def dlin_kernel(*args, width, heads):
    dqkv_refs = args[:heads]
    norm_ref, small_ref = args[heads : heads + 2]
    b_refs = args[heads + 2 : heads + 5]
    cos_ref, sin_ref, dlin_ref, dsmall_ref, grad_ref, acc_ref = args[heads + 5 :]
    step = pl.program_id(0)

    @pl.when(step == 0)
    def _():
        acc_ref[...] = jnp.zeros(acc_ref.shape, f32)

    small = small_ref[...]
    per = 128 // width
    for which in range(3):
        pieces = []
        for part in range(COL // 128):
            subs = [join_heads(dqkv_refs, part * per + sub, which) for sub in range(per)]
            u = jnp.concatenate(subs, 1) if per > 1 else subs[0]
            if which < 2:
                u = u.astype(f32)
                u = (u * cos_ref[...] - lane_swap(u) * sin_ref[...]).astype(bf16)
            pieces.append(u)
        dlin = jnp.concatenate(pieces, 1)
        dlin_ref[which] = dlin
        acc_ref[...] += nt(b_refs[which][...], dlin)
        grad_ref[(which + 1) * pl.num_programs(0) + step] = nn(small, dlin)

    @pl.when(step == pl.num_programs(0) - 1)
    def _():
        dsmall = acc_ref[...].astype(bf16)
        dsmall_ref[...] = dsmall
        grad_a = nn(dsmall, norm_ref[...])
        for at in range(grad_a.shape[1] // COL):
            grad_ref[at] = grad_a[:, at * COL : (at + 1) * COL]


def dlin_call(at, dqkv, norm, small, b, cosine, sine):
    _, _, fold, width = dqkv[0].shape
    _, rows, model = norm.shape
    rank = small.shape[1]
    dests = COL // width
    steps = model // COL
    b_spec = lambda kind: pl.BlockSpec((rank, COL), lambda j: (0, kind * steps + j))
    row_spec = lambda shape: pl.BlockSpec((None,) + shape, lambda j: (at, 0, 0))
    return pl.pallas_call(
        functools.partial(dlin_kernel, width=width, heads=len(dqkv)),
        grid=(steps,),
        out_shape=(
            jax.ShapeDtypeStruct((3, rows, model), bf16),
            jax.ShapeDtypeStruct((rank, rows), bf16),
            jax.ShapeDtypeStruct((4 * steps, rank, COL), f32),
        ),
        in_specs=[pl.BlockSpec((dests, 3, fold, width), lambda j: (j, 0, 0, 0))] * len(dqkv)
        + [
            row_spec((rows, model)),
            row_spec((rank, rows)),
            *[b_spec(kind) for kind in range(3)],
            row_spec((rows, 128)),
            row_spec((rows, 128)),
        ],
        out_specs=[
            pl.BlockSpec((3, rows, COL), lambda j: (0, 0, j)),
            whole_spec((rank, rows)),
            whole_spec((4 * steps, rank, COL)),
        ],
        scratch_shapes=[pltpu.VMEM((rank, rows), f32)],
        compiler_params=params(),
        name="dlin",
        cost_estimate=work(4 * rows * model * model),
    )(*dqkv, norm, small, b, b, b, cosine, sine)


def input_grad_kernel(core_ref, dlin_ref, dsmall_ref, x_ref, g_ref, dmid_ref, *refs):
    w_refs = refs[:6]
    a_ref = refs[6]
    out_ref, acc_ref = refs[-2:]
    step = pl.program_id(0)
    core = core_ref[0]
    value = sum(
        nt(dlin_ref[which], both_halves(core, w_refs[2 * which], w_refs[2 * which + 1]))
        for which in range(3)
    )

    @pl.when(step == 0)
    def _():
        acc_ref[...] = value + tn(dsmall_ref[...], a_ref[...])

    @pl.when(step > 0)
    def _():
        acc_ref[...] += value

    @pl.when(step == pl.num_programs(0) - 1)
    def _():
        unit, scale = normalize(x_ref[...].astype(f32))
        out_ref[...] = (
            dmid_ref[...] + norm_back(unit, scale, acc_ref[...] * g_ref[...])
        ).astype(bf16)


def input_grad_call(at, given, dlin, dsmall, x, gain, dmid, core, halves, a):
    count, rows, model = x.shape
    given = [] if given is None else [given]
    rank = a.shape[0]
    steps = model // COL
    return pl.pallas_call(
        input_grad_kernel,
        out_shape=jax.ShapeDtypeStruct((count, rows, model), bf16),
        grid_spec=pltpu.PrefetchScalarGridSpec(
            num_scalar_prefetch=1,
            grid=(steps,),
            in_specs=[
                pl.BlockSpec((3, rows, COL), lambda j, core: (0, 0, j)),
                whole_spec((rank, rows)),
                pl.BlockSpec((None, rows, model), lambda j, core: (at, 0, 0)),
                whole_spec((1, model)),
                whole_spec((rows, model)),
            ]
            + half_specs(halves[0].shape, steps, range(3))
            + [whole_spec((rank, model))]
            + [pl.BlockSpec(memory_space=pl.ANY)] * len(given),
            out_specs=pl.BlockSpec((None, rows, model), lambda j, core: (at, 0, 0)),
            scratch_shapes=[pltpu.VMEM((rows, model), f32)],
        ),
        input_output_aliases={13: 0} if given else {},
        compiler_params=params(),
        name="input_grad",
        cost_estimate=work(8 * rows * model * model),
    )(core, dlin, dsmall, x, gain, dmid, *halves * 3, a, *given)


def mlp_kernel(
    x_ref, cot_ref, o_ref, g_ref, wo_ref, wu_ref, wv_ref, wt_ref,
    aout_ref, bout_ref, ain_ref, bu_ref, bv_ref, a2_ref, b2_ref, id_ref, *rest, width,
):
    mlp_body(
        x_ref, cot_ref, o_ref, g_ref, wo_ref, wu_ref, wv_ref, wt_ref,
        aout_ref, bout_ref, ain_ref, bu_ref, bv_ref, a2_ref, b2_ref, id_ref, *rest, width=width,
    )


def natural(ref):
    cores, groups, chips = ref.shape[:3]
    return jnp.concatenate(
        [ref[core, d, c] for d in range(groups) for c in range(chips) for core in range(cores)], 0
    )


def mlp_body(
    x_ref, cot_ref, o_ref, g_ref, wo_ref, wu_ref, wv_ref, wt_ref,
    aout_ref, bout_ref, ain_ref, bu_ref, bv_ref, a2_ref, b2_ref, id_ref,
    out_ref, dmid_ref, datt_ref, grad_ref,
    att_s, norm_s, unit_s, scale_s, acc_s, dnorm_s, small2_s, small3_s, small4_s, dsmall4_s, dsmall3_s,
    *, width,
):
    step = pl.program_id(0)
    pieces = o_ref.shape[0]
    model = x_ref.shape[1]
    per = model // COL
    first_block = grad_ref.shape[0] - BLOCK_PAD - 4 * per

    def put(which, value):
        for at in range(per):
            grad_ref[first_block + which * per + at] = value[:, at * COL : (at + 1) * COL]

    @pl.when(step == 0)
    def _():
        for at in range(first_block + 4 * per, grad_ref.shape[0]):
            grad_ref[at] = id_ref[...]
        for at in range(pieces):
            att_s[:, at * width : (at + 1) * width] = o_ref[at]
        att = att_s[...]
        small2 = nt(aout_ref[...], att).astype(bf16)
        small2_s[...] = small2
        middle = x_ref[...].astype(f32) + nn(att, natural(wo_ref)) + tn(small2, bout_ref[...])
        acc_s[...] = middle
        unit, scale = normalize(middle)
        unit_s[...] = unit
        scale_s[...] = jnp.broadcast_to(scale, scale_s.shape)
        norm = (unit * g_ref[...]).astype(bf16)
        norm_s[...] = norm
        small3_s[...] = nt(ain_ref[...], norm).astype(bf16)
        dsmall4_s[...] = nt(b2_ref[...], cot_ref[...]).astype(bf16)
        dnorm_s[...] = jnp.zeros(dnorm_s.shape, f32)
        small4_s[...] = jnp.zeros(small4_s.shape, f32)
        dsmall3_s[...] = jnp.zeros(dsmall3_s.shape, f32)

    norm = norm_s[...]
    small3 = small3_s[...]
    dsmall4 = dsmall4_s[...]
    wu, wv, wt = natural(wu_ref), natural(wv_ref), natural(wt_ref)
    u = nn(norm, wu) + tn(small3, bu_ref[...])
    v = nn(norm, wv) + tn(small3, bv_ref[...])
    dmixed = nn(cot_ref[...], wt) + tn(dsmall4, a2_ref[...])
    below = 0.5 * (1.0 + lax.erf(u * RSQRT2))
    gelu = u * below
    mixed = (gelu * v).astype(bf16)
    slope = below + u * (jnp.exp(-0.5 * u * u) * RSQRT2PI)
    du = (dmixed * v * slope).astype(bf16)
    dv = (dmixed * gelu).astype(bf16)
    acc_s[...] += nt(mixed, wt)
    dnorm_s[...] += nt(du, wu) + nt(dv, wv)
    small4_s[...] += nt(a2_ref[...], mixed)
    dsmall3_s[...] += nt(bu_ref[...], du) + nt(bv_ref[...], dv)
    steps = pl.num_programs(0)
    grad_ref[step] = nn(small3, du)
    grad_ref[steps + step] = nn(small3, dv)
    grad_ref[2 * steps + step] = nn(dsmall4, mixed)

    @pl.when(step == pl.num_programs(0) - 1)
    def _():
        small4 = small4_s[...].astype(bf16)
        dsmall3 = dsmall3_s[...].astype(bf16)
        out_ref[...] = (acc_s[...] + tn(small4, b2_ref[...])).astype(bf16)
        put(3, nn(small4, cot_ref[...]))
        dnorm = dnorm_s[...] + tn(dsmall3, ain_ref[...])
        put(2, nn(dsmall3, norm_s[...]))
        dmid = cot_ref[...].astype(f32) + norm_back(unit_s[...], scale_s[:, 0:1], dnorm * g_ref[...])
        dmid_ref[...] = dmid
        dlow = dmid.astype(bf16)
        dsmall2 = nt(bout_ref[...], dlow).astype(bf16)
        put(1, nn(small2_s[...], dlow))
        put(0, nn(dsmall2, att_s[...]))
        datt = (nt(dlow, natural(wo_ref)) + tn(dsmall2, aout_ref[...])).astype(bf16)
        for at in range(pieces):
            datt_ref[at] = datt[:, at * width : (at + 1) * width]


def mlp_call(
    which_seq, x, cot, o, gain, w_all, a_out, b_out, a_in, b_u, b_v, a_out2, b_out2, own_id
):
    seq_count, rows, model = x.shape
    pieces, _, width = o.shape
    rank = a_out.shape[0]
    hidden = b_u.shape[1]
    steps = hidden // COL
    blocks = 3 * steps + 4 * (model // COL) + BLOCK_PAD
    full = lambda shape: pl.BlockSpec(shape, lambda j: (0,) * len(shape), pipeline_mode=pl.Buffered(1))
    lead = w_all.shape[:-1]
    ff_spec = lambda which: pl.BlockSpec(
        lead + (COL,), lambda j: (0, 0, 0, 0, model // COL + which * steps + j)
    )
    one_seq = pl.BlockSpec((None, rows, model), lambda j: (which_seq, 0, 0))
    small_ff = pl.BlockSpec((rank, COL), lambda j: (0, j))
    small = full((rank, model))
    return pl.pallas_call(
        functools.partial(mlp_kernel, width=width),
        grid=(steps,),
        out_shape=(
            jax.ShapeDtypeStruct((rows, model), bf16),
            jax.ShapeDtypeStruct((rows, model), f32),
            jax.ShapeDtypeStruct((pieces, rows, width), bf16),
            jax.ShapeDtypeStruct((blocks, rank, COL), f32),
        ),
        in_specs=[
            one_seq,
            one_seq,
            full((pieces, rows, width)),
            full((1, model)),
            full(lead + (model,)),
            ff_spec(0),
            ff_spec(1),
            ff_spec(2),
            small,
            small,
            small,
            small_ff,
            small_ff,
            small_ff,
            small,
            full((rank, COL)),
        ],
        out_specs=[
            whole_spec((rows, model)),
            whole_spec((rows, model)),
            whole_spec((pieces, rows, width)),
            whole_spec((blocks, rank, COL)),
        ],
        scratch_shapes=[
            pltpu.VMEM((rows, model), bf16),
            pltpu.VMEM((rows, model), bf16),
            pltpu.VMEM((rows, model), f32),
            pltpu.VMEM((rows, 128), f32),
            pltpu.VMEM((rows, model), f32),
            pltpu.VMEM((rows, model), f32),
            pltpu.VMEM((rank, rows), bf16),
            pltpu.VMEM((rank, rows), bf16),
            pltpu.VMEM((rank, rows), f32),
            pltpu.VMEM((rank, rows), bf16),
            pltpu.VMEM((rank, rows), f32),
        ],
        compiler_params=params(),
        name="feed_forward",
        cost_estimate=work(26 * rows * model * hidden),
    )(
        x, cot, o, gain, w_all, w_all, w_all, w_all, a_out, b_out, a_in, b_u, b_v, a_out2, b_out2,
        own_id,
    )


def assemble_kernel(ids_ref, *refs, layout, arrays):
    which = pl.program_id(0)
    sources, outs, acc_ref = refs[:arrays], refs[arrays:-1], refs[-1]
    acc_ref[...] = jnp.zeros(acc_ref.shape, f32)
    count = sources[0].shape[0]
    for at, source in enumerate(sources):

        def add(index, carry):
            @pl.when(ids_ref[at * count + index] == which)
            def _():
                acc_ref[...] += source[index].astype(f32)

            return carry

        lax.fori_loop(0, count, add, 0)
    for out_ref, segments in zip(outs, layout):
        start = 0
        for first, blocks, size in segments:
            for block in range(blocks):
                wide = min(COL, size - block * COL)
                if wide > 0:
                    spot = start + block * COL
                    out_ref[:, spot : spot + wide] = acc_ref[first + block][:, :wide]
            start += size


def assemble_call(sources, ids, adapters, layout):
    _, blocks, rank, _ = sources[0].shape
    sizes = [sum(size for _, _, size in segments) for segments in layout]
    return pl.pallas_call(
        functools.partial(assemble_kernel, layout=layout, arrays=len(sources)),
        out_shape=[jax.ShapeDtypeStruct((adapters, rank, size), f32) for size in sizes],
        grid_spec=pltpu.PrefetchScalarGridSpec(
            num_scalar_prefetch=1,
            grid=(adapters,),
            in_specs=[whole_spec(source.shape) for source in sources],
            out_specs=[pl.BlockSpec((None, rank, size), lambda e, ids: (e, 0, 0)) for size in sizes],
            scratch_shapes=[pltpu.VMEM((blocks, rank, COL), f32)],
        ),
        compiler_params=params(),
        name="assemble",
        cost_estimate=work(4096 * adapters * rank * sum(sizes) // 256),
    )(ids, *sources)


def pad_columns(values, size):
    return jnp.pad(values, [(0, 0)] * (values.ndim - 1) + [(0, size - values.shape[-1])])


def local(
    tokens,
    segment_ids,
    positions,
    adapter_id,
    gain_attn,
    gain_mlp,
    w_qkv,
    w_out,
    w_in,
    w_out2,
    a_qkv,
    b_qkv,
    a_out,
    b_out,
    a_in,
    b_in,
    a_out2,
    b_out2,
    cotangent,
):
    seq_count, piece_len, model = tokens.shape
    pieces = lax.axis_size("seq")
    groups = HEADS // pieces
    width = groups * HD
    length = piece_len * pieces
    rank = a_qkv.shape[1]
    adapters = a_qkv.shape[0]
    hidden = w_out2.shape[0]
    padded = -(-hidden // COL) * COL
    tile = min(512, length)
    both = ("dp", "seq")

    dp = lax.axis_size("dp")
    before = [jnp.sum((segment_ids < d).astype(jnp.int32), axis=1) for d in range(1, DOCS)]
    swap = lambda value: lax.all_to_all(value, "seq", split_axis=0, concat_axis=0, tiled=True)
    facts = jnp.stack(before, 1)
    shard = jnp.concatenate(
        [
            w_out,
            pad_columns(w_in[:, :hidden], padded),
            pad_columns(w_in[:, hidden:], padded),
            pad_columns(w_out2.T, padded),
        ],
        1,
    )
    chips = pieces // 2
    same_core = [[2 * chip + core for chip in range(chips)] for core in range(2)]
    same_chip = [[2 * chip, 2 * chip + 1] for chip in range(chips)]
    half = HD // 2
    lane = jnp.arange(128, dtype=jnp.int32) % HD
    frequency = theta_base ** (-((lane % half).astype(f32) * 2.0) / HD)
    angles = positions.astype(f32)[..., None] * frequency
    cosine = jnp.cos(angles)
    sine = jnp.where(lane < half, -1.0, 1.0) * jnp.sin(angles)

    gain1 = gain_attn.reshape(1, model)
    gain2 = gain_mlp.reshape(1, model)
    pick = lambda table, s: lax.dynamic_index_in_dim(table, adapter_id[s], 0, keepdims=False)
    each = range(seq_count)

    aq = [pick(a_qkv, s) for s in each]
    bq = [pick(b_qkv, s) for s in each]
    norm, small = norm_call(tokens, gain1, jnp.stack(aq, 0))
    maps = []
    for s in each:
        b_in_s = pick(b_in, s)
        maps.append(
            (
                pick(a_out, s),
                pick(b_out, s),
                pick(a_in, s),
                pad_columns(b_in_s[:, :hidden], padded),
                pad_columns(b_in_s[:, hidden:], padded),
                pad_columns(pick(a_out2, s), padded),
                pick(b_out2, s),
                jnp.full((rank, COL), adapter_id[s].astype(f32)),
            )
        )
    same_pair = [(at, at ^ 1) for at in range(pieces)]
    core = (lax.axis_index("seq") % 2).astype(jnp.int32).reshape(1)
    qkv_column = lax.all_gather(w_qkv, "seq", axis=0, tiled=True, axis_index_groups=same_core)
    qkv_column, shard = lax.optimization_barrier((qkv_column, shard))
    qkv_own = lax.all_to_all(
        jnp.broadcast_to(qkv_column[None], (dp,) + qkv_column.shape),
        "dp",
        split_axis=0,
        concat_axis=0,
        tiled=True,
    ).reshape(dp, chips, -1, 3 * model)
    ready = (qkv_own, facts, norm, small, cosine, sine, bq)
    qkv_own, facts, norm, small, cosine, sine, bq = lax.optimization_barrier(ready)
    counts = jnp.sum(swap(jnp.broadcast_to(facts[None], (pieces,) + facts.shape)), 0)
    cuts = jnp.concatenate(
        [
            jnp.zeros((seq_count, 1), jnp.int32),
            counts,
            jnp.full((seq_count, 1), length, jnp.int32),
        ],
        1,
    )
    halves = [qkv_own, lax.ppermute(qkv_own, "seq", same_pair)]
    column = lax.all_gather(shard, "seq", axis=0, tiled=True, axis_index_groups=same_core)

    def project_of(s, kinds):
        return qkv_project(
            s, kinds, norm, small, core, halves, bq[s], cosine, sine, pieces, width
        )

    packed = [[project_of(0, (0, 1, 2))]]
    norm, packed[0], column, cuts = lax.optimization_barrier((norm, packed[0], column, cuts))
    own = lax.all_gather(column, "dp", axis=0, tiled=True)
    packed.append([project_of(1, (0,)), project_of(1, (1, 2))])
    maps, packed[1] = lax.optimization_barrier((maps, packed[1]))
    headed = [[swap(packed[0][0])]]
    packed[1], headed[0] = lax.optimization_barrier((packed[1], headed[0]))
    query_keys = swap(packed[1][0])
    attended = [attend(headed[0], cuts[0], tile)]
    own, attended[0], query_keys = lax.optimization_barrier((own, attended[0], query_keys))
    full_rest = lax.all_gather(own, "seq", axis=0, tiled=True, axis_index_groups=same_chip)
    full_rest = full_rest.reshape(2, dp, chips, -1, full_rest.shape[-1])
    query_keys, o_first = lax.optimization_barrier((query_keys, attended[0][0]))
    o_tokens = [swap(o_first)]
    values, o_tokens[0] = lax.optimization_barrier((packed[1][1], o_tokens[0]))
    values = swap(values)

    def feed_forward(s):
        return mlp_call(
            s, tokens, cotangent, o_tokens[s], gain2, full_rest, *maps[s]
        )

    middle = [feed_forward(0)]

    def scatter(grads):
        lead = grads.reshape(-1, COL)
        return lax.psum_scatter(lead, "seq", scatter_dimension=0, tiled=True).astype(bf16)

    first_sum = scatter(middle[0][3])
    values, query_keys, middle[0] = lax.optimization_barrier((values, query_keys, middle[0]))
    headed.append([query_keys, values])
    do_items = [swap(middle[0][2])]
    attended.append(attend(headed[1], cuts[1], tile))
    do_items[0], attended[1], first_sum = lax.optimization_barrier(
        (do_items[0], attended[1], first_sum)
    )

    def back(s, h):
        return attend_back(
            headed[s], attended[s][0], do_items[s], attended[s][1], cuts[s], tile, h
        )

    first_back = back(0, 0)
    o_tokens.append(swap(attended[1][0]))
    o_tokens[1], _ = lax.optimization_barrier((o_tokens[1], first_back))
    dqkv = [[swap(first_back)]]
    middle.append(feed_forward(1))
    second_sum = scatter(middle[1][3])
    dqkv[0][0], do_second = lax.optimization_barrier((dqkv[0][0], middle[1][2]))
    do_items.append(swap(do_second))
    do_items[0], _ = lax.optimization_barrier((do_items[0], middle[1][3]))
    ff = padded // COL
    per = model // COL
    mods = 3 * ff

    def dlin_of(s):
        return dlin_call(s, dqkv[s], norm, small, bq[s], cosine, sine)

    def input_grad_of(s, dlin, given):
        return input_grad_call(
            s, given, dlin[0], dlin[1], tokens, gain1, middle[s][1], core, halves, aq[s]
        )

    others = [back(0, h) for h in range(1, groups)]
    dqkv[0] += [swap(part) for part in others]
    do_items[1], second_sum, _ = lax.optimization_barrier((do_items[1], second_sum, others))
    parts = [back(1, h) for h in range(groups)]
    parts[0], dqkv[0] = lax.optimization_barrier((parts[0], dqkv[0]))
    dqkv.append([swap(part) for part in parts])
    sums = jnp.stack([first_sum, second_sum], 0)
    sums, dqkv[1][0], _ = lax.optimization_barrier((sums, dqkv[1][0], parts[-1]))
    every = lax.all_gather(sums[None], both, axis=0, tiled=True)
    every = every.reshape((dp, pieces) + sums.shape)
    gathered = [every[:, :, s].reshape(dp, -1, rank, COL) for s in each]
    ids = [
        (part[:, -1, 0, 0].astype(f32) * (1.0 / pieces)).astype(jnp.int32) for part in gathered
    ]
    dlins = [dlin_of(0)]
    input_grads = input_grad_of(0, dlins[0], None)
    dqkv[1], input_grads = lax.optimization_barrier((dqkv[1], input_grads))
    dlins += [dlin_of(s) for s in each[1:]]
    late_grads = jnp.stack([dlins[s][2] for s in each], 0)
    parts = swap(late_grads.astype(bf16).reshape(pieces, -1, COL))
    mine = jnp.sum(parts.astype(f32), 0).astype(bf16)
    copies = jnp.broadcast_to(mine[None], (dp * pieces,) + mine.shape)
    every = lax.all_to_all(copies, both, split_axis=0, concat_axis=0, tiled=True)
    for s in each[1:]:
        input_grads = input_grad_of(s, dlins[s], input_grads)
    early = assemble_call(
        gathered,
        jnp.concatenate(ids),
        adapters,
        [[(mods + which * per, per, model)] for which in range(3)]
        + [[(0, ff, hidden), (ff, ff, hidden)], [(2 * ff, ff, hidden)], [(mods + 3 * per, per, model)]],
    )
    late = assemble_call(
        [every.reshape((dp * seq_count,) + late_grads.shape[1:])],
        jnp.stack(ids, 1).reshape(-1),
        adapters,
        [[(0, per, model)], [(per, 3 * per, 3 * model)]],
    )
    layer_out = jnp.stack([middle[s][0] for s in each], 0)
    return (
        layer_out,
        input_grads,
        late[0],
        late[1],
        early[0],
        early[1],
        early[2],
        early[3],
        early[4],
        early[5],
    )


def solution(mesh):
    placed = (
        P("dp", "seq", None),
        P("dp", "seq"),
        P("dp", "seq"),
        P("dp"),
        P(),
        P(),
        P(("dp", "seq"), None),
        P(("dp", "seq"), None),
        P(("dp", "seq"), None),
        P(None, ("dp", "seq")),
        P(),
        P(),
        P(),
        P(),
        P(),
        P(),
        P(),
        P(),
        P("dp", "seq", None),
    )
    return jax.shard_map(
        local,
        mesh=mesh,
        in_specs=placed,
        out_specs=(
            P("dp", "seq", None),
            P("dp", "seq", None),
            P(),
            P(),
            P(),
            P(),
            P(),
            P(),
            P(),
            P(),
        ),
        check_vma=False,
    )
```

```python
import functools

import jax
import jax.numpy as jnp
from jax import lax
from jax.experimental import pallas as pl
from jax.experimental.pallas import tpu as pltpu
from jax.sharding import PartitionSpec as P

HEADS = 16
HD = 64
DOCS = 4
COL = 256
BLOCK_PAD = 7

eps_norm = 1e-05
theta_base = 160000.0
LOG2E = 1.4426950408889634
NEG = -1e30
RSQRT2 = 0.7071067811865476
RSQRT2PI = 0.3989422804014327
bf16 = jnp.bfloat16
f32 = jnp.float32


def nt(left, right):
    return lax.dot_general(left, right, (((1,), (1,)), ((), ())), preferred_element_type=f32)


def nn(left, right):
    return lax.dot_general(left, right, (((1,), (0,)), ((), ())), preferred_element_type=f32)


def tn(left, right):
    return lax.dot_general(left, right, (((0,), (0,)), ((), ())), preferred_element_type=f32)


def params():
    return pltpu.CompilerParams(dimension_semantics=("arbitrary",))


def work(amount):
    return pl.CostEstimate(flops=int(amount), transcendentals=0, bytes_accessed=0)


def whole_spec(shape):
    zeros = (0,) * len(shape)
    return pl.BlockSpec(shape, lambda *_: zeros)


def mask_heads(rows, heads, groups):
    if groups == 1:
        return rows
    lane = lax.broadcasted_iota(jnp.int32, rows.shape, 1)
    parts = [
        jnp.where((lane >= h * HD) & (lane < (h + 1) * HD), rows, jnp.zeros_like(rows))
        for h in heads
    ]
    return jnp.concatenate(parts, 0) if len(parts) > 1 else parts[0]


def inside(low, high, shape, axis):
    at = lax.broadcasted_iota(jnp.int32, shape, axis)
    return (at >= low) & (at < high)

def for_sizes(part, tile, first_end, second_end):
    sizes = (tile // 2, tile) if tile % (2 * COL) == 0 else (tile,)

    def fits(size, end):
        small = end <= size
        return small if size == sizes[0] else jnp.logical_not(end <= sizes[0])

    for first in sizes:
        for second in sizes:
            if len(sizes) == 1:
                part(first, second)
            else:

                @pl.when(fits(first, first_end) & fits(second, second_end))
                def _():
                    part(first, second)


def safe_keys(keys, low, high):
    pick = jnp.where(lax.broadcasted_iota(jnp.int32, (16, keys.shape[0]), 1) == low, 1.0, 0.0)
    row = nn(pick.astype(bf16), keys)[0:1, :].astype(bf16)
    return jnp.where(inside(low, high, keys.shape, 0), keys, jnp.broadcast_to(row, keys.shape))


def tile_range(cuts_ref, doc, index, tile, length):
    first = cuts_ref[doc]
    last = cuts_ref[doc + 1]
    nominal = (first // 16) * 16 + index * tile
    off = pl.multiple_of(jnp.minimum(nominal, length - tile), 16)
    low = jnp.maximum(nominal, first) - off
    high = jnp.minimum(nominal + tile, last) - off
    return off, low, high


def tile_count(cuts_ref, doc, tile):
    base = (cuts_ref[doc] // 16) * 16
    return lax.div(cuts_ref[doc + 1] - base + (tile - 1), tile)


def attend_kernel(
    cuts_ref, q_ref, k_ref, v_ref, o_ref, lse_ref, vt_ref, m_ref, acc_ref, *, tile, groups, length
):
    width = groups * HD
    qf = q_ref.reshape(length, width)
    kf = k_ref.reshape(length, width)
    vf = v_ref.reshape(length, width)
    of = o_ref.reshape(length, width)
    wide = groups * tile
    vt_ref[:, width:, :] = jnp.ones((vt_ref.shape[0], 16, tile), bf16)

    def doc_step(doc, first_tile):
        count = tile_count(cuts_ref, doc, tile)

        def prepare(j, carry):
            off, low, high = tile_range(cuts_ref, doc, j, tile, length)
            vt_ref[j, 0:width, :] = vf[pl.ds(off, tile), :].T
            return carry

        lax.fori_loop(0, count, prepare, 0)

        def q_tile(i, carry):
            off, low, high = tile_range(cuts_ref, doc, i, tile, length)
            qm = mask_heads(qf[pl.ds(off, tile), :] * bf16(0.125), range(groups), groups)
            m_ref[...] = jnp.full(m_ref.shape, NEG, f32)
            acc_ref[...] = jnp.zeros(acc_ref.shape, f32)

            def k_tile(j, inner):
                koff, klow, khigh = tile_range(cuts_ref, doc, j, tile, length)

                def part(key_rows, _):
                    keep = inside(klow, khigh, (key_rows, wide), 0)
                    s = nt(kf[pl.ds(koff, key_rows), :], qm) * LOG2E
                    s = jnp.where(keep, s, NEG)
                    m_old = m_ref[0:1, :]
                    m_new = jnp.maximum(m_old, jnp.max(s, axis=0, keepdims=True))
                    p = jnp.exp2(s - m_new).astype(bf16)
                    acc_ref[...] = acc_ref[...] * jnp.exp2(m_old - m_new) + nn(
                        vt_ref[j, :, 0:key_rows], p
                    )
                    m_ref[0:1, :] = m_new

                key_sizes = (tile // 2, tile) if tile % (2 * COL) == 0 else (tile,)
                if len(key_sizes) == 1:
                    part(tile, None)
                else:

                    @pl.when(khigh <= key_sizes[0])
                    def _():
                        part(key_sizes[0], None)

                    @pl.when(khigh > key_sizes[0])
                    def _():
                        part(tile, None)

                return inner

            lax.fori_loop(0, count, k_tile, 0)
            total = acc_ref[width : width + 1, :]
            inverse = 1.0 / total
            lse_ref[first_tile + i, 0:1, :] = m_ref[0:1, :] + jnp.log2(total)
            parts = [
                acc_ref[h * HD : (h + 1) * HD, h * tile : (h + 1) * tile]
                * inverse[:, h * tile : (h + 1) * tile]
                for h in range(groups)
            ]
            out = (jnp.concatenate(parts, 0) if groups > 1 else parts[0]).T.astype(bf16)
            keep = inside(low, high, (tile, width), 0)
            of[pl.ds(off, tile), :] = jnp.where(keep, out, of[pl.ds(off, tile), :])
            return carry

        lax.fori_loop(0, count, q_tile, 0)
        return first_tile + count

    lax.fori_loop(0, DOCS, doc_step, 0)


def qkv_operands(headed):
    pieces, _, piece_len, width = headed[0].shape
    last = headed[-1].shape[1] - 1
    at = [(headed[0], 0), (headed[-1], last - 1), (headed[-1], last)]
    spec = lambda which: pl.BlockSpec(
        (pieces, None, piece_len, width), lambda i, cuts: (0, which, 0, 0)
    )
    return [array for array, _ in at], [spec(which) for _, which in at]


def attend(headed, cuts, tile):
    operands, specs = qkv_operands(headed)
    pieces, _, piece_len, width = headed[0].shape
    groups = width // HD
    length = pieces * piece_len
    tiles = length // tile + DOCS
    wide = groups * tile
    return pl.pallas_call(
        functools.partial(attend_kernel, tile=tile, groups=groups, length=length),
        out_shape=(
            jax.ShapeDtypeStruct((pieces, piece_len, width), bf16),
            jax.ShapeDtypeStruct((tiles, 8, wide), f32),
        ),
        grid_spec=pltpu.PrefetchScalarGridSpec(
            num_scalar_prefetch=1,
            grid=(1,),
            in_specs=specs,
            out_specs=[whole_spec((pieces, piece_len, width)), whole_spec((tiles, 8, wide))],
            scratch_shapes=[
                pltpu.VMEM((length // tile + 1, width + 16, tile), bf16),
                pltpu.VMEM((8, wide), f32),
                pltpu.VMEM((width + 16, wide), f32),
            ],
        ),
        compiler_params=params(),
        name="attend",
        cost_estimate=work(8192 * length * wide),
    )(cuts, *operands)


def attend_back_kernel(
    cuts_ref, q_ref, k_ref, v_ref, o_ref, do_ref, lse_ref, out_ref,
    qm_s, dom_s, lse_s, delta_s, dqt_s, ks_s, kt_s, p_s, ds_s, dk_s, dv_s, dqf, dkf, dvf,
    *, tile, groups, length, head,
):
    width = groups * HD
    own = slice(head * HD, (head + 1) * HD)
    qf = q_ref.reshape(length, width)
    kf = k_ref.reshape(length, width)
    vf = v_ref.reshape(length, width)
    of = o_ref.reshape(length, width)
    dof = do_ref.reshape(length, width)
    head_lane = lax.broadcasted_iota(jnp.int32, (16, width), 1)
    head_row = jnp.where(head_lane // HD == head, 1.0, 0.0).astype(bf16)

    def doc_step(doc, first_tile):
        count = tile_count(cuts_ref, doc, tile)

        def prepare(i, carry):
            off, low, high = tile_range(cuts_ref, doc, i, tile, length)
            spot = pl.ds(off, tile)
            qm_s[i] = mask_heads(qf[spot, :] * bf16(0.125), [head], groups)
            dom_s[i] = mask_heads(dof[spot, :], [head], groups)
            product = dof[spot, :].astype(f32) * of[spot, :].astype(f32)
            upper = product.astype(bf16)
            lower = (product - upper.astype(f32)).astype(bf16)
            delta_s[i, 0:1, :] = (nt(head_row, upper) + nt(head_row, lower))[0:1, :]
            lse = lse_ref[first_tile + i, 0:1, head * tile : (head + 1) * tile]
            lse_s[i, 0:1, :] = jnp.where(inside(low, high, (1, tile), 1), lse, -NEG)
            dqt_s[i] = jnp.zeros((HD, tile), f32)
            return carry

        lax.fori_loop(0, count, prepare, 0)

        def k_tile(j, carry):
            koff, klow, khigh = tile_range(cuts_ref, doc, j, tile, length)
            spot = pl.ds(koff, tile)
            keys = kf[spot, :]
            ks_s[...] = safe_keys(keys, klow, khigh)
            keys = jnp.where(inside(klow, khigh, keys.shape, 0), keys, jnp.zeros_like(keys))
            kt_s[...] = keys.T[own, :]
            dk_s[...] = jnp.zeros(dk_s.shape, f32)
            dv_s[...] = jnp.zeros(dv_s.shape, f32)

            def q_tile(i, inner):
                off, low, high = tile_range(cuts_ref, doc, i, tile, length)

                def part(key_rows, query_rows):
                    for c in range(0, query_rows, COL):
                        lanes = slice(c, c + COL)
                        qm = qm_s[i, lanes, :]
                        dom = dom_s[i, lanes, :]
                        for r in range(0, key_rows, COL):
                            rows = slice(r, r + COL)
                            s = nt(ks_s[rows, :], qm)
                            dp = nt(vf[pl.ds(pl.multiple_of(koff + r, 16), COL), :], dom)
                            p = jnp.exp2(s * LOG2E - lse_s[i, 0:1, lanes])
                            p_s[rows, lanes] = p.astype(bf16)
                            ds_s[rows, lanes] = (p * (dp - delta_s[i, 0:1, lanes])).astype(bf16)
                    k, q = slice(0, key_rows), slice(0, query_rows)
                    dv_s[k, :] += nn(p_s[k, q], dom_s[i, q, :])
                    dk_s[k, :] += nn(ds_s[k, q], qm_s[i, q, :])
                    dqt_s[i, :, q] += nn(kt_s[:, k], ds_s[k, q])

                for_sizes(part, tile, khigh, high)
                return inner

            lax.fori_loop(0, count, q_tile, 0)
            keep = inside(klow, khigh, (tile, width), 0)
            dkf[spot, :] = jnp.where(keep, dk_s[...].astype(bf16), dkf[spot, :])
            dvf[spot, :] = jnp.where(keep, dv_s[...].astype(bf16), dvf[spot, :])
            return carry

        lax.fori_loop(0, count, k_tile, 0)

        def finish(i, carry):
            off, low, high = tile_range(cuts_ref, doc, i, tile, length)
            out = (dqt_s[i] * 0.125).T.astype(bf16)
            spot = pl.ds(off, tile)
            dqf[spot, :] = jnp.where(inside(low, high, (tile, HD), 0), out, dqf[spot, :])
            return carry

        lax.fori_loop(0, count, finish, 0)
        return first_tile + count

    lax.fori_loop(0, DOCS, doc_step, 0)
    piece_len = q_ref.shape[1]
    fold = piece_len // groups
    for at in range(q_ref.shape[0]):
        for which, full in enumerate((dqf, dkf, dvf)):
            start = at * piece_len
            lanes = slice(0, HD) if which == 0 else own
            parts = [full[start + g * fold : start + (g + 1) * fold, lanes] for g in range(groups)]
            out_ref[at, which] = jnp.concatenate(parts, 1) if groups > 1 else parts[0]

def attend_back(headed, o, do, lse, cuts, tile, head):
    operands, specs = qkv_operands(headed)
    pieces, _, piece_len, width = headed[0].shape
    groups = width // HD
    length = pieces * piece_len
    tiles = length // tile + DOCS
    per_doc = length // tile + 1
    flat = whole_spec((pieces, piece_len, width))
    out = (pieces, 3, piece_len // groups, width)
    return pl.pallas_call(
        functools.partial(attend_back_kernel, tile=tile, groups=groups, length=length, head=head),
        out_shape=jax.ShapeDtypeStruct(out, bf16),
        grid_spec=pltpu.PrefetchScalarGridSpec(
            num_scalar_prefetch=1,
            grid=(1,),
            in_specs=specs
            + [flat, flat, whole_spec((tiles, 8, groups * tile))],
            out_specs=whole_spec(out),
            scratch_shapes=[
                pltpu.VMEM((per_doc, tile, width), bf16),
                pltpu.VMEM((per_doc, tile, width), bf16),
                pltpu.VMEM((per_doc, 8, tile), f32),
                pltpu.VMEM((per_doc, 8, tile), f32),
                pltpu.VMEM((per_doc, HD, tile), f32),
                pltpu.VMEM((tile, width), bf16),
                pltpu.VMEM((HD, tile), bf16),
                pltpu.VMEM((tile, tile), bf16),
                pltpu.VMEM((tile, tile), bf16),
                pltpu.VMEM((tile, width), f32),
                pltpu.VMEM((tile, width), f32),
            ]
            + [pltpu.VMEM((length, HD), bf16)]
            + [pltpu.VMEM((length, width), bf16)] * 2,
        ),
        compiler_params=params(),
        name="attend_back",
        cost_estimate=work(16384 * length * tile),
    )(cuts, *operands, o, do, lse)


def normalize(values):
    center = values - jnp.mean(values, axis=-1, keepdims=True)
    spread = jnp.mean(center * center, axis=-1, keepdims=True)
    scale = lax.rsqrt(spread + eps_norm)
    return center * scale, scale


def norm_back(unit, scale, scaled_grad):
    return scale * (
        scaled_grad
        - jnp.mean(scaled_grad, axis=-1, keepdims=True)
        - unit * jnp.mean(scaled_grad * unit, axis=-1, keepdims=True)
    )


def lane_swap(values):
    lane = lax.broadcasted_iota(jnp.int32, values.shape, 1)
    size = values.shape[1]
    half = HD // 2
    return jnp.where(
        lane % HD < half, pltpu.roll(values, size - half, 1), pltpu.roll(values, half, 1)
    )


def norm_kernel(x_ref, g_ref, a_ref, norm_ref, small_ref):
    unit, _ = normalize(x_ref[...].astype(f32))
    norm = (unit * g_ref[...]).astype(bf16)
    norm_ref[...] = norm
    small_ref[...] = nt(a_ref[...], norm).astype(bf16)


def norm_call(x, gain, a):
    count, rows, model = x.shape
    rank = a.shape[1]
    return pl.pallas_call(
        norm_kernel,
        grid=(count,),
        out_shape=(
            jax.ShapeDtypeStruct((count, rows, model), bf16),
            jax.ShapeDtypeStruct((count, rank, rows), bf16),
        ),
        in_specs=[
            pl.BlockSpec((None, rows, model), lambda s: (s, 0, 0)),
            whole_spec((1, model)),
            pl.BlockSpec((None, rank, model), lambda s: (s, 0, 0)),
        ],
        out_specs=[
            pl.BlockSpec((None, rows, model), lambda s: (s, 0, 0)),
            pl.BlockSpec((None, rank, rows), lambda s: (s, 0, 0)),
        ],
        compiler_params=params(),
        name="norm",
        cost_estimate=work(4096 * count * rows * model),
    )(x, gain, a)


def both_halves(core, own_ref, other_ref):
    groups, chips = own_ref.shape[:2]
    slabs = []
    for d in range(groups):
        for c in range(chips):
            own, other = own_ref[d, c], other_ref[d, c]
            slabs += [jnp.where(core == 0, own, other), jnp.where(core == 0, other, own)]
    return jnp.concatenate(slabs, 0)


def qkv_kernel(core_ref, norm_ref, small_ref, *refs, width, kinds):
    count = len(kinds)
    w_refs, b_refs = refs[: 2 * count], refs[2 * count : 3 * count]
    cos_ref, sin_ref, out_ref = refs[3 * count :]
    core = core_ref[0]
    norm = norm_ref[...]
    small = small_ref[...]
    for at, kind in enumerate(kinds):
        w = both_halves(core, w_refs[2 * at], w_refs[2 * at + 1])
        lin = nn(norm, w) + tn(small, b_refs[at][...])
        for part in range(COL // 128):
            u = lin[:, part * 128 : (part + 1) * 128]
            if kind < 2:
                u = u * cos_ref[...] + lane_swap(u) * sin_ref[...]
            u = u.astype(bf16)
            for sub in range(128 // width):
                dest = part * (128 // width) + sub
                out_ref[dest, at] = u[:, sub * width : (sub + 1) * width]


def half_specs(shape, steps, kinds):
    block = shape[:-1] + (COL,)
    spec = lambda kind: pl.BlockSpec(block, lambda j, core: (0, 0, 0, kind * steps + j))
    return [spec(kind) for kind in kinds for _ in range(2)]


def qkv_project(at, kinds, norm, small, core, halves, b, cosine, sine, pieces, width):
    _, rows, model = norm.shape
    dests = COL // width
    steps = model // COL
    rank = small.shape[1]
    count = len(kinds)
    row_spec = lambda shape: pl.BlockSpec((None,) + shape, lambda j, core: (at, 0, 0))
    b_spec = lambda kind: pl.BlockSpec((rank, COL), lambda j, core: (0, kind * steps + j))
    return pl.pallas_call(
        functools.partial(qkv_kernel, width=width, kinds=kinds),
        out_shape=jax.ShapeDtypeStruct((pieces, count, rows, width), bf16),
        grid_spec=pltpu.PrefetchScalarGridSpec(
            num_scalar_prefetch=1,
            grid=(steps,),
            in_specs=[row_spec((rows, model)), row_spec((rank, rows))]
            + half_specs(halves[0].shape, steps, kinds)
            + [b_spec(kind) for kind in kinds]
            + [row_spec((rows, 128)), row_spec((rows, 128))],
            out_specs=pl.BlockSpec((dests, count, rows, width), lambda j, core: (j, 0, 0, 0)),
        ),
        compiler_params=params(),
        name="qkv_project",
        cost_estimate=work(2 * count * rows * model * model),
    )(core, norm, small, *halves * count, *[b] * count, cosine, sine)


def join_heads(refs, dest, which):
    if len(refs) == 1:
        return refs[0][dest, which]
    blocks = [ref[dest, which] for ref in refs]
    folds = [
        jnp.concatenate([block[:, g * HD : (g + 1) * HD] for block in blocks], 1)
        for g in range(len(refs))
    ]
    return jnp.concatenate(folds, 0)


def dlin_kernel(*args, width, heads):
    dqkv_refs = args[:heads]
    norm_ref, small_ref = args[heads : heads + 2]
    b_refs = args[heads + 2 : heads + 5]
    cos_ref, sin_ref, dlin_ref, dsmall_ref, grad_ref, acc_ref = args[heads + 5 :]
    step = pl.program_id(0)

    @pl.when(step == 0)
    def _():
        acc_ref[...] = jnp.zeros(acc_ref.shape, f32)

    small = small_ref[...]
    per = 128 // width
    for which in range(3):
        pieces = []
        for part in range(COL // 128):
            subs = [join_heads(dqkv_refs, part * per + sub, which) for sub in range(per)]
            u = jnp.concatenate(subs, 1) if per > 1 else subs[0]
            if which < 2:
                u = u.astype(f32)
                u = (u * cos_ref[...] - lane_swap(u) * sin_ref[...]).astype(bf16)
            pieces.append(u)
        dlin = jnp.concatenate(pieces, 1)
        dlin_ref[which] = dlin
        acc_ref[...] += nt(b_refs[which][...], dlin)
        grad_ref[(which + 1) * pl.num_programs(0) + step] = nn(small, dlin)

    @pl.when(step == pl.num_programs(0) - 1)
    def _():
        dsmall = acc_ref[...].astype(bf16)
        dsmall_ref[...] = dsmall
        grad_a = nn(dsmall, norm_ref[...])
        for at in range(grad_a.shape[1] // COL):
            grad_ref[at] = grad_a[:, at * COL : (at + 1) * COL]


def dlin_call(at, dqkv, norm, small, b, cosine, sine):
    _, _, fold, width = dqkv[0].shape
    _, rows, model = norm.shape
    rank = small.shape[1]
    dests = COL // width
    steps = model // COL
    b_spec = lambda kind: pl.BlockSpec((rank, COL), lambda j: (0, kind * steps + j))
    row_spec = lambda shape: pl.BlockSpec((None,) + shape, lambda j: (at, 0, 0))
    return pl.pallas_call(
        functools.partial(dlin_kernel, width=width, heads=len(dqkv)),
        grid=(steps,),
        out_shape=(
            jax.ShapeDtypeStruct((3, rows, model), bf16),
            jax.ShapeDtypeStruct((rank, rows), bf16),
            jax.ShapeDtypeStruct((4 * steps, rank, COL), f32),
        ),
        in_specs=[pl.BlockSpec((dests, 3, fold, width), lambda j: (j, 0, 0, 0))] * len(dqkv)
        + [
            row_spec((rows, model)),
            row_spec((rank, rows)),
            *[b_spec(kind) for kind in range(3)],
            row_spec((rows, 128)),
            row_spec((rows, 128)),
        ],
        out_specs=[
            pl.BlockSpec((3, rows, COL), lambda j: (0, 0, j)),
            whole_spec((rank, rows)),
            whole_spec((4 * steps, rank, COL)),
        ],
        scratch_shapes=[pltpu.VMEM((rank, rows), f32)],
        compiler_params=params(),
        name="dlin",
        cost_estimate=work(4 * rows * model * model),
    )(*dqkv, norm, small, b, b, b, cosine, sine)


def input_grad_kernel(core_ref, dlin_ref, dsmall_ref, x_ref, g_ref, dmid_ref, *refs):
    w_refs = refs[:6]
    a_ref = refs[6]
    out_ref, acc_ref = refs[-2:]
    step = pl.program_id(0)
    core = core_ref[0]
    value = sum(
        nt(dlin_ref[which], both_halves(core, w_refs[2 * which], w_refs[2 * which + 1]))
        for which in range(3)
    )

    @pl.when(step == 0)
    def _():
        acc_ref[...] = value + tn(dsmall_ref[...], a_ref[...])

    @pl.when(step > 0)
    def _():
        acc_ref[...] += value

    @pl.when(step == pl.num_programs(0) - 1)
    def _():
        unit, scale = normalize(x_ref[...].astype(f32))
        out_ref[...] = (
            dmid_ref[...] + norm_back(unit, scale, acc_ref[...] * g_ref[...])
        ).astype(bf16)


def input_grad_call(at, given, dlin, dsmall, x, gain, dmid, core, halves, a):
    count, rows, model = x.shape
    given = [] if given is None else [given]
    rank = a.shape[0]
    steps = model // COL
    return pl.pallas_call(
        input_grad_kernel,
        out_shape=jax.ShapeDtypeStruct((count, rows, model), bf16),
        grid_spec=pltpu.PrefetchScalarGridSpec(
            num_scalar_prefetch=1,
            grid=(steps,),
            in_specs=[
                pl.BlockSpec((3, rows, COL), lambda j, core: (0, 0, j)),
                whole_spec((rank, rows)),
                pl.BlockSpec((None, rows, model), lambda j, core: (at, 0, 0)),
                whole_spec((1, model)),
                whole_spec((rows, model)),
            ]
            + half_specs(halves[0].shape, steps, range(3))
            + [whole_spec((rank, model))]
            + [pl.BlockSpec(memory_space=pl.ANY)] * len(given),
            out_specs=pl.BlockSpec((None, rows, model), lambda j, core: (at, 0, 0)),
            scratch_shapes=[pltpu.VMEM((rows, model), f32)],
        ),
        input_output_aliases={13: 0} if given else {},
        compiler_params=params(),
        name="input_grad",
        cost_estimate=work(8 * rows * model * model),
    )(core, dlin, dsmall, x, gain, dmid, *halves * 3, a, *given)


def mlp_kernel(
    x_ref, cot_ref, o_ref, g_ref, wo_ref, wu_ref, wv_ref, wt_ref,
    aout_ref, bout_ref, ain_ref, bu_ref, bv_ref, a2_ref, b2_ref, id_ref, *rest, width,
):
    mlp_body(
        x_ref, cot_ref, o_ref, g_ref, wo_ref, wu_ref, wv_ref, wt_ref,
        aout_ref, bout_ref, ain_ref, bu_ref, bv_ref, a2_ref, b2_ref, id_ref, *rest, width=width,
    )


def natural(ref):
    cores, groups, chips = ref.shape[:3]
    return jnp.concatenate(
        [ref[core, d, c] for d in range(groups) for c in range(chips) for core in range(cores)], 0
    )


def mlp_body(
    x_ref, cot_ref, o_ref, g_ref, wo_ref, wu_ref, wv_ref, wt_ref,
    aout_ref, bout_ref, ain_ref, bu_ref, bv_ref, a2_ref, b2_ref, id_ref,
    out_ref, dmid_ref, datt_ref, grad_ref,
    att_s, norm_s, unit_s, scale_s, acc_s, dnorm_s, small2_s, small3_s, small4_s, dsmall4_s, dsmall3_s,
    *, width,
):
    step = pl.program_id(0)
    pieces = o_ref.shape[0]
    model = x_ref.shape[1]
    per = model // COL
    first_block = grad_ref.shape[0] - BLOCK_PAD - 4 * per

    def put(which, value):
        for at in range(per):
            grad_ref[first_block + which * per + at] = value[:, at * COL : (at + 1) * COL]

    @pl.when(step == 0)
    def _():
        for at in range(first_block + 4 * per, grad_ref.shape[0]):
            grad_ref[at] = id_ref[...]
        for at in range(pieces):
            att_s[:, at * width : (at + 1) * width] = o_ref[at]
        att = att_s[...]
        small2 = nt(aout_ref[...], att).astype(bf16)
        small2_s[...] = small2
        middle = x_ref[...].astype(f32) + nn(att, natural(wo_ref)) + tn(small2, bout_ref[...])
        acc_s[...] = middle
        unit, scale = normalize(middle)
        unit_s[...] = unit
        scale_s[...] = jnp.broadcast_to(scale, scale_s.shape)
        norm = (unit * g_ref[...]).astype(bf16)
        norm_s[...] = norm
        small3_s[...] = nt(ain_ref[...], norm).astype(bf16)
        dsmall4_s[...] = nt(b2_ref[...], cot_ref[...]).astype(bf16)
        dnorm_s[...] = jnp.zeros(dnorm_s.shape, f32)
        small4_s[...] = jnp.zeros(small4_s.shape, f32)
        dsmall3_s[...] = jnp.zeros(dsmall3_s.shape, f32)

    norm = norm_s[...]
    small3 = small3_s[...]
    dsmall4 = dsmall4_s[...]
    wu, wv, wt = natural(wu_ref), natural(wv_ref), natural(wt_ref)
    u = nn(norm, wu) + tn(small3, bu_ref[...])
    v = nn(norm, wv) + tn(small3, bv_ref[...])
    dmixed = nn(cot_ref[...], wt) + tn(dsmall4, a2_ref[...])
    below = 0.5 * (1.0 + lax.erf(u * RSQRT2))
    gelu = u * below
    mixed = (gelu * v).astype(bf16)
    slope = below + u * (jnp.exp(-0.5 * u * u) * RSQRT2PI)
    du = (dmixed * v * slope).astype(bf16)
    dv = (dmixed * gelu).astype(bf16)
    acc_s[...] += nt(mixed, wt)
    dnorm_s[...] += nt(du, wu) + nt(dv, wv)
    small4_s[...] += nt(a2_ref[...], mixed)
    dsmall3_s[...] += nt(bu_ref[...], du) + nt(bv_ref[...], dv)
    steps = pl.num_programs(0)
    grad_ref[step] = nn(small3, du)
    grad_ref[steps + step] = nn(small3, dv)
    grad_ref[2 * steps + step] = nn(dsmall4, mixed)

    @pl.when(step == pl.num_programs(0) - 1)
    def _():
        small4 = small4_s[...].astype(bf16)
        dsmall3 = dsmall3_s[...].astype(bf16)
        out_ref[...] = (acc_s[...] + tn(small4, b2_ref[...])).astype(bf16)
        put(3, nn(small4, cot_ref[...]))
        dnorm = dnorm_s[...] + tn(dsmall3, ain_ref[...])
        put(2, nn(dsmall3, norm_s[...]))
        dmid = cot_ref[...].astype(f32) + norm_back(unit_s[...], scale_s[:, 0:1], dnorm * g_ref[...])
        dmid_ref[...] = dmid
        dlow = dmid.astype(bf16)
        dsmall2 = nt(bout_ref[...], dlow).astype(bf16)
        put(1, nn(small2_s[...], dlow))
        put(0, nn(dsmall2, att_s[...]))
        datt = (nt(dlow, natural(wo_ref)) + tn(dsmall2, aout_ref[...])).astype(bf16)
        for at in range(pieces):
            datt_ref[at] = datt[:, at * width : (at + 1) * width]


def mlp_call(
    which_seq, x, cot, o, gain, w_all, a_out, b_out, a_in, b_u, b_v, a_out2, b_out2, own_id
):
    seq_count, rows, model = x.shape
    pieces, _, width = o.shape
    rank = a_out.shape[0]
    hidden = b_u.shape[1]
    steps = hidden // COL
    blocks = 3 * steps + 4 * (model // COL) + BLOCK_PAD
    full = lambda shape: pl.BlockSpec(shape, lambda j: (0,) * len(shape), pipeline_mode=pl.Buffered(1))
    lead = w_all.shape[:-1]
    ff_spec = lambda which: pl.BlockSpec(
        lead + (COL,), lambda j: (0, 0, 0, 0, model // COL + which * steps + j)
    )
    one_seq = pl.BlockSpec((None, rows, model), lambda j: (which_seq, 0, 0))
    small_ff = pl.BlockSpec((rank, COL), lambda j: (0, j))
    small = full((rank, model))
    return pl.pallas_call(
        functools.partial(mlp_kernel, width=width),
        grid=(steps,),
        out_shape=(
            jax.ShapeDtypeStruct((rows, model), bf16),
            jax.ShapeDtypeStruct((rows, model), f32),
            jax.ShapeDtypeStruct((pieces, rows, width), bf16),
            jax.ShapeDtypeStruct((blocks, rank, COL), f32),
        ),
        in_specs=[
            one_seq,
            one_seq,
            full((pieces, rows, width)),
            full((1, model)),
            full(lead + (model,)),
            ff_spec(0),
            ff_spec(1),
            ff_spec(2),
            small,
            small,
            small,
            small_ff,
            small_ff,
            small_ff,
            small,
            full((rank, COL)),
        ],
        out_specs=[
            whole_spec((rows, model)),
            whole_spec((rows, model)),
            whole_spec((pieces, rows, width)),
            whole_spec((blocks, rank, COL)),
        ],
        scratch_shapes=[
            pltpu.VMEM((rows, model), bf16),
            pltpu.VMEM((rows, model), bf16),
            pltpu.VMEM((rows, model), f32),
            pltpu.VMEM((rows, 128), f32),
            pltpu.VMEM((rows, model), f32),
            pltpu.VMEM((rows, model), f32),
            pltpu.VMEM((rank, rows), bf16),
            pltpu.VMEM((rank, rows), bf16),
            pltpu.VMEM((rank, rows), f32),
            pltpu.VMEM((rank, rows), bf16),
            pltpu.VMEM((rank, rows), f32),
        ],
        compiler_params=params(),
        name="feed_forward",
        cost_estimate=work(26 * rows * model * hidden),
    )(
        x, cot, o, gain, w_all, w_all, w_all, w_all, a_out, b_out, a_in, b_u, b_v, a_out2, b_out2,
        own_id,
    )


def assemble_kernel(ids_ref, *refs, layout, arrays):
    which = pl.program_id(0)
    sources, outs, acc_ref = refs[:arrays], refs[arrays:-1], refs[-1]
    acc_ref[...] = jnp.zeros(acc_ref.shape, f32)
    count = sources[0].shape[0]
    for at, source in enumerate(sources):

        def add(index, carry):
            @pl.when(ids_ref[at * count + index] == which)
            def _():
                acc_ref[...] += source[index].astype(f32)

            return carry

        lax.fori_loop(0, count, add, 0)
    for out_ref, segments in zip(outs, layout):
        start = 0
        for first, blocks, size in segments:
            for block in range(blocks):
                wide = min(COL, size - block * COL)
                if wide > 0:
                    spot = start + block * COL
                    out_ref[:, spot : spot + wide] = acc_ref[first + block][:, :wide]
            start += size


def assemble_call(sources, ids, adapters, layout):
    _, blocks, rank, _ = sources[0].shape
    sizes = [sum(size for _, _, size in segments) for segments in layout]
    return pl.pallas_call(
        functools.partial(assemble_kernel, layout=layout, arrays=len(sources)),
        out_shape=[jax.ShapeDtypeStruct((adapters, rank, size), f32) for size in sizes],
        grid_spec=pltpu.PrefetchScalarGridSpec(
            num_scalar_prefetch=1,
            grid=(adapters,),
            in_specs=[whole_spec(source.shape) for source in sources],
            out_specs=[pl.BlockSpec((None, rank, size), lambda e, ids: (e, 0, 0)) for size in sizes],
            scratch_shapes=[pltpu.VMEM((blocks, rank, COL), f32)],
        ),
        compiler_params=params(),
        name="assemble",
        cost_estimate=work(4096 * adapters * rank * sum(sizes) // 256),
    )(ids, *sources)


def pad_columns(values, size):
    return jnp.pad(values, [(0, 0)] * (values.ndim - 1) + [(0, size - values.shape[-1])])


def local(
    tokens,
    segment_ids,
    positions,
    adapter_id,
    gain_attn,
    gain_mlp,
    w_qkv,
    w_out,
    w_in,
    w_out2,
    a_qkv,
    b_qkv,
    a_out,
    b_out,
    a_in,
    b_in,
    a_out2,
    b_out2,
    cotangent,
):
    seq_count, piece_len, model = tokens.shape
    pieces = lax.axis_size("seq")
    groups = HEADS // pieces
    width = groups * HD
    length = piece_len * pieces
    rank = a_qkv.shape[1]
    adapters = a_qkv.shape[0]
    hidden = w_out2.shape[0]
    padded = -(-hidden // COL) * COL
    tile = min(512, length)
    both = ("dp", "seq")

    dp = lax.axis_size("dp")
    before = [jnp.sum((segment_ids < d).astype(jnp.int32), axis=1) for d in range(1, DOCS)]
    swap = lambda value: lax.all_to_all(value, "seq", split_axis=0, concat_axis=0, tiled=True)
    facts = jnp.stack(before, 1)
    shard = jnp.concatenate(
        [
            w_out,
            pad_columns(w_in[:, :hidden], padded),
            pad_columns(w_in[:, hidden:], padded),
            pad_columns(w_out2.T, padded),
        ],
        1,
    )
    chips = pieces // 2
    same_core = [[2 * chip + core for chip in range(chips)] for core in range(2)]
    same_chip = [[2 * chip, 2 * chip + 1] for chip in range(chips)]
    half = HD // 2
    lane = jnp.arange(128, dtype=jnp.int32) % HD
    frequency = theta_base ** (-((lane % half).astype(f32) * 2.0) / HD)
    angles = positions.astype(f32)[..., None] * frequency
    cosine = jnp.cos(angles)
    sine = jnp.where(lane < half, -1.0, 1.0) * jnp.sin(angles)

    gain1 = gain_attn.reshape(1, model)
    gain2 = gain_mlp.reshape(1, model)
    pick = lambda table, s: lax.dynamic_index_in_dim(table, adapter_id[s], 0, keepdims=False)
    each = range(seq_count)

    aq = [pick(a_qkv, s) for s in each]
    bq = [pick(b_qkv, s) for s in each]
    norm, small = norm_call(tokens, gain1, jnp.stack(aq, 0))
    maps = []
    for s in each:
        b_in_s = pick(b_in, s)
        maps.append(
            (
                pick(a_out, s),
                pick(b_out, s),
                pick(a_in, s),
                pad_columns(b_in_s[:, :hidden], padded),
                pad_columns(b_in_s[:, hidden:], padded),
                pad_columns(pick(a_out2, s), padded),
                pick(b_out2, s),
                jnp.full((rank, COL), adapter_id[s].astype(f32)),
            )
        )
    same_pair = [(at, at ^ 1) for at in range(pieces)]
    core = (lax.axis_index("seq") % 2).astype(jnp.int32).reshape(1)
    qkv_column = lax.all_gather(w_qkv, "seq", axis=0, tiled=True, axis_index_groups=same_core)
    qkv_column, shard = lax.optimization_barrier((qkv_column, shard))
    qkv_own = lax.all_to_all(
        jnp.broadcast_to(qkv_column[None], (dp,) + qkv_column.shape),
        "dp",
        split_axis=0,
        concat_axis=0,
        tiled=True,
    ).reshape(dp, chips, -1, 3 * model)
    ready = (qkv_own, facts, norm, small, cosine, sine, bq)
    qkv_own, facts, norm, small, cosine, sine, bq = lax.optimization_barrier(ready)
    counts = jnp.sum(swap(jnp.broadcast_to(facts[None], (pieces,) + facts.shape)), 0)
    cuts = jnp.concatenate(
        [
            jnp.zeros((seq_count, 1), jnp.int32),
            counts,
            jnp.full((seq_count, 1), length, jnp.int32),
        ],
        1,
    )
    halves = [qkv_own, lax.ppermute(qkv_own, "seq", same_pair)]
    column = lax.all_gather(shard, "seq", axis=0, tiled=True, axis_index_groups=same_core)

    def project_of(s, kinds):
        return qkv_project(
            s, kinds, norm, small, core, halves, bq[s], cosine, sine, pieces, width
        )

    packed = [[project_of(0, (0, 1, 2))]]
    norm, packed[0], column, cuts = lax.optimization_barrier((norm, packed[0], column, cuts))
    own = lax.all_gather(column, "dp", axis=0, tiled=True)
    packed.append([project_of(1, (0,)), project_of(1, (1, 2))])
    maps, packed[1] = lax.optimization_barrier((maps, packed[1]))
    headed = [[swap(packed[0][0])]]
    packed[1], headed[0] = lax.optimization_barrier((packed[1], headed[0]))
    query_keys = swap(packed[1][0])
    attended = [attend(headed[0], cuts[0], tile)]
    own, attended[0], query_keys = lax.optimization_barrier((own, attended[0], query_keys))
    full_rest = lax.all_gather(own, "seq", axis=0, tiled=True, axis_index_groups=same_chip)
    full_rest = full_rest.reshape(2, dp, chips, -1, full_rest.shape[-1])
    query_keys, o_first = lax.optimization_barrier((query_keys, attended[0][0]))
    o_tokens = [swap(o_first)]
    values, o_tokens[0] = lax.optimization_barrier((packed[1][1], o_tokens[0]))
    values = swap(values)

    def feed_forward(s):
        return mlp_call(
            s, tokens, cotangent, o_tokens[s], gain2, full_rest, *maps[s]
        )

    middle = [feed_forward(0)]

    def scatter(grads):
        lead = grads.reshape(-1, COL)
        return lax.psum_scatter(lead, "seq", scatter_dimension=0, tiled=True).astype(bf16)

    first_sum = scatter(middle[0][3])
    values, query_keys, middle[0] = lax.optimization_barrier((values, query_keys, middle[0]))
    headed.append([query_keys, values])
    do_items = [swap(middle[0][2])]
    attended.append(attend(headed[1], cuts[1], tile))
    do_items[0], attended[1], first_sum = lax.optimization_barrier(
        (do_items[0], attended[1], first_sum)
    )

    def back(s, h):
        return attend_back(
            headed[s], attended[s][0], do_items[s], attended[s][1], cuts[s], tile, h
        )

    first_back = back(0, 0)
    o_tokens.append(swap(attended[1][0]))
    o_tokens[1], _ = lax.optimization_barrier((o_tokens[1], first_back))
    dqkv = [[swap(first_back)]]
    middle.append(feed_forward(1))
    second_sum = scatter(middle[1][3])
    dqkv[0][0], do_second = lax.optimization_barrier((dqkv[0][0], middle[1][2]))
    do_items.append(swap(do_second))
    do_items[0], _ = lax.optimization_barrier((do_items[0], middle[1][3]))
    ff = padded // COL
    per = model // COL
    mods = 3 * ff

    def dlin_of(s):
        return dlin_call(s, dqkv[s], norm, small, bq[s], cosine, sine)

    def input_grad_of(s, dlin, given):
        return input_grad_call(
            s, given, dlin[0], dlin[1], tokens, gain1, middle[s][1], core, halves, aq[s]
        )

    others = [back(0, h) for h in range(1, groups)]
    dqkv[0] += [swap(part) for part in others]
    do_items[1], second_sum, _ = lax.optimization_barrier((do_items[1], second_sum, others))
    parts = [back(1, h) for h in range(groups)]
    parts[0], dqkv[0] = lax.optimization_barrier((parts[0], dqkv[0]))
    dqkv.append([swap(part) for part in parts])
    sums = jnp.stack([first_sum, second_sum], 0)
    sums, dqkv[1][0], _ = lax.optimization_barrier((sums, dqkv[1][0], parts[-1]))
    every = lax.all_gather(sums[None], both, axis=0, tiled=True)
    every = every.reshape((dp, pieces) + sums.shape)
    gathered = [every[:, :, s].reshape(dp, -1, rank, COL) for s in each]
    ids = [
        (part[:, -1, 0, 0].astype(f32) * (1.0 / pieces)).astype(jnp.int32) for part in gathered
    ]
    dlins = [dlin_of(0)]
    input_grads = input_grad_of(0, dlins[0], None)
    dqkv[1], input_grads = lax.optimization_barrier((dqkv[1], input_grads))
    dlins += [dlin_of(s) for s in each[1:]]
    late_grads = jnp.stack([dlins[s][2] for s in each], 0)
    parts = swap(late_grads.astype(bf16).reshape(pieces, -1, COL))
    mine = jnp.sum(parts.astype(f32), 0).astype(bf16)
    copies = jnp.broadcast_to(mine[None], (dp * pieces,) + mine.shape)
    every = lax.all_to_all(copies, both, split_axis=0, concat_axis=0, tiled=True)
    for s in each[1:]:
        input_grads = input_grad_of(s, dlins[s], input_grads)
    early = assemble_call(
        gathered,
        jnp.concatenate(ids),
        adapters,
        [[(mods + which * per, per, model)] for which in range(3)]
        + [[(0, ff, hidden), (ff, ff, hidden)], [(2 * ff, ff, hidden)], [(mods + 3 * per, per, model)]],
    )
    late = assemble_call(
        [every.reshape((dp * seq_count,) + late_grads.shape[1:])],
        jnp.stack(ids, 1).reshape(-1),
        adapters,
        [[(0, per, model)], [(per, 3 * per, 3 * model)]],
    )
    layer_out = jnp.stack([middle[s][0] for s in each], 0)
    return (
        layer_out,
        input_grads,
        late[0],
        late[1],
        early[0],
        early[1],
        early[2],
        early[3],
        early[4],
        early[5],
    )


def solution(mesh):
    placed = (
        P("dp", "seq", None),
        P("dp", "seq"),
        P("dp", "seq"),
        P("dp"),
        P(),
        P(),
        P(("dp", "seq"), None),
        P(("dp", "seq"), None),
        P(("dp", "seq"), None),
        P(None, ("dp", "seq")),
        P(),
        P(),
        P(),
        P(),
        P(),
        P(),
        P(),
        P(),
        P("dp", "seq", None),
    )
    return jax.shard_map(
        local,
        mesh=mesh,
        in_specs=placed,
        out_specs=(
            P("dp", "seq", None),
            P("dp", "seq", None),
            P(),
            P(),
            P(),
            P(),
            P(),
            P(),
            P(),
            P(),
        ),
        check_vma=False,
    )
```

```python
import functools

import jax
import jax.numpy as jnp
from jax import lax
from jax.experimental import pallas as pl
from jax.experimental.pallas import tpu as pltpu
from jax.sharding import PartitionSpec as P

HEADS = 16
HD = 64
DOCS = 4
COL = 256
BLOCK_PAD = 7

eps_norm = 1e-05
theta_base = 160000.0
LOG2E = 1.4426950408889634
NEG = -1e30
RSQRT2 = 0.7071067811865476
RSQRT2PI = 0.3989422804014327
bf16 = jnp.bfloat16
f32 = jnp.float32


def nt(left, right):
    return lax.dot_general(left, right, (((1,), (1,)), ((), ())), preferred_element_type=f32)


def nn(left, right):
    return lax.dot_general(left, right, (((1,), (0,)), ((), ())), preferred_element_type=f32)


def tn(left, right):
    return lax.dot_general(left, right, (((0,), (0,)), ((), ())), preferred_element_type=f32)


def params():
    return pltpu.CompilerParams(dimension_semantics=("arbitrary",))


def work(amount):
    return pl.CostEstimate(flops=int(amount), transcendentals=0, bytes_accessed=0)


def whole_spec(shape):
    zeros = (0,) * len(shape)
    return pl.BlockSpec(shape, lambda *_: zeros)


def mask_heads(rows, heads, groups):
    if groups == 1:
        return rows
    lane = lax.broadcasted_iota(jnp.int32, rows.shape, 1)
    parts = [
        jnp.where((lane >= h * HD) & (lane < (h + 1) * HD), rows, jnp.zeros_like(rows))
        for h in heads
    ]
    return jnp.concatenate(parts, 0) if len(parts) > 1 else parts[0]


def inside(low, high, shape, axis):
    at = lax.broadcasted_iota(jnp.int32, shape, axis)
    return (at >= low) & (at < high)

def for_sizes(part, tile, first_end, second_end):
    sizes = (tile // 2, tile) if tile % (2 * COL) == 0 else (tile,)

    def fits(size, end):
        small = end <= size
        return small if size == sizes[0] else jnp.logical_not(end <= sizes[0])

    for first in sizes:
        for second in sizes:
            if len(sizes) == 1:
                part(first, second)
            else:

                @pl.when(fits(first, first_end) & fits(second, second_end))
                def _():
                    part(first, second)


def safe_keys(keys, low, high):
    pick = jnp.where(lax.broadcasted_iota(jnp.int32, (16, keys.shape[0]), 1) == low, 1.0, 0.0)
    row = nn(pick.astype(bf16), keys)[0:1, :].astype(bf16)
    return jnp.where(inside(low, high, keys.shape, 0), keys, jnp.broadcast_to(row, keys.shape))


def tile_range(cuts_ref, doc, index, tile, length):
    first = cuts_ref[doc]
    last = cuts_ref[doc + 1]
    nominal = (first // 16) * 16 + index * tile
    off = pl.multiple_of(jnp.minimum(nominal, length - tile), 16)
    low = jnp.maximum(nominal, first) - off
    high = jnp.minimum(nominal + tile, last) - off
    return off, low, high


def tile_count(cuts_ref, doc, tile):
    base = (cuts_ref[doc] // 16) * 16
    return lax.div(cuts_ref[doc + 1] - base + (tile - 1), tile)


def attend_kernel(
    cuts_ref, q_ref, k_ref, v_ref, o_ref, lse_ref, vt_ref, m_ref, acc_ref, *, tile, groups, length
):
    width = groups * HD
    qf = q_ref.reshape(length, width)
    kf = k_ref.reshape(length, width)
    vf = v_ref.reshape(length, width)
    of = o_ref.reshape(length, width)
    wide = groups * tile
    vt_ref[:, width:, :] = jnp.ones((vt_ref.shape[0], 16, tile), bf16)

    def doc_step(doc, first_tile):
        count = tile_count(cuts_ref, doc, tile)

        def prepare(j, carry):
            off, low, high = tile_range(cuts_ref, doc, j, tile, length)
            vt_ref[j, 0:width, :] = vf[pl.ds(off, tile), :].T
            return carry

        lax.fori_loop(0, count, prepare, 0)

        def q_tile(i, carry):
            off, low, high = tile_range(cuts_ref, doc, i, tile, length)
            qm = mask_heads(qf[pl.ds(off, tile), :] * bf16(0.125), range(groups), groups)
            m_ref[...] = jnp.full(m_ref.shape, NEG, f32)
            acc_ref[...] = jnp.zeros(acc_ref.shape, f32)

            def k_tile(j, inner):
                koff, klow, khigh = tile_range(cuts_ref, doc, j, tile, length)

                def part(key_rows, _):
                    keep = inside(klow, khigh, (key_rows, wide), 0)
                    s = nt(kf[pl.ds(koff, key_rows), :], qm) * LOG2E
                    s = jnp.where(keep, s, NEG)
                    m_old = m_ref[0:1, :]
                    m_new = jnp.maximum(m_old, jnp.max(s, axis=0, keepdims=True))
                    p = jnp.exp2(s - m_new).astype(bf16)
                    acc_ref[...] = acc_ref[...] * jnp.exp2(m_old - m_new) + nn(
                        vt_ref[j, :, 0:key_rows], p
                    )
                    m_ref[0:1, :] = m_new

                key_sizes = (tile // 2, tile) if tile % (2 * COL) == 0 else (tile,)
                if len(key_sizes) == 1:
                    part(tile, None)
                else:

                    @pl.when(khigh <= key_sizes[0])
                    def _():
                        part(key_sizes[0], None)

                    @pl.when(khigh > key_sizes[0])
                    def _():
                        part(tile, None)

                return inner

            lax.fori_loop(0, count, k_tile, 0)
            total = acc_ref[width : width + 1, :]
            inverse = 1.0 / total
            lse_ref[first_tile + i, 0:1, :] = m_ref[0:1, :] + jnp.log2(total)
            parts = [
                acc_ref[h * HD : (h + 1) * HD, h * tile : (h + 1) * tile]
                * inverse[:, h * tile : (h + 1) * tile]
                for h in range(groups)
            ]
            out = (jnp.concatenate(parts, 0) if groups > 1 else parts[0]).T.astype(bf16)
            keep = inside(low, high, (tile, width), 0)
            of[pl.ds(off, tile), :] = jnp.where(keep, out, of[pl.ds(off, tile), :])
            return carry

        lax.fori_loop(0, count, q_tile, 0)
        return first_tile + count

    lax.fori_loop(0, DOCS, doc_step, 0)


def qkv_operands(headed):
    pieces, _, piece_len, width = headed[0].shape
    last = headed[-1].shape[1] - 1
    at = [(headed[0], 0), (headed[-1], last - 1), (headed[-1], last)]
    spec = lambda which: pl.BlockSpec(
        (pieces, None, piece_len, width), lambda i, cuts: (0, which, 0, 0)
    )
    return [array for array, _ in at], [spec(which) for _, which in at]


def attend(headed, cuts, tile):
    operands, specs = qkv_operands(headed)
    pieces, _, piece_len, width = headed[0].shape
    groups = width // HD
    length = pieces * piece_len
    tiles = length // tile + DOCS
    wide = groups * tile
    return pl.pallas_call(
        functools.partial(attend_kernel, tile=tile, groups=groups, length=length),
        out_shape=(
            jax.ShapeDtypeStruct((pieces, piece_len, width), bf16),
            jax.ShapeDtypeStruct((tiles, 8, wide), f32),
        ),
        grid_spec=pltpu.PrefetchScalarGridSpec(
            num_scalar_prefetch=1,
            grid=(1,),
            in_specs=specs,
            out_specs=[whole_spec((pieces, piece_len, width)), whole_spec((tiles, 8, wide))],
            scratch_shapes=[
                pltpu.VMEM((length // tile + 1, width + 16, tile), bf16),
                pltpu.VMEM((8, wide), f32),
                pltpu.VMEM((width + 16, wide), f32),
            ],
        ),
        compiler_params=params(),
        name="attend",
        cost_estimate=work(8192 * length * wide),
    )(cuts, *operands)


def attend_back_kernel(
    cuts_ref, q_ref, k_ref, v_ref, o_ref, do_ref, lse_ref, out_ref,
    qm_s, dom_s, lse_s, delta_s, dqt_s, ks_s, kt_s, p_s, ds_s, dk_s, dv_s, dqf, dkf, dvf,
    *, tile, groups, length, head,
):
    width = groups * HD
    own = slice(head * HD, (head + 1) * HD)
    qf = q_ref.reshape(length, width)
    kf = k_ref.reshape(length, width)
    vf = v_ref.reshape(length, width)
    of = o_ref.reshape(length, width)
    dof = do_ref.reshape(length, width)
    head_lane = lax.broadcasted_iota(jnp.int32, (16, width), 1)
    head_row = jnp.where(head_lane // HD == head, 1.0, 0.0).astype(bf16)

    def doc_step(doc, first_tile):
        count = tile_count(cuts_ref, doc, tile)

        def prepare(i, carry):
            off, low, high = tile_range(cuts_ref, doc, i, tile, length)
            spot = pl.ds(off, tile)
            qm_s[i] = mask_heads(qf[spot, :] * bf16(0.125), [head], groups)
            dom_s[i] = mask_heads(dof[spot, :], [head], groups)
            product = dof[spot, :].astype(f32) * of[spot, :].astype(f32)
            upper = product.astype(bf16)
            lower = (product - upper.astype(f32)).astype(bf16)
            delta_s[i, 0:1, :] = (nt(head_row, upper) + nt(head_row, lower))[0:1, :]
            lse = lse_ref[first_tile + i, 0:1, head * tile : (head + 1) * tile]
            lse_s[i, 0:1, :] = jnp.where(inside(low, high, (1, tile), 1), lse, -NEG)
            dqt_s[i] = jnp.zeros((HD, tile), f32)
            return carry

        lax.fori_loop(0, count, prepare, 0)

        def k_tile(j, carry):
            koff, klow, khigh = tile_range(cuts_ref, doc, j, tile, length)
            spot = pl.ds(koff, tile)
            keys = kf[spot, :]
            ks_s[...] = safe_keys(keys, klow, khigh)
            keys = jnp.where(inside(klow, khigh, keys.shape, 0), keys, jnp.zeros_like(keys))
            kt_s[...] = keys.T[own, :]
            dk_s[...] = jnp.zeros(dk_s.shape, f32)
            dv_s[...] = jnp.zeros(dv_s.shape, f32)

            def q_tile(i, inner):
                off, low, high = tile_range(cuts_ref, doc, i, tile, length)

                def part(key_rows, query_rows):
                    for c in range(0, query_rows, COL):
                        lanes = slice(c, c + COL)
                        qm = qm_s[i, lanes, :]
                        dom = dom_s[i, lanes, :]
                        for r in range(0, key_rows, COL):
                            rows = slice(r, r + COL)
                            s = nt(ks_s[rows, :], qm)
                            dp = nt(vf[pl.ds(pl.multiple_of(koff + r, 16), COL), :], dom)
                            p = jnp.exp2(s * LOG2E - lse_s[i, 0:1, lanes])
                            p_s[rows, lanes] = p.astype(bf16)
                            ds_s[rows, lanes] = (p * (dp - delta_s[i, 0:1, lanes])).astype(bf16)
                    k, q = slice(0, key_rows), slice(0, query_rows)
                    dv_s[k, :] += nn(p_s[k, q], dom_s[i, q, :])
                    dk_s[k, :] += nn(ds_s[k, q], qm_s[i, q, :])
                    dqt_s[i, :, q] += nn(kt_s[:, k], ds_s[k, q])

                for_sizes(part, tile, khigh, high)
                return inner

            lax.fori_loop(0, count, q_tile, 0)
            keep = inside(klow, khigh, (tile, width), 0)
            dkf[spot, :] = jnp.where(keep, dk_s[...].astype(bf16), dkf[spot, :])
            dvf[spot, :] = jnp.where(keep, dv_s[...].astype(bf16), dvf[spot, :])
            return carry

        lax.fori_loop(0, count, k_tile, 0)

        def finish(i, carry):
            off, low, high = tile_range(cuts_ref, doc, i, tile, length)
            out = (dqt_s[i] * 0.125).T.astype(bf16)
            spot = pl.ds(off, tile)
            dqf[spot, :] = jnp.where(inside(low, high, (tile, HD), 0), out, dqf[spot, :])
            return carry

        lax.fori_loop(0, count, finish, 0)
        return first_tile + count

    lax.fori_loop(0, DOCS, doc_step, 0)
    piece_len = q_ref.shape[1]
    fold = piece_len // groups
    for at in range(q_ref.shape[0]):
        for which, full in enumerate((dqf, dkf, dvf)):
            start = at * piece_len
            lanes = slice(0, HD) if which == 0 else own
            parts = [full[start + g * fold : start + (g + 1) * fold, lanes] for g in range(groups)]
            out_ref[at, which] = jnp.concatenate(parts, 1) if groups > 1 else parts[0]

def attend_back(headed, o, do, lse, cuts, tile, head):
    operands, specs = qkv_operands(headed)
    pieces, _, piece_len, width = headed[0].shape
    groups = width // HD
    length = pieces * piece_len
    tiles = length // tile + DOCS
    per_doc = length // tile + 1
    flat = whole_spec((pieces, piece_len, width))
    out = (pieces, 3, piece_len // groups, width)
    return pl.pallas_call(
        functools.partial(attend_back_kernel, tile=tile, groups=groups, length=length, head=head),
        out_shape=jax.ShapeDtypeStruct(out, bf16),
        grid_spec=pltpu.PrefetchScalarGridSpec(
            num_scalar_prefetch=1,
            grid=(1,),
            in_specs=specs
            + [flat, flat, whole_spec((tiles, 8, groups * tile))],
            out_specs=whole_spec(out),
            scratch_shapes=[
                pltpu.VMEM((per_doc, tile, width), bf16),
                pltpu.VMEM((per_doc, tile, width), bf16),
                pltpu.VMEM((per_doc, 8, tile), f32),
                pltpu.VMEM((per_doc, 8, tile), f32),
                pltpu.VMEM((per_doc, HD, tile), f32),
                pltpu.VMEM((tile, width), bf16),
                pltpu.VMEM((HD, tile), bf16),
                pltpu.VMEM((tile, tile), bf16),
                pltpu.VMEM((tile, tile), bf16),
                pltpu.VMEM((tile, width), f32),
                pltpu.VMEM((tile, width), f32),
            ]
            + [pltpu.VMEM((length, HD), bf16)]
            + [pltpu.VMEM((length, width), bf16)] * 2,
        ),
        compiler_params=params(),
        name="attend_back",
        cost_estimate=work(16384 * length * tile),
    )(cuts, *operands, o, do, lse)


def normalize(values):
    center = values - jnp.mean(values, axis=-1, keepdims=True)
    spread = jnp.mean(center * center, axis=-1, keepdims=True)
    scale = lax.rsqrt(spread + eps_norm)
    return center * scale, scale


def norm_back(unit, scale, scaled_grad):
    return scale * (
        scaled_grad
        - jnp.mean(scaled_grad, axis=-1, keepdims=True)
        - unit * jnp.mean(scaled_grad * unit, axis=-1, keepdims=True)
    )


def lane_swap(values):
    lane = lax.broadcasted_iota(jnp.int32, values.shape, 1)
    size = values.shape[1]
    half = HD // 2
    return jnp.where(
        lane % HD < half, pltpu.roll(values, size - half, 1), pltpu.roll(values, half, 1)
    )


def norm_kernel(x_ref, g_ref, a_ref, norm_ref, small_ref):
    unit, _ = normalize(x_ref[...].astype(f32))
    norm = (unit * g_ref[...]).astype(bf16)
    norm_ref[...] = norm
    small_ref[...] = nt(a_ref[...], norm).astype(bf16)


def norm_call(x, gain, a):
    count, rows, model = x.shape
    rank = a.shape[1]
    return pl.pallas_call(
        norm_kernel,
        grid=(count,),
        out_shape=(
            jax.ShapeDtypeStruct((count, rows, model), bf16),
            jax.ShapeDtypeStruct((count, rank, rows), bf16),
        ),
        in_specs=[
            pl.BlockSpec((None, rows, model), lambda s: (s, 0, 0)),
            whole_spec((1, model)),
            pl.BlockSpec((None, rank, model), lambda s: (s, 0, 0)),
        ],
        out_specs=[
            pl.BlockSpec((None, rows, model), lambda s: (s, 0, 0)),
            pl.BlockSpec((None, rank, rows), lambda s: (s, 0, 0)),
        ],
        compiler_params=params(),
        name="norm",
        cost_estimate=work(4096 * count * rows * model),
    )(x, gain, a)


def both_halves(core, own_ref, other_ref):
    groups, chips = own_ref.shape[:2]
    slabs = []
    for d in range(groups):
        for c in range(chips):
            own, other = own_ref[d, c], other_ref[d, c]
            slabs += [jnp.where(core == 0, own, other), jnp.where(core == 0, other, own)]
    return jnp.concatenate(slabs, 0)


def qkv_kernel(core_ref, norm_ref, small_ref, *refs, width, kinds):
    count = len(kinds)
    w_refs, b_refs = refs[: 2 * count], refs[2 * count : 3 * count]
    cos_ref, sin_ref, out_ref = refs[3 * count :]
    core = core_ref[0]
    norm = norm_ref[...]
    small = small_ref[...]
    for at, kind in enumerate(kinds):
        w = both_halves(core, w_refs[2 * at], w_refs[2 * at + 1])
        lin = nn(norm, w) + tn(small, b_refs[at][...])
        for part in range(COL // 128):
            u = lin[:, part * 128 : (part + 1) * 128]
            if kind < 2:
                u = u * cos_ref[...] + lane_swap(u) * sin_ref[...]
            u = u.astype(bf16)
            for sub in range(128 // width):
                dest = part * (128 // width) + sub
                out_ref[dest, at] = u[:, sub * width : (sub + 1) * width]


def half_specs(shape, steps, kinds):
    block = shape[:-1] + (COL,)
    spec = lambda kind: pl.BlockSpec(block, lambda j, core: (0, 0, 0, kind * steps + j))
    return [spec(kind) for kind in kinds for _ in range(2)]


def qkv_project(at, kinds, norm, small, core, halves, b, cosine, sine, pieces, width):
    _, rows, model = norm.shape
    dests = COL // width
    steps = model // COL
    rank = small.shape[1]
    count = len(kinds)
    row_spec = lambda shape: pl.BlockSpec((None,) + shape, lambda j, core: (at, 0, 0))
    b_spec = lambda kind: pl.BlockSpec((rank, COL), lambda j, core: (0, kind * steps + j))
    return pl.pallas_call(
        functools.partial(qkv_kernel, width=width, kinds=kinds),
        out_shape=jax.ShapeDtypeStruct((pieces, count, rows, width), bf16),
        grid_spec=pltpu.PrefetchScalarGridSpec(
            num_scalar_prefetch=1,
            grid=(steps,),
            in_specs=[row_spec((rows, model)), row_spec((rank, rows))]
            + half_specs(halves[0].shape, steps, kinds)
            + [b_spec(kind) for kind in kinds]
            + [row_spec((rows, 128)), row_spec((rows, 128))],
            out_specs=pl.BlockSpec((dests, count, rows, width), lambda j, core: (j, 0, 0, 0)),
        ),
        compiler_params=params(),
        name="qkv_project",
        cost_estimate=work(2 * count * rows * model * model),
    )(core, norm, small, *halves * count, *[b] * count, cosine, sine)


def join_heads(refs, dest, which):
    if len(refs) == 1:
        return refs[0][dest, which]
    blocks = [ref[dest, which] for ref in refs]
    folds = [
        jnp.concatenate([block[:, g * HD : (g + 1) * HD] for block in blocks], 1)
        for g in range(len(refs))
    ]
    return jnp.concatenate(folds, 0)


def dlin_kernel(*args, width, heads):
    dqkv_refs = args[:heads]
    norm_ref, small_ref = args[heads : heads + 2]
    b_refs = args[heads + 2 : heads + 5]
    cos_ref, sin_ref, dlin_ref, dsmall_ref, grad_ref, acc_ref = args[heads + 5 :]
    step = pl.program_id(0)

    @pl.when(step == 0)
    def _():
        acc_ref[...] = jnp.zeros(acc_ref.shape, f32)

    small = small_ref[...]
    per = 128 // width
    for which in range(3):
        pieces = []
        for part in range(COL // 128):
            subs = [join_heads(dqkv_refs, part * per + sub, which) for sub in range(per)]
            u = jnp.concatenate(subs, 1) if per > 1 else subs[0]
            if which < 2:
                u = u.astype(f32)
                u = (u * cos_ref[...] - lane_swap(u) * sin_ref[...]).astype(bf16)
            pieces.append(u)
        dlin = jnp.concatenate(pieces, 1)
        dlin_ref[which] = dlin
        acc_ref[...] += nt(b_refs[which][...], dlin)
        grad_ref[(which + 1) * pl.num_programs(0) + step] = nn(small, dlin)

    @pl.when(step == pl.num_programs(0) - 1)
    def _():
        dsmall = acc_ref[...].astype(bf16)
        dsmall_ref[...] = dsmall
        grad_a = nn(dsmall, norm_ref[...])
        for at in range(grad_a.shape[1] // COL):
            grad_ref[at] = grad_a[:, at * COL : (at + 1) * COL]


def dlin_call(at, dqkv, norm, small, b, cosine, sine):
    _, _, fold, width = dqkv[0].shape
    _, rows, model = norm.shape
    rank = small.shape[1]
    dests = COL // width
    steps = model // COL
    b_spec = lambda kind: pl.BlockSpec((rank, COL), lambda j: (0, kind * steps + j))
    row_spec = lambda shape: pl.BlockSpec((None,) + shape, lambda j: (at, 0, 0))
    return pl.pallas_call(
        functools.partial(dlin_kernel, width=width, heads=len(dqkv)),
        grid=(steps,),
        out_shape=(
            jax.ShapeDtypeStruct((3, rows, model), bf16),
            jax.ShapeDtypeStruct((rank, rows), bf16),
            jax.ShapeDtypeStruct((4 * steps, rank, COL), f32),
        ),
        in_specs=[pl.BlockSpec((dests, 3, fold, width), lambda j: (j, 0, 0, 0))] * len(dqkv)
        + [
            row_spec((rows, model)),
            row_spec((rank, rows)),
            *[b_spec(kind) for kind in range(3)],
            row_spec((rows, 128)),
            row_spec((rows, 128)),
        ],
        out_specs=[
            pl.BlockSpec((3, rows, COL), lambda j: (0, 0, j)),
            whole_spec((rank, rows)),
            whole_spec((4 * steps, rank, COL)),
        ],
        scratch_shapes=[pltpu.VMEM((rank, rows), f32)],
        compiler_params=params(),
        name="dlin",
        cost_estimate=work(4 * rows * model * model),
    )(*dqkv, norm, small, b, b, b, cosine, sine)


def input_grad_kernel(core_ref, dlin_ref, dsmall_ref, x_ref, g_ref, dmid_ref, *refs):
    w_refs = refs[:6]
    a_ref = refs[6]
    out_ref, acc_ref = refs[-2:]
    step = pl.program_id(0)
    core = core_ref[0]
    value = sum(
        nt(dlin_ref[which], both_halves(core, w_refs[2 * which], w_refs[2 * which + 1]))
        for which in range(3)
    )

    @pl.when(step == 0)
    def _():
        acc_ref[...] = value + tn(dsmall_ref[...], a_ref[...])

    @pl.when(step > 0)
    def _():
        acc_ref[...] += value

    @pl.when(step == pl.num_programs(0) - 1)
    def _():
        unit, scale = normalize(x_ref[...].astype(f32))
        out_ref[...] = (
            dmid_ref[...] + norm_back(unit, scale, acc_ref[...] * g_ref[...])
        ).astype(bf16)


def input_grad_call(at, given, dlin, dsmall, x, gain, dmid, core, halves, a):
    count, rows, model = x.shape
    given = [] if given is None else [given]
    rank = a.shape[0]
    steps = model // COL
    return pl.pallas_call(
        input_grad_kernel,
        out_shape=jax.ShapeDtypeStruct((count, rows, model), bf16),
        grid_spec=pltpu.PrefetchScalarGridSpec(
            num_scalar_prefetch=1,
            grid=(steps,),
            in_specs=[
                pl.BlockSpec((3, rows, COL), lambda j, core: (0, 0, j)),
                whole_spec((rank, rows)),
                pl.BlockSpec((None, rows, model), lambda j, core: (at, 0, 0)),
                whole_spec((1, model)),
                whole_spec((rows, model)),
            ]
            + half_specs(halves[0].shape, steps, range(3))
            + [whole_spec((rank, model))]
            + [pl.BlockSpec(memory_space=pl.ANY)] * len(given),
            out_specs=pl.BlockSpec((None, rows, model), lambda j, core: (at, 0, 0)),
            scratch_shapes=[pltpu.VMEM((rows, model), f32)],
        ),
        input_output_aliases={13: 0} if given else {},
        compiler_params=params(),
        name="input_grad",
        cost_estimate=work(8 * rows * model * model),
    )(core, dlin, dsmall, x, gain, dmid, *halves * 3, a, *given)


def mlp_kernel(
    x_ref, cot_ref, o_ref, g_ref, wo_ref, wu_ref, wv_ref, wt_ref,
    aout_ref, bout_ref, ain_ref, bu_ref, bv_ref, a2_ref, b2_ref, id_ref, *rest, width,
):
    mlp_body(
        x_ref, cot_ref, o_ref, g_ref, wo_ref, wu_ref, wv_ref, wt_ref,
        aout_ref, bout_ref, ain_ref, bu_ref, bv_ref, a2_ref, b2_ref, id_ref, *rest, width=width,
    )


def natural(ref):
    cores, groups, chips = ref.shape[:3]
    return jnp.concatenate(
        [ref[core, d, c] for d in range(groups) for c in range(chips) for core in range(cores)], 0
    )


def mlp_body(
    x_ref, cot_ref, o_ref, g_ref, wo_ref, wu_ref, wv_ref, wt_ref,
    aout_ref, bout_ref, ain_ref, bu_ref, bv_ref, a2_ref, b2_ref, id_ref,
    out_ref, dmid_ref, datt_ref, grad_ref,
    att_s, norm_s, unit_s, scale_s, acc_s, dnorm_s, small2_s, small3_s, small4_s, dsmall4_s, dsmall3_s,
    *, width,
):
    step = pl.program_id(0)
    pieces = o_ref.shape[0]
    model = x_ref.shape[1]
    per = model // COL
    first_block = grad_ref.shape[0] - BLOCK_PAD - 4 * per

    def put(which, value):
        for at in range(per):
            grad_ref[first_block + which * per + at] = value[:, at * COL : (at + 1) * COL]

    @pl.when(step == 0)
    def _():
        for at in range(first_block + 4 * per, grad_ref.shape[0]):
            grad_ref[at] = id_ref[...]
        for at in range(pieces):
            att_s[:, at * width : (at + 1) * width] = o_ref[at]
        att = att_s[...]
        small2 = nt(aout_ref[...], att).astype(bf16)
        small2_s[...] = small2
        middle = x_ref[...].astype(f32) + nn(att, natural(wo_ref)) + tn(small2, bout_ref[...])
        acc_s[...] = middle
        unit, scale = normalize(middle)
        unit_s[...] = unit
        scale_s[...] = jnp.broadcast_to(scale, scale_s.shape)
        norm = (unit * g_ref[...]).astype(bf16)
        norm_s[...] = norm
        small3_s[...] = nt(ain_ref[...], norm).astype(bf16)
        dsmall4_s[...] = nt(b2_ref[...], cot_ref[...]).astype(bf16)
        dnorm_s[...] = jnp.zeros(dnorm_s.shape, f32)
        small4_s[...] = jnp.zeros(small4_s.shape, f32)
        dsmall3_s[...] = jnp.zeros(dsmall3_s.shape, f32)

    norm = norm_s[...]
    small3 = small3_s[...]
    dsmall4 = dsmall4_s[...]
    wu, wv, wt = natural(wu_ref), natural(wv_ref), natural(wt_ref)
    u = nn(norm, wu) + tn(small3, bu_ref[...])
    v = nn(norm, wv) + tn(small3, bv_ref[...])
    dmixed = nn(cot_ref[...], wt) + tn(dsmall4, a2_ref[...])
    below = 0.5 * (1.0 + lax.erf(u * RSQRT2))
    gelu = u * below
    mixed = (gelu * v).astype(bf16)
    slope = below + u * (jnp.exp(-0.5 * u * u) * RSQRT2PI)
    du = (dmixed * v * slope).astype(bf16)
    dv = (dmixed * gelu).astype(bf16)
    acc_s[...] += nt(mixed, wt)
    dnorm_s[...] += nt(du, wu) + nt(dv, wv)
    small4_s[...] += nt(a2_ref[...], mixed)
    dsmall3_s[...] += nt(bu_ref[...], du) + nt(bv_ref[...], dv)
    steps = pl.num_programs(0)
    grad_ref[step] = nn(small3, du)
    grad_ref[steps + step] = nn(small3, dv)
    grad_ref[2 * steps + step] = nn(dsmall4, mixed)

    @pl.when(step == pl.num_programs(0) - 1)
    def _():
        small4 = small4_s[...].astype(bf16)
        dsmall3 = dsmall3_s[...].astype(bf16)
        out_ref[...] = (acc_s[...] + tn(small4, b2_ref[...])).astype(bf16)
        put(3, nn(small4, cot_ref[...]))
        dnorm = dnorm_s[...] + tn(dsmall3, ain_ref[...])
        put(2, nn(dsmall3, norm_s[...]))
        dmid = cot_ref[...].astype(f32) + norm_back(unit_s[...], scale_s[:, 0:1], dnorm * g_ref[...])
        dmid_ref[...] = dmid
        dlow = dmid.astype(bf16)
        dsmall2 = nt(bout_ref[...], dlow).astype(bf16)
        put(1, nn(small2_s[...], dlow))
        put(0, nn(dsmall2, att_s[...]))
        datt = (nt(dlow, natural(wo_ref)) + tn(dsmall2, aout_ref[...])).astype(bf16)
        for at in range(pieces):
            datt_ref[at] = datt[:, at * width : (at + 1) * width]


def mlp_call(
    which_seq, x, cot, o, gain, w_all, a_out, b_out, a_in, b_u, b_v, a_out2, b_out2, own_id
):
    seq_count, rows, model = x.shape
    pieces, _, width = o.shape
    rank = a_out.shape[0]
    hidden = b_u.shape[1]
    steps = hidden // COL
    blocks = 3 * steps + 4 * (model // COL) + BLOCK_PAD
    full = lambda shape: pl.BlockSpec(shape, lambda j: (0,) * len(shape), pipeline_mode=pl.Buffered(1))
    lead = w_all.shape[:-1]
    ff_spec = lambda which: pl.BlockSpec(
        lead + (COL,), lambda j: (0, 0, 0, 0, model // COL + which * steps + j)
    )
    one_seq = pl.BlockSpec((None, rows, model), lambda j: (which_seq, 0, 0))
    small_ff = pl.BlockSpec((rank, COL), lambda j: (0, j))
    small = full((rank, model))
    return pl.pallas_call(
        functools.partial(mlp_kernel, width=width),
        grid=(steps,),
        out_shape=(
            jax.ShapeDtypeStruct((rows, model), bf16),
            jax.ShapeDtypeStruct((rows, model), f32),
            jax.ShapeDtypeStruct((pieces, rows, width), bf16),
            jax.ShapeDtypeStruct((blocks, rank, COL), f32),
        ),
        in_specs=[
            one_seq,
            one_seq,
            full((pieces, rows, width)),
            full((1, model)),
            full(lead + (model,)),
            ff_spec(0),
            ff_spec(1),
            ff_spec(2),
            small,
            small,
            small,
            small_ff,
            small_ff,
            small_ff,
            small,
            full((rank, COL)),
        ],
        out_specs=[
            whole_spec((rows, model)),
            whole_spec((rows, model)),
            whole_spec((pieces, rows, width)),
            whole_spec((blocks, rank, COL)),
        ],
        scratch_shapes=[
            pltpu.VMEM((rows, model), bf16),
            pltpu.VMEM((rows, model), bf16),
            pltpu.VMEM((rows, model), f32),
            pltpu.VMEM((rows, 128), f32),
            pltpu.VMEM((rows, model), f32),
            pltpu.VMEM((rows, model), f32),
            pltpu.VMEM((rank, rows), bf16),
            pltpu.VMEM((rank, rows), bf16),
            pltpu.VMEM((rank, rows), f32),
            pltpu.VMEM((rank, rows), bf16),
            pltpu.VMEM((rank, rows), f32),
        ],
        compiler_params=params(),
        name="feed_forward",
        cost_estimate=work(26 * rows * model * hidden),
    )(
        x, cot, o, gain, w_all, w_all, w_all, w_all, a_out, b_out, a_in, b_u, b_v, a_out2, b_out2,
        own_id,
    )


def assemble_kernel(ids_ref, *refs, layout, arrays):
    which = pl.program_id(0)
    sources, outs, acc_ref = refs[:arrays], refs[arrays:-1], refs[-1]
    acc_ref[...] = jnp.zeros(acc_ref.shape, f32)
    count = sources[0].shape[0]
    for at, source in enumerate(sources):

        def add(index, carry):
            @pl.when(ids_ref[at * count + index] == which)
            def _():
                acc_ref[...] += source[index].astype(f32)

            return carry

        lax.fori_loop(0, count, add, 0)
    for out_ref, segments in zip(outs, layout):
        start = 0
        for first, blocks, size in segments:
            for block in range(blocks):
                wide = min(COL, size - block * COL)
                if wide > 0:
                    spot = start + block * COL
                    out_ref[:, spot : spot + wide] = acc_ref[first + block][:, :wide]
            start += size


def assemble_call(sources, ids, adapters, layout):
    _, blocks, rank, _ = sources[0].shape
    sizes = [sum(size for _, _, size in segments) for segments in layout]
    return pl.pallas_call(
        functools.partial(assemble_kernel, layout=layout, arrays=len(sources)),
        out_shape=[jax.ShapeDtypeStruct((adapters, rank, size), f32) for size in sizes],
        grid_spec=pltpu.PrefetchScalarGridSpec(
            num_scalar_prefetch=1,
            grid=(adapters,),
            in_specs=[whole_spec(source.shape) for source in sources],
            out_specs=[pl.BlockSpec((None, rank, size), lambda e, ids: (e, 0, 0)) for size in sizes],
            scratch_shapes=[pltpu.VMEM((blocks, rank, COL), f32)],
        ),
        compiler_params=params(),
        name="assemble",
        cost_estimate=work(4096 * adapters * rank * sum(sizes) // 256),
    )(ids, *sources)


def pad_columns(values, size):
    return jnp.pad(values, [(0, 0)] * (values.ndim - 1) + [(0, size - values.shape[-1])])


def local(
    tokens,
    segment_ids,
    positions,
    adapter_id,
    gain_attn,
    gain_mlp,
    w_qkv,
    w_out,
    w_in,
    w_out2,
    a_qkv,
    b_qkv,
    a_out,
    b_out,
    a_in,
    b_in,
    a_out2,
    b_out2,
    cotangent,
):
    seq_count, piece_len, model = tokens.shape
    pieces = lax.axis_size("seq")
    groups = HEADS // pieces
    width = groups * HD
    length = piece_len * pieces
    rank = a_qkv.shape[1]
    adapters = a_qkv.shape[0]
    hidden = w_out2.shape[0]
    padded = -(-hidden // COL) * COL
    tile = min(512, length)
    both = ("dp", "seq")

    dp = lax.axis_size("dp")
    before = [jnp.sum((segment_ids < d).astype(jnp.int32), axis=1) for d in range(1, DOCS)]
    swap = lambda value: lax.all_to_all(value, "seq", split_axis=0, concat_axis=0, tiled=True)
    facts = jnp.stack(before, 1)
    shard = jnp.concatenate(
        [
            w_out,
            pad_columns(w_in[:, :hidden], padded),
            pad_columns(w_in[:, hidden:], padded),
            pad_columns(w_out2.T, padded),
        ],
        1,
    )
    chips = pieces // 2
    same_core = [[2 * chip + core for chip in range(chips)] for core in range(2)]
    same_chip = [[2 * chip, 2 * chip + 1] for chip in range(chips)]
    half = HD // 2
    lane = jnp.arange(128, dtype=jnp.int32) % HD
    frequency = theta_base ** (-((lane % half).astype(f32) * 2.0) / HD)
    angles = positions.astype(f32)[..., None] * frequency
    cosine = jnp.cos(angles)
    sine = jnp.where(lane < half, -1.0, 1.0) * jnp.sin(angles)

    gain1 = gain_attn.reshape(1, model)
    gain2 = gain_mlp.reshape(1, model)
    pick = lambda table, s: lax.dynamic_index_in_dim(table, adapter_id[s], 0, keepdims=False)
    each = range(seq_count)

    aq = [pick(a_qkv, s) for s in each]
    bq = [pick(b_qkv, s) for s in each]
    norm, small = norm_call(tokens, gain1, jnp.stack(aq, 0))
    maps = []
    for s in each:
        b_in_s = pick(b_in, s)
        maps.append(
            (
                pick(a_out, s),
                pick(b_out, s),
                pick(a_in, s),
                pad_columns(b_in_s[:, :hidden], padded),
                pad_columns(b_in_s[:, hidden:], padded),
                pad_columns(pick(a_out2, s), padded),
                pick(b_out2, s),
                jnp.full((rank, COL), adapter_id[s].astype(f32)),
            )
        )
    same_pair = [(at, at ^ 1) for at in range(pieces)]
    core = (lax.axis_index("seq") % 2).astype(jnp.int32).reshape(1)
    qkv_column = lax.all_gather(w_qkv, "seq", axis=0, tiled=True, axis_index_groups=same_core)
    qkv_column, shard = lax.optimization_barrier((qkv_column, shard))
    qkv_own = lax.all_to_all(
        jnp.broadcast_to(qkv_column[None], (dp,) + qkv_column.shape),
        "dp",
        split_axis=0,
        concat_axis=0,
        tiled=True,
    ).reshape(dp, chips, -1, 3 * model)
    ready = (qkv_own, facts, norm, small, cosine, sine, bq)
    qkv_own, facts, norm, small, cosine, sine, bq = lax.optimization_barrier(ready)
    counts = jnp.sum(swap(jnp.broadcast_to(facts[None], (pieces,) + facts.shape)), 0)
    cuts = jnp.concatenate(
        [
            jnp.zeros((seq_count, 1), jnp.int32),
            counts,
            jnp.full((seq_count, 1), length, jnp.int32),
        ],
        1,
    )
    halves = [qkv_own, lax.ppermute(qkv_own, "seq", same_pair)]
    column = lax.all_gather(shard, "seq", axis=0, tiled=True, axis_index_groups=same_core)

    def project_of(s, kinds):
        return qkv_project(
            s, kinds, norm, small, core, halves, bq[s], cosine, sine, pieces, width
        )

    packed = [[project_of(0, (0, 1, 2))]]
    norm, packed[0], column, cuts = lax.optimization_barrier((norm, packed[0], column, cuts))
    own = lax.all_gather(column, "dp", axis=0, tiled=True)
    packed.append([project_of(1, (0,)), project_of(1, (1, 2))])
    maps, packed[1] = lax.optimization_barrier((maps, packed[1]))
    headed = [[swap(packed[0][0])]]
    packed[1], headed[0] = lax.optimization_barrier((packed[1], headed[0]))
    query_keys = swap(packed[1][0])
    attended = [attend(headed[0], cuts[0], tile)]
    own, attended[0], query_keys = lax.optimization_barrier((own, attended[0], query_keys))
    full_rest = lax.all_gather(own, "seq", axis=0, tiled=True, axis_index_groups=same_chip)
    full_rest = full_rest.reshape(2, dp, chips, -1, full_rest.shape[-1])
    query_keys, o_first = lax.optimization_barrier((query_keys, attended[0][0]))
    o_tokens = [swap(o_first)]
    values, o_tokens[0] = lax.optimization_barrier((packed[1][1], o_tokens[0]))
    values = swap(values)

    def feed_forward(s):
        return mlp_call(
            s, tokens, cotangent, o_tokens[s], gain2, full_rest, *maps[s]
        )

    middle = [feed_forward(0)]

    def scatter(grads):
        lead = grads.reshape(-1, COL)
        return lax.psum_scatter(lead, "seq", scatter_dimension=0, tiled=True).astype(bf16)

    first_sum = scatter(middle[0][3])
    values, query_keys, middle[0] = lax.optimization_barrier((values, query_keys, middle[0]))
    headed.append([query_keys, values])
    do_items = [swap(middle[0][2])]
    attended.append(attend(headed[1], cuts[1], tile))
    do_items[0], attended[1], first_sum = lax.optimization_barrier(
        (do_items[0], attended[1], first_sum)
    )

    first_every = lax.all_gather(first_sum, both, axis=0, tiled=True)

    def back(s, h):
        return attend_back(
            headed[s], attended[s][0], do_items[s], attended[s][1], cuts[s], tile, h
        )

    first_back = back(0, 0)
    o_tokens.append(swap(attended[1][0]))
    o_tokens[1], _ = lax.optimization_barrier((o_tokens[1], first_back))
    dqkv = [[swap(first_back)]]
    middle.append(feed_forward(1))
    second_sum = scatter(middle[1][3])
    dqkv[0][0], do_second = lax.optimization_barrier((dqkv[0][0], middle[1][2]))
    do_items.append(swap(do_second))
    do_items[0], first_every, _ = lax.optimization_barrier(
        (do_items[0], first_every, middle[1][3])
    )
    ff = padded // COL
    per = model // COL
    mods = 3 * ff

    def dlin_of(s):
        return dlin_call(s, dqkv[s], norm, small, bq[s], cosine, sine)

    def input_grad_of(s, dlin, given):
        return input_grad_call(
            s, given, dlin[0], dlin[1], tokens, gain1, middle[s][1], core, halves, aq[s]
        )

    others = [back(0, h) for h in range(1, groups)]
    dqkv[0] += [swap(part) for part in others]
    do_items[1], second_sum, _ = lax.optimization_barrier((do_items[1], second_sum, others))
    parts = [back(1, h) for h in range(groups)]
    parts[0], dqkv[0] = lax.optimization_barrier((parts[0], dqkv[0]))
    dqkv.append([swap(part) for part in parts])
    second_sum, dqkv[1][0], _ = lax.optimization_barrier((second_sum, dqkv[1][0], parts[-1]))
    second_every = lax.all_gather(second_sum, both, axis=0, tiled=True)
    gathered = [every.reshape(dp, -1, rank, COL) for every in (first_every, second_every)]
    ids = [
        (part[:, -1, 0, 0].astype(f32) * (1.0 / pieces)).astype(jnp.int32) for part in gathered
    ]
    dlins = [dlin_of(0)]
    input_grads = input_grad_of(0, dlins[0], None)
    dqkv[1], input_grads = lax.optimization_barrier((dqkv[1], input_grads))
    dlins += [dlin_of(s) for s in each[1:]]
    late_grads = jnp.stack([dlins[s][2] for s in each], 0)
    parts = swap(late_grads.astype(bf16).reshape(pieces, -1, COL))
    mine = jnp.sum(parts.astype(f32), 0).astype(bf16)
    copies = jnp.broadcast_to(mine[None], (dp * pieces,) + mine.shape)
    every = lax.all_to_all(copies, both, split_axis=0, concat_axis=0, tiled=True)
    for s in each[1:]:
        input_grads = input_grad_of(s, dlins[s], input_grads)
    early = assemble_call(
        gathered,
        jnp.concatenate(ids),
        adapters,
        [[(mods + which * per, per, model)] for which in range(3)]
        + [[(0, ff, hidden), (ff, ff, hidden)], [(2 * ff, ff, hidden)], [(mods + 3 * per, per, model)]],
    )
    late = assemble_call(
        [every.reshape((dp * seq_count,) + late_grads.shape[1:])],
        jnp.stack(ids, 1).reshape(-1),
        adapters,
        [[(0, per, model)], [(per, 3 * per, 3 * model)]],
    )
    layer_out = jnp.stack([middle[s][0] for s in each], 0)
    return (
        layer_out,
        input_grads,
        late[0],
        late[1],
        early[0],
        early[1],
        early[2],
        early[3],
        early[4],
        early[5],
    )


def solution(mesh):
    placed = (
        P("dp", "seq", None),
        P("dp", "seq"),
        P("dp", "seq"),
        P("dp"),
        P(),
        P(),
        P(("dp", "seq"), None),
        P(("dp", "seq"), None),
        P(("dp", "seq"), None),
        P(None, ("dp", "seq")),
        P(),
        P(),
        P(),
        P(),
        P(),
        P(),
        P(),
        P(),
        P("dp", "seq", None),
    )
    return jax.shard_map(
        local,
        mesh=mesh,
        in_specs=placed,
        out_specs=(
            P("dp", "seq", None),
            P("dp", "seq", None),
            P(),
            P(),
            P(),
            P(),
            P(),
            P(),
            P(),
            P(),
        ),
        check_vma=False,
    )
```
